32 devices in a mesh: groups: 2 (over x), tile: 8 (over z, y), section: 2 (over core).
Axes of the slice: x: 2, y: 2, z: 4, core: 2. Of those that a mesh axis runs over, the one named last changes fastest.
Arguments:
- frames: bfloat16 [2, 128, 8192], P(None, ('groups', 'tile', 'section')), parts along dimension 1, may hold values from -6 to 6
- start_fine: bfloat16 [128, 32768], P(('groups', 'tile', 'section')), parts along dimension 0, may hold values from -0.8984375 to 0.8984375
- start_coarse: bfloat16 [64, 49152], P(('groups', 'tile', 'section')), parts along dimension 0, may hold values from -0.8984375 to 0.8984375
- enc_stem: bfloat16 [16, 64], replicated, may hold values from -1.5 to 1.5
- enc_fine_x: bfloat16 [3, 3, 64, 192], replicated, may hold values from -0.25 to 0.25
- enc_fine_h: bfloat16 [3, 3, 64, 192], replicated, may hold values from -0.25 to 0.25
- enc_down: bfloat16 [3, 3, 64, 192], replicated, may hold values from -0.25 to 0.25
- enc_coarse_x: bfloat16 [3, 3, 192, 576], replicated, may hold values from -0.15625 to 0.15625
- enc_coarse_h: bfloat16 [3, 3, 192, 576], replicated, may hold values from -0.15625 to 0.15625
- fc_coarse_h: bfloat16 [3, 3, 192, 576], replicated, may hold values from -0.15625 to 0.15625
- fc_up: bfloat16 [3, 3, 192, 64], replicated, may hold values from -0.25 to 0.25
- fc_fine_x: bfloat16 [3, 3, 64, 192], replicated, may hold values from -0.25 to 0.25
- fc_fine_h: bfloat16 [3, 3, 64, 192], replicated, may hold values from -0.25 to 0.25
- fc_head: bfloat16 [64, 16], replicated, may hold values from -0.75 to 0.75
Outputs:
- forecast: bfloat16 [2, 128, 8192], P(None, ('groups', 'tile', 'section')), parts along dimension 1
The draws below stay inside these ranges and needn't reach their ends.
There are 2 independent parts, one for each index of `groups`. The reference program is written for one: setup_inputs(seed, part) draws one part's arguments, and reference() takes and returns one part's arrays. A program takes and returns all parts, laid end to end along the dimension named above; an argument that names none is the same for every part. Nothing has to cross between parts.
All inputs are finite; a program needn't handle non-finite values.
Results may differ from the reference program's by a relative error of at most 0.007.
Values may be sent and summed in bfloat16 or wider, within the bound.
No kernel may reach another device: no remote copies, remote signals or barrier semaphores. Data moves between devices by JAX's collectives and lax.ppermute only.
A program may use at most 64 MiB of HBM per device.

```python
import jax
import jax.numpy as jnp
from jax import lax

C1 = 64
C2 = 192
PATCH = 16
FRAMES = 2
HORIZON = 2
COLS = 512
ROWS = 64


def levels(key, dims, cuts, smallest, top_value):
    factor_of, own = 1.0, jax.random.fold_in(key, 6)
    for axis_at, parts in cuts:
        heights = jnp.exp(jax.random.uniform(jax.random.fold_in(own, axis_at), (parts,), jnp.float32, smallest / len(cuts), top_value / len(cuts)))
        factor_of = factor_of * jnp.repeat(heights, dims[axis_at] // parts).reshape([-1 if axis == axis_at else 1 for axis in range(len(dims))])
    return factor_of


def bell_draw(key, extent, scale, reach, split=(), held_as=jnp.bfloat16):
    loudness = levels(key, extent, split, -0.22, 0.18) if split else 1.0
    array = jax.random.normal(key, extent, jnp.float32) * scale * loudness
    return jnp.minimum(jnp.maximum(array, -reach), reach).astype(held_as)


def setup_inputs(seed: int = 0, part: int = 0) -> dict:
    streams_of = jax.random.split(jax.random.key(seed), 15)
    part_keys = jax.random.split(jax.random.fold_in(streams_of[14], part), 15)
    return {
        "frames": bell_draw(part_keys[0], (FRAMES, ROWS, COLS * PATCH), 1.0, 6.0, ((1, 16),)),
        "start_fine": jnp.clip(jax.random.uniform(part_keys[1], (ROWS, COLS * C1), jnp.float32, -0.8984375, 0.8984375) * levels(part_keys[1], (ROWS, COLS * C1), ((0, 16),), -0.4, 0.0), -0.8984375, 0.8984375).astype(jnp.bfloat16),
        "start_coarse": jnp.clip(jax.random.uniform(part_keys[2], (ROWS // 2, (COLS // 2) * C2), jnp.float32, -0.8984375, 0.8984375) * levels(part_keys[2], (ROWS // 2, (COLS // 2) * C2), ((0, 16),), -0.4, 0.0), -0.8984375, 0.8984375).astype(jnp.bfloat16),
        "enc_stem": bell_draw(streams_of[3], (PATCH, C1), PATCH ** -0.5, 1.5),
        "enc_fine_x": bell_draw(streams_of[4], (3, 3, C1, 3 * C1), (9 * C1) ** -0.5, 0.25),
        "enc_fine_h": bell_draw(streams_of[5], (3, 3, C1, 3 * C1), (9 * C1) ** -0.5, 0.25),
        "enc_down": bell_draw(streams_of[6], (3, 3, C1, C2), (9 * C1) ** -0.5, 0.25),
        "enc_coarse_x": bell_draw(streams_of[7], (3, 3, C2, 3 * C2), (9 * C2) ** -0.5, 0.15625),
        "enc_coarse_h": bell_draw(streams_of[8], (3, 3, C2, 3 * C2), (9 * C2) ** -0.5, 0.15625),
        "fc_coarse_h": bell_draw(streams_of[9], (3, 3, C2, 3 * C2), (9 * C2) ** -0.5, 0.15625),
        "fc_up": bell_draw(streams_of[10], (3, 3, C2, C1), (3 * C2) ** -0.5, 0.25),
        "fc_fine_x": bell_draw(streams_of[11], (3, 3, C1, 3 * C1), (9 * C1) ** -0.5, 0.25),
        "fc_fine_h": bell_draw(streams_of[12], (3, 3, C1, 3 * C1), (9 * C1) ** -0.5, 0.25),
        "fc_head": bell_draw(streams_of[13], (C1, PATCH), C1 ** -0.5, 0.75),
    }


def convolve(values, kernel, strides, padding, dilation):
    return lax.conv_general_dilated(values[None], kernel, strides, padding, lhs_dilation=dilation, dimension_numbers=("NHWC", "HWIO", "NHWC"), preferred_element_type=jnp.float32)[0]


def same_conv(values, kernel):
    return convolve(values, kernel, (1, 1), ((1, 1), (1, 1)), (1, 1))


def leaky(values):
    return jnp.where(values > 0, values, 0.2 * values)


def gate_update(from_input, from_state, state):
    width = state.shape[-1]
    if from_input is None:
        mixed = from_state[..., :2 * width]
        cand_input = 0.0
    else:
        mixed = from_input[..., :2 * width] + from_state[..., :2 * width]
        cand_input = from_input[..., 2 * width:]
    reset = jax.nn.sigmoid(mixed[..., :width])
    update = jax.nn.sigmoid(mixed[..., width:])
    candidate = jnp.tanh(cand_input + reset * from_state[..., 2 * width:])
    return ((1.0 - update) * candidate + update * state.astype(jnp.float32)).astype(jnp.bfloat16)


def reference(frames, start_fine, start_coarse, enc_stem, enc_fine_x, enc_fine_h, enc_down, enc_coarse_x, enc_coarse_h, fc_coarse_h, fc_up, fc_fine_x, fc_fine_h, fc_head):
    fine_state = start_fine.reshape(ROWS, COLS, C1)
    coarse_state = start_coarse.reshape(ROWS // 2, COLS // 2, C2)
    for frame_index in range(FRAMES):
        patches = frames[frame_index].reshape(ROWS * COLS, PATCH)
        stem_out = leaky(jnp.dot(patches, enc_stem, preferred_element_type=jnp.float32)).astype(jnp.bfloat16).reshape(ROWS, COLS, C1)
        fine_state = gate_update(same_conv(stem_out, enc_fine_x), same_conv(fine_state, enc_fine_h), fine_state)
        lowered = leaky(convolve(fine_state, enc_down, (2, 2), ((1, 1), (1, 1)), (1, 1))).astype(jnp.bfloat16)
        coarse_state = gate_update(same_conv(lowered, enc_coarse_x), same_conv(coarse_state, enc_coarse_h), coarse_state)
    outputs = []
    for step_index in range(HORIZON):
        coarse_state = gate_update(None, same_conv(coarse_state, fc_coarse_h), coarse_state)
        raised = leaky(convolve(coarse_state, fc_up, (1, 1), ((1, 2), (1, 2)), (2, 2))).astype(jnp.bfloat16)
        fine_state = gate_update(same_conv(raised, fc_fine_x), same_conv(fine_state, fc_fine_h), fine_state)
        predicted = jnp.dot(fine_state.reshape(ROWS * COLS, C1), fc_head, preferred_element_type=jnp.float32)
        outputs.append(predicted.astype(jnp.bfloat16).reshape(ROWS, COLS * PATCH))
    return jnp.stack(outputs)
```

```python
import jax
import jax.numpy as jnp
from jax import lax
from jax.experimental import pallas as pl
from jax.experimental.pallas import tpu as pltpu
from jax.sharding import PartitionSpec as P

C1 = 64
C2 = 192
PATCH = 16
FRAMES = 2
HORIZON = 2
COLS = 512
SUB = 16
FB = COLS // SUB
CB = COLS // 2 // SUB
LANES = 128
BF = jnp.bfloat16
F32 = jnp.float32
LINE = ("tile", "section")


def leaky(values):
    return jnp.where(values > 0, values, 0.2 * values)


def low_half(shape):
    return lax.broadcasted_iota(jnp.int32, shape, len(shape) - 1) < 64


def swap_halves(x):
    flat = x.reshape(-1, LANES)
    return pltpu.roll(flat, 64, 1).reshape(x.shape)


def swap_bf(x):
    return swap_halves(x.astype(F32)).astype(BF)


def sigmoid(x):
    return 0.5 * jnp.tanh(0.5 * x) + 0.5


def shift_sub(x, by):
    wide = x.astype(F32)
    row = lax.broadcasted_iota(jnp.int32, wide.shape, 0)
    if by > 0:
        moved = jnp.where(row == 0, 0.0, pltpu.roll(wide, 1, 0))
    else:
        moved = jnp.where(row == SUB - 1, 0.0, pltpu.roll(wide, SUB - 1, 0))
    return moved.astype(BF)


def seal(ref, idx, blocks):
    ref[idx, 0] = shift_sub(ref[idx, blocks], 1)
    ref[idx, blocks + 1] = shift_sub(ref[idx, 1], -1)


def fine_patches(ref, idx, lo, count):
    parts = [
        ref[idx + dr, pl.ds(lo + dj, count)].reshape(count * SUB, LANES)
        for dr in (-1, 0, 1)
        for dj in (0, 1, 2)
    ]
    return jnp.concatenate(parts, axis=-1)


def fine_gru(src, idx, weight, valid, emit):
    count = 16
    for lo in range(0, FB, count):
        acc = jnp.dot(fine_patches(src, idx, lo, count), weight[...], preferred_element_type=F32)
        gates = sigmoid(acc[:, :LANES])
        cand = acc[:, LANES:]
        cand = jnp.tanh(cand + swap_halves(gates * cand))
        old = src[idx, pl.ds(1 + lo, count)].reshape(count * SUB, LANES).astype(F32)
        new = (1.0 - gates) * cand + gates * old
        new = jnp.where(valid, new, 0.0).astype(BF)
        emit(lo, count, new.reshape(count, SUB, LANES))


def down_row(src, idx, weight):
    parts = []
    for dr in (-1, 0, 1):
        row = src[idx + dr].reshape(FB // 2 + 1, 2, SUB, LANES)
        for tap in (row[:CB, 0], row[:CB, 1], row[1:, 0]):
            parts.append(tap.reshape(CB * SUB, LANES))
    lhs = jnp.concatenate(parts, axis=-1)
    return jnp.dot(lhs, weight[...], preferred_element_type=F32)


def coarse_forms(t0, t1):
    lo = low_half(t0.shape)
    r0, r1 = swap_halves(t0), swap_halves(t1)
    return (
        t0.astype(BF),
        jnp.where(lo, t1, 0.0).astype(BF),
        jnp.where(lo, 0.0, r0).astype(BF),
        jnp.where(lo, r0, r1).astype(BF),
    )


def put_forms(ref, idx, forms):
    for k, tile in enumerate(forms):
        ref[idx, 1 : CB + 1, :, k * LANES : (k + 1) * LANES] = tile.reshape(CB, SUB, LANES)
    seal(ref, idx, CB)


def put_packed(ref, idx, tiles):
    t = [tiles(i).astype(F32) for i in range(3)]
    r = [swap_halves(x) for x in t]
    lo = low_half(t[0].shape)
    even = (t[0], jnp.where(lo, t[1], 0.0), jnp.where(lo, 0.0, r[0]), jnp.where(lo, r[0], r[1]))
    odd = (
        jnp.where(lo, r[1], r[2]),
        jnp.where(lo, r[2], 0.0),
        jnp.where(lo, 0.0, t[1]),
        t[2],
    )
    for k in range(4):
        both = jnp.stack([even[k].astype(BF), odd[k].astype(BF)], axis=1)
        ref[idx, 1 : CB + 1, :, k * LANES : (k + 1) * LANES] = both.reshape(CB, SUB, LANES)
    seal(ref, idx, CB)


def pack_forms(forms):
    f = [x.reshape(CB // 2, 2, SUB, LANES) for x in forms]
    lo = low_half((CB // 2, SUB, LANES))
    return (f[0][:, 0], jnp.where(lo, f[1][:, 0], f[2][:, 1]), f[3][:, 1])


def coarse_patches(ref, idx):
    def tile(dr, dj, k):
        return ref[idx + dr, dj : dj + CB, :, k * LANES : (k + 1) * LANES].reshape(CB * SUB, LANES)

    lo = low_half((CB * SUB, LANES))

    def aligned(dr):
        return [
            tile(dr, 0, 0),
            jnp.where(lo, tile(dr, 0, 1), tile(dr, 1, 2)),
            tile(dr, 1, 3),
            tile(dr, 2, 0),
        ]

    parts = aligned(-1)
    parts.append(jnp.where(lo, tile(-1, 2, 1), tile(0, 0, 2)))
    parts += [tile(0, 0, 3), tile(0, 1, 0), jnp.where(lo, tile(0, 1, 1), tile(0, 2, 2)), tile(0, 2, 3)]
    parts += aligned(1)
    parts.append(tile(1, 2, 1))
    return jnp.concatenate(parts, axis=-1)[:, : 9 * C2]


def coarse_gru(x_ref, x_idx, h_ref, h_idx, w_x, w_h, acc_x, acc_h, valid):
    width = 3 * C2
    acc_h[:, :width] = jnp.dot(coarse_patches(h_ref, h_idx), w_h[...], preferred_element_type=F32)
    if x_ref is not None:
        acc_x[:, :width] = jnp.dot(coarse_patches(x_ref, x_idx), w_x[...], preferred_element_type=F32)

    def part(ref, k):
        return ref[:, k * LANES : (k + 1) * LANES]

    gates = []
    for k in range(3):
        mixed = part(acc_h, k)
        if x_ref is not None:
            mixed = part(acc_x, k) + mixed
        gates.append(sigmoid(mixed))
    lo = low_half(gates[0].shape)
    g1, g2 = swap_halves(gates[1]), swap_halves(gates[2])
    update = (jnp.where(lo, g1, g2), g2)
    out = []
    for k in range(2):
        cand = gates[k] * part(acc_h, 3 + k)
        if x_ref is not None:
            cand = part(acc_x, 3 + k) + cand
        cand = jnp.tanh(cand)
        old = h_ref[h_idx, 1 : CB + 1, :, k * LANES : (k + 1) * LANES].reshape(CB * SUB, LANES).astype(F32)
        new = (1.0 - update[k]) * cand + update[k] * old
        out.append(jnp.where(valid, new, 0.0).astype(BF).astype(F32))
    return coarse_forms(out[0], out[1])


def in_grid(row, rows):
    return jnp.logical_and(row >= 0, row < rows)


def fine_encoder_body(
    where_ref, own, outer, inner, fr_own, fr_outer, fr_inner, w_stem, w_gru, w_down,
    state_out, low_own, low_outer, low_inner, p1, p2, p3, stem2,
):
    upper = where_ref[0] == 0
    first = where_ref[1] * 4
    rows = where_ref[2] * 4
    lo = low_half((1, SUB, LANES))

    def pick(own_ref, outer_ref, inner_ref, idx, lanes, frame=None):
        def at(ref, r):
            return ref[r, :, lanes] if frame is None else ref[frame, r, :, lanes]

        if 3 <= idx < 7:
            return at(own_ref, idx - 3)
        r = idx + 1 if idx < 3 else idx - 7
        a, b = at(outer_ref, r), at(inner_ref, r)
        return jnp.where(upper, a, b) if idx < 3 else jnp.where(upper, b, a)

    for frame in range(FRAMES):
        for t in range(4):
            lanes = slice(t * LANES, (t + 1) * LANES)
            patches = jnp.concatenate(
                [pick(fr_own, fr_outer, fr_inner, idx, lanes, frame) for idx in range(9)], axis=0
            )
            for half in range(2):
                acc = jnp.dot(patches, w_stem[:, half * 512 : half * 512 + 512], preferred_element_type=F32)
                acc = leaky(acc).astype(BF)
                for k in range(4):
                    block = acc[:, k * LANES : (k + 1) * LANES].reshape(9, SUB, LANES)
                    at = 8 * t + 4 * half + k
                    if frame == 0:
                        p1[:, 1 + at] = block
                    else:
                        stem2[:, at] = block
    for idx in range(9):
        for k in range(FB // 2):
            pair = pick(own, outer, inner, idx, slice(k * LANES, (k + 1) * LANES))
            p1[idx, 1 + 2 * k] = jnp.where(lo[0], p1[idx, 1 + 2 * k], swap_bf(pair))
            p1[idx, 2 + 2 * k] = jnp.where(lo[0], p1[idx, 2 + 2 * k], pair)
        seal(p1, idx, FB)

    @pl.loop(1, 8)
    def _(idx):
        def emit(lo_block, count, new):
            stems = stem2[idx, pl.ds(lo_block, count)]
            p2[idx, pl.ds(1 + lo_block, count)] = jnp.where(lo, stems, new)

        fine_gru(p1, idx, w_gru, in_grid(first + idx - 3, rows), emit)
        seal(p2, idx, FB)

    @pl.loop(2, 7)
    def _(idx):
        def emit(lo_block, count, new):
            p3[idx, pl.ds(1 + lo_block, count)] = jnp.where(lo, jnp.zeros_like(new), new)

        fine_gru(p2, idx, w_gru, in_grid(first + idx - 3, rows), emit)
        seal(p3, idx, FB)

    def lowered(src, p):
        acc = leaky(down_row(src, 3 + 2 * p, w_down)).astype(BF).astype(F32)
        return pack_forms(coarse_forms(acc[:, :LANES], acc[:, LANES:]))

    def put(ref, at, tiles):
        for k, tile in enumerate(tiles):
            ref[at, :, :, k * LANES : (k + 1) * LANES] = tile

    for p in range(2):
        tiles = lowered(p2, p)
        put(low_own, p, tiles)
        put(low_outer, p, tiles)
        put(low_inner, p, tiles)
    for p in range(2):
        tiles = lowered(p3, p)
        put(low_own, 2 + p, tiles)
        to_outer = upper if p == 0 else jnp.logical_not(upper)

        @pl.when(to_outer)
        def _():
            put(low_outer, 2, tiles)

        @pl.when(jnp.logical_not(to_outer))
        def _():
            put(low_inner, 2, tiles)

    for r in range(4):
        for k in range(FB // 2):
            state_out[r, k] = jnp.where(lo[0], swap_bf(p3[3 + r, 1 + 2 * k]), p3[3 + r, 2 + 2 * k])


def zero_tail(acc):
    acc[:, 4 * LANES :] = jnp.zeros((CB * SUB, LANES), F32)


def packed_tiles(ref, at):
    return lambda i: ref[at, :, :, i * LANES : (i + 1) * LANES]


def coarse_encoder_body(
    where_ref, own, outer, inner, low_own, low_outer, low_inner, w_x, w_h,
    state_out, x1, x2, h0, h1, acc_x, acc_h,
):
    upper = where_ref[0] == 0
    first = where_ref[1] * 2
    rows = where_ref[2] * 2
    zero_tail(acc_x)
    zero_tail(acc_h)

    def raw_tiles(get):
        def tiles(i):
            return jnp.stack([get(slice((3 * k + i) * LANES, (3 * k + i + 1) * LANES)) for k in range(CB // 2)])

        return tiles

    for idx in range(6):
        if 2 <= idx < 4:
            put_packed(h0, idx, raw_tiles(lambda lanes: own[idx - 2, :, lanes]))
            put_packed(x1, idx, packed_tiles(low_own, idx - 2))
            continue
        r = idx if idx < 2 else idx - 4
        first_ref, second_ref = (outer, inner) if idx < 2 else (inner, outer)
        put_packed(
            h0, idx, raw_tiles(lambda lanes: jnp.where(upper, first_ref[r, :, lanes], second_ref[r, :, lanes]))
        )
        low_a, low_b = (low_outer, low_inner) if idx < 2 else (low_inner, low_outer)
        put_packed(x1, idx, lambda i: jnp.where(upper, packed_tiles(low_a, r)(i), packed_tiles(low_b, r)(i)))
    put_packed(x2, 1, packed_tiles(low_own, 2))
    put_packed(x2, 2, packed_tiles(low_own, 3))
    put_packed(x2, 0, lambda i: jnp.where(upper, packed_tiles(low_outer, 2)(i), packed_tiles(low_inner, 2)(i)))
    put_packed(x2, 3, lambda i: jnp.where(upper, packed_tiles(low_inner, 2)(i), packed_tiles(low_outer, 2)(i)))

    @pl.loop(0, 4)
    def _(idx):
        forms = coarse_gru(x1, idx + 1, h0, idx + 1, w_x, w_h, acc_x, acc_h, in_grid(first + idx - 1, rows))
        put_forms(h1, idx, forms)

    @pl.loop(0, 2)
    def _(idx):
        forms = coarse_gru(x2, idx + 1, h1, idx + 1, w_x, w_h, acc_x, acc_h, in_grid(first + idx, rows))
        for k, tile in enumerate(pack_forms(forms)):
            state_out[idx, :, :, k * LANES : (k + 1) * LANES] = tile


def raise_pair(src, idx, weight):
    def tile(dr, dj, k):
        return src[idx + dr, 1 + dj : 1 + dj + CB, :, k * LANES : (k + 1) * LANES].reshape(CB * SUB, LANES)

    lo = low_half((CB * SUB, LANES))
    parts = []
    for dr in (0, 1):
        parts += [tile(dr, 0, 0), jnp.where(lo, tile(dr, 0, 1), tile(dr, 1, 2)), tile(dr, 1, 3)]
    return jnp.dot(jnp.concatenate(parts, axis=-1), weight[...], preferred_element_type=F32)


def forecaster_body(
    where_ref, c_own, c_outer, c_inner, c_third, f_own, f_outer, f_inner, w_h, w_up, w_gru, w_head,
    out, h2, s1, s2, pf1, pf2, states, acc_h,
):
    upper = where_ref[0] == 0
    first_c = where_ref[1] * 2
    rows_c = where_ref[2] * 2
    first_f = where_ref[1] * 4
    rows_f = where_ref[2] * 4
    lo = low_half((1, SUB, LANES))
    zero_tail(acc_h)

    put_packed(h2, 3, packed_tiles(c_own, 0))
    put_packed(h2, 4, packed_tiles(c_own, 1))

    def either(a, b):
        return lambda i: jnp.where(upper, a(i), b(i))

    put_packed(h2, 0, either(packed_tiles(c_outer, 0), packed_tiles(c_third, 0)))
    put_packed(h2, 1, either(packed_tiles(c_outer, 1), packed_tiles(c_inner, 0)))
    put_packed(h2, 2, either(packed_tiles(c_outer, 2), packed_tiles(c_inner, 1)))
    put_packed(h2, 5, either(packed_tiles(c_inner, 0), packed_tiles(c_outer, 0)))
    put_packed(h2, 6, either(packed_tiles(c_inner, 1), packed_tiles(c_outer, 1)))
    put_packed(h2, 7, either(packed_tiles(c_third, 0), packed_tiles(c_outer, 2)))

    for idx in range(8):
        for k in range(FB // 2):
            if 2 <= idx < 6:
                pair = f_own[idx - 2, k]
            elif idx < 2:
                pair = jnp.where(upper, f_outer[2 + idx, k], f_inner[2 + idx, k])
            else:
                pair = jnp.where(upper, f_inner[idx - 6, k], f_outer[idx - 6, k])
            pf1[idx, 1 + 2 * k] = swap_bf(pair)
            pf1[idx, 2 + 2 * k] = pair

    @pl.loop(0, 6)
    def _(idx):
        forms = coarse_gru(None, 0, h2, idx + 1, None, w_h, None, acc_h, in_grid(first_c + idx - 2, rows_c))
        put_forms(s1, idx, forms)

    @pl.loop(0, 4)
    def _(idx):
        forms = coarse_gru(None, 0, s1, idx + 1, None, w_h, None, acc_h, in_grid(first_c + idx - 1, rows_c))
        put_forms(s2, idx, forms)

    s2[4] = jnp.zeros(s2.shape[1:], BF)

    def raise_rows(src, idx, fine, at, coarse_row):
        acc = raise_pair(src, idx, w_up)
        acc = jnp.where(in_grid(coarse_row, rows_c), leaky(acc), 0.0)
        for half, row in enumerate(at):
            if row is None:
                continue
            tile = acc[:, half * LANES : (half + 1) * LANES]
            even = tile.astype(BF).reshape(CB, SUB, LANES)
            odd = swap_halves(tile).astype(BF).reshape(CB, SUB, LANES)
            both = jnp.stack([even, odd], axis=1).reshape(FB, SUB, LANES)
            fine[row, 1 : FB + 1] = jnp.where(lo, both, fine[row, 1 : FB + 1])

    @pl.loop(0, 4)
    def _(k):
        raise_rows(s1, k + 1, pf1, (2 * k, 2 * k + 1), first_c + k - 1)
        seal(pf1, 2 * k, FB)
        seal(pf1, 2 * k + 1, FB)

    @pl.loop(0, 6)
    def _(idx):
        def emit(lo_block, count, new):
            pf2[idx, pl.ds(1 + lo_block, count)] = new

        fine_gru(pf1, idx + 1, w_gru, in_grid(first_f + idx - 1, rows_f), emit)

    def head(step, ref, base):
        for t in range(4):
            lhs = jnp.concatenate(
                [ref[base : base + 4, 1 + 8 * t + k].reshape(4 * SUB, LANES) for k in range(8)], axis=-1
            )
            acc = jnp.dot(lhs, w_head[...], preferred_element_type=F32).astype(BF)
            out[step, :, :, t * LANES : (t + 1) * LANES] = acc.reshape(4, SUB, LANES)

    head(0, pf2, 1)

    raise_rows(s2, 0, pf2, (None, 0), first_c - 1)
    raise_rows(s2, 1, pf2, (1, 2), first_c)
    raise_rows(s2, 2, pf2, (3, 4), first_c + 1)
    raise_rows(s2, 3, pf2, (5, None), first_c + 2)
    for idx in range(6):
        seal(pf2, idx, FB)

    @pl.loop(0, 4)
    def _(idx):
        def emit(lo_block, count, new):
            states[idx, pl.ds(1 + lo_block, count)] = new

        fine_gru(pf2, idx + 1, w_gru, True, emit)

    head(1, states, 0)


def fine_weight(kernel_x, kernel_h):
    x = kernel_x.reshape(9, C1, 3 * C1)
    h = kernel_h.reshape(9, C1, 3 * C1)
    none = jnp.zeros((9, C1, C1), BF)
    top = jnp.concatenate([x[..., : 2 * C1], none, x[..., 2 * C1 :]], axis=-1)
    low = jnp.concatenate([h, none], axis=-1)
    return jnp.concatenate([top, low], axis=1).reshape(9 * LANES, 2 * LANES)


def down_weight(kernel):
    k = kernel.reshape(9, C1, C2)
    return jnp.pad(k, ((0, 0), (C1, 0), (0, 2 * LANES - C2))).reshape(9 * LANES, 2 * LANES)


def up_weight(kernel):
    none = jnp.zeros((C2, C1), BF)

    def rows(even, odd):
        def group(a):
            if a is None:
                return [none, none], [none, none]
            return [kernel[a, 1], kernel[a, 0]], [none, kernel[a, 2]]

        e, o = group(even), group(odd)
        return [jnp.concatenate(e[i] + o[i], axis=-1) for i in range(2)]

    return jnp.concatenate(rows(1, 0) + rows(None, 2), axis=0)


def stem_weight(kernel):
    eye = jnp.eye(8, dtype=BF)
    wide = jnp.pad(kernel, ((0, 0), (0, LANES - C1)))
    return (eye[:, None, :, None] * wide[None, :, None, :]).reshape(8 * PATCH, 8 * LANES)


def head_weight(kernel):
    eye = jnp.eye(8, dtype=BF)
    tall = jnp.pad(kernel, ((LANES - C1, 0), (0, 0)))
    return (eye[:, None, :, None] * tall[None, :, None, :]).reshape(8 * LANES, 8 * PATCH)


def call(body, name, args, outs, scratch):
    return pl.pallas_call(
        body,
        name=name,
        out_shape=[jax.ShapeDtypeStruct(s, BF) for s in outs],
        in_specs=[pl.BlockSpec(memory_space=pltpu.SMEM)]
        + [pl.BlockSpec(memory_space=pltpu.VMEM)] * (len(args) - 1),
        out_specs=[pl.BlockSpec(memory_space=pltpu.VMEM)] * len(outs),
        scratch_shapes=scratch,
        compiler_params=pltpu.CompilerParams(vmem_limit_bytes=48 * 1024 * 1024),
    )(*args)


def on_device(
    frames,
    start_fine,
    start_coarse,
    enc_stem,
    enc_fine_x,
    enc_fine_h,
    enc_down,
    enc_coarse_x,
    enc_coarse_h,
    fc_coarse_h,
    fc_up,
    fc_fine_x,
    fc_fine_h,
    fc_head,
):
    count = lax.axis_size(LINE)
    section = lax.axis_index("section")
    position = lax.axis_index(LINE)
    where = jnp.stack([section, position, jnp.int32(count)]).astype(jnp.int32)
    across = [(i, i + 1) for i in range(1, count - 1, 2)]
    across = across + [(b, a) for a, b in across]

    def outer_swap(x):
        return lax.ppermute(x, LINE, across)

    def inner_swap(x):
        return lax.ppermute(x, "section", [(0, 1), (1, 0)])

    fine = start_fine.reshape(4, SUB, FB * C1)
    coarse = start_coarse.reshape(2, SUB, CB * C2)
    patches = frames.reshape(FRAMES, 4, SUB, FB * PATCH)
    fine_o, fr_o = outer_swap(fine), outer_swap(patches)
    fine_i, fr_i = inner_swap(fine), inner_swap(patches)
    coarse_o, coarse_i = outer_swap(coarse), inner_swap(coarse)

    w_enc = fine_weight(enc_fine_x, enc_fine_h)
    w_fc = fine_weight(fc_fine_x, fc_fine_h)

    def fine_buf(rows):
        return pltpu.VMEM((rows, FB + 2, SUB, LANES), BF)

    def coarse_buf(rows):
        return pltpu.VMEM((rows, CB + 2, SUB, 4 * LANES), BF)

    acc_buf = pltpu.VMEM((CB * SUB, 5 * LANES), F32)
    packed = (CB // 2, SUB, 3 * LANES)

    state_f, low_own, low_o, low_i = call(
        fine_encoder_body,
        "fine_encoder",
        [where, fine, fine_o, fine_i, patches, fr_o, fr_i, stem_weight(enc_stem), w_enc, down_weight(enc_down)],
        [(4, FB // 2, SUB, LANES), (4,) + packed, (3,) + packed, (3,) + packed],
        [fine_buf(9), fine_buf(9), fine_buf(9), pltpu.VMEM((9, FB, SUB, LANES), BF)],
    )
    got_o, got_i = outer_swap(low_o), inner_swap(low_i)
    state_fo, state_fi = outer_swap(state_f), inner_swap(state_f)

    flat = (9 * C2, 3 * C2)
    (state_c,) = call(
        coarse_encoder_body,
        "coarse_encoder",
        [where, coarse, coarse_o, coarse_i, low_own, got_o, got_i, enc_coarse_x.reshape(flat), enc_coarse_h.reshape(flat)],
        [(2,) + packed],
        [coarse_buf(6), coarse_buf(4), coarse_buf(6), coarse_buf(4), acc_buf, acc_buf],
    )
    state_ci = inner_swap(state_c)
    near = jnp.where(section == 0, state_ci[0], state_ci[1])[None]
    send = jnp.where(
        section == 0,
        jnp.concatenate([state_c, near], axis=0),
        jnp.concatenate([near, state_c], axis=0),
    )
    state_co = outer_swap(send)
    third = inner_swap(jnp.where(section == 0, state_co[2], state_co[0])[None])

    (out,) = call(
        forecaster_body,
        "forecaster",
        [where, state_c, state_co, state_ci, third, state_f, state_fo, state_fi,
         fc_coarse_h.reshape(flat), up_weight(fc_up), w_fc, head_weight(fc_head)],
        [(HORIZON, 4, SUB, FB * PATCH)],
        [coarse_buf(8), coarse_buf(6), coarse_buf(5), fine_buf(8), fine_buf(6), fine_buf(4), acc_buf],
    )
    return out.reshape(HORIZON, 4, COLS * PATCH)


def solution(mesh):
    line = ("groups", "tile", "section")
    return jax.shard_map(
        on_device,
        mesh=mesh,
        in_specs=(P(None, line, None), P(line, None), P(line, None)) + (P(),) * 11,
        out_specs=P(None, line, None),
        check_vma=False,
    )
```

```python
import jax
import jax.numpy as jnp
from jax import lax
from jax.experimental import pallas as pl
from jax.experimental.pallas import tpu as pltpu
from jax.sharding import PartitionSpec as P

C1 = 64
C2 = 192
PATCH = 16
FRAMES = 2
HORIZON = 2
COLS = 512
SUB = 16
FB = COLS // SUB
CB = COLS // 2 // SUB
LANES = 128
BF = jnp.bfloat16
F32 = jnp.float32
LINE = ("tile", "section")
PAIRS = CB // 2
ROW_TILES = 3 * PAIRS


def leaky(values):
    return jnp.where(values > 0, values, 0.2 * values)


def low_half(shape):
    return lax.broadcasted_iota(jnp.int32, shape, len(shape) - 1) < 64


def swap_halves(x):
    flat = x.reshape(-1, LANES)
    return pltpu.roll(flat, 64, 1).reshape(x.shape)


def swap_bf(x):
    return swap_halves(x.astype(F32)).astype(BF)


def sigmoid(x):
    return 0.5 * jnp.tanh(0.5 * x) + 0.5


def shift_sub(x, by):
    wide = x.astype(F32)
    row = lax.broadcasted_iota(jnp.int32, wide.shape, 0)
    if by > 0:
        moved = jnp.where(row == 0, 0.0, pltpu.roll(wide, 1, 0))
    else:
        moved = jnp.where(row == SUB - 1, 0.0, pltpu.roll(wide, SUB - 1, 0))
    return moved.astype(BF)


def seal(ref, idx, blocks):
    ref[idx, 0] = shift_sub(ref[idx, blocks], 1)
    ref[idx, blocks + 1] = shift_sub(ref[idx, 1], -1)


def fine_patches(ref, idx, lo, count):
    parts = [
        ref[idx + dr, pl.ds(lo + dj, count)].reshape(count * SUB, LANES)
        for dr in (-1, 0, 1)
        for dj in (0, 1, 2)
    ]
    return jnp.concatenate(parts, axis=-1)


def fine_gru(src, idx, weight, valid, emit):
    count = 16
    for lo in range(0, FB, count):
        acc = jnp.dot(fine_patches(src, idx, lo, count), weight[...], preferred_element_type=F32)
        gates = sigmoid(acc[:, :LANES])
        cand = acc[:, LANES:]
        cand = jnp.tanh(cand + swap_halves(gates * cand))
        old = src[idx, pl.ds(1 + lo, count)].reshape(count * SUB, LANES).astype(F32)
        new = (1.0 - gates) * cand + gates * old
        new = jnp.where(valid, new, 0.0).astype(BF)
        emit(lo, count, new.reshape(count, SUB, LANES))


def down_row(src, idx, weight):
    parts = []
    for dr in (-1, 0, 1):
        row = src[idx + dr].reshape(FB // 2 + 1, 2, SUB, LANES)
        for tap in (row[:CB, 0], row[:CB, 1], row[1:, 0]):
            parts.append(tap.reshape(CB * SUB, LANES))
    lhs = jnp.concatenate(parts, axis=-1)
    return jnp.dot(lhs, weight[...], preferred_element_type=F32)


def coarse_forms(t0, t1):
    lo = low_half(t0.shape)
    r0, r1 = swap_halves(t0), swap_halves(t1)
    return (
        t0.astype(BF),
        jnp.where(lo, t1, 0.0).astype(BF),
        jnp.where(lo, 0.0, r0).astype(BF),
        jnp.where(lo, r0, r1).astype(BF),
    )


def put_forms(ref, idx, forms):
    for k, tile in enumerate(forms):
        ref[idx, 1 : CB + 1, :, k * LANES : (k + 1) * LANES] = tile.reshape(CB, SUB, LANES)
    seal(ref, idx, CB)


def put_packed(ref, idx, tiles):
    t = [tiles(i).astype(F32) for i in range(3)]
    r = [swap_halves(x) for x in t]
    lo = low_half(t[0].shape)
    even = (t[0], jnp.where(lo, t[1], 0.0), jnp.where(lo, 0.0, r[0]), jnp.where(lo, r[0], r[1]))
    odd = (
        jnp.where(lo, r[1], r[2]),
        jnp.where(lo, r[2], 0.0),
        jnp.where(lo, 0.0, t[1]),
        t[2],
    )
    for k in range(4):
        both = jnp.stack([even[k].astype(BF), odd[k].astype(BF)], axis=1)
        ref[idx, 1 : CB + 1, :, k * LANES : (k + 1) * LANES] = both.reshape(CB, SUB, LANES)
    seal(ref, idx, CB)


def pack_forms(forms):
    f = [x.reshape(CB // 2, 2, SUB, LANES) for x in forms]
    lo = low_half((CB // 2, SUB, LANES))
    return (f[0][:, 0], jnp.where(lo, f[1][:, 0], f[2][:, 1]), f[3][:, 1])


def coarse_patches(ref, idx):
    def tile(dr, dj, k):
        return ref[idx + dr, dj : dj + CB, :, k * LANES : (k + 1) * LANES].reshape(CB * SUB, LANES)

    lo = low_half((CB * SUB, LANES))

    def aligned(dr):
        return [
            tile(dr, 0, 0),
            jnp.where(lo, tile(dr, 0, 1), tile(dr, 1, 2)),
            tile(dr, 1, 3),
            tile(dr, 2, 0),
        ]

    parts = aligned(-1)
    parts.append(jnp.where(lo, tile(-1, 2, 1), tile(0, 0, 2)))
    parts += [tile(0, 0, 3), tile(0, 1, 0), jnp.where(lo, tile(0, 1, 1), tile(0, 2, 2)), tile(0, 2, 3)]
    parts += aligned(1)
    parts.append(tile(1, 2, 1))
    return jnp.concatenate(parts, axis=-1)[:, : 9 * C2]


def coarse_gru(x_ref, x_idx, h_ref, h_idx, w_x, w_h, acc_x, acc_h, valid):
    width = 3 * C2
    acc_h[:, :width] = jnp.dot(coarse_patches(h_ref, h_idx), w_h[...], preferred_element_type=F32)
    if x_ref is not None:
        acc_x[:, :width] = jnp.dot(coarse_patches(x_ref, x_idx), w_x[...], preferred_element_type=F32)

    def part(ref, k):
        return ref[:, k * LANES : (k + 1) * LANES]

    gates = []
    for k in range(3):
        mixed = part(acc_h, k)
        if x_ref is not None:
            mixed = part(acc_x, k) + mixed
        gates.append(sigmoid(mixed))
    lo = low_half(gates[0].shape)
    g1, g2 = swap_halves(gates[1]), swap_halves(gates[2])
    update = (jnp.where(lo, g1, g2), g2)
    out = []
    for k in range(2):
        cand = gates[k] * part(acc_h, 3 + k)
        if x_ref is not None:
            cand = part(acc_x, 3 + k) + cand
        cand = jnp.tanh(cand)
        old = h_ref[h_idx, 1 : CB + 1, :, k * LANES : (k + 1) * LANES].reshape(CB * SUB, LANES).astype(F32)
        new = (1.0 - update[k]) * cand + update[k] * old
        out.append(jnp.where(valid, new, 0.0).astype(BF).astype(F32))
    return coarse_forms(out[0], out[1])


def in_grid(row, rows):
    return jnp.logical_and(row >= 0, row < rows)


def fine_encoder_body(
    where_ref, own, outer, inner, w_stem, w_gru, w_down,
    state_out, low_own, to_outer, to_inner, p1, p2, p3, stem2,
):
    upper = where_ref[0] == 0
    first = where_ref[1] * 4
    rows = where_ref[2] * 4
    lo = low_half((1, SUB, LANES))

    def pick(idx, lanes):
        if 3 <= idx < 7:
            return own[idx - 3, :, lanes]
        r = idx + 1 if idx < 3 else idx - 7
        a, b = outer[r, :, lanes], inner[r, :, lanes]
        return jnp.where(upper, a, b) if idx < 3 else jnp.where(upper, b, a)

    for frame in range(FRAMES):
        for t in range(4):
            at = FB * C1 + frame * FB * PATCH + t * LANES
            patches = jnp.concatenate([pick(idx, slice(at, at + LANES)) for idx in range(9)], axis=0)
            for half in range(2):
                acc = jnp.dot(patches, w_stem[:, half * 512 : half * 512 + 512], preferred_element_type=F32)
                acc = leaky(acc).astype(BF)
                for k in range(4):
                    block = acc[:, k * LANES : (k + 1) * LANES].reshape(9, SUB, LANES)
                    at = 8 * t + 4 * half + k
                    if frame == 0:
                        p1[:, 1 + at] = block
                    else:
                        stem2[:, at] = block
    for idx in range(9):
        for k in range(FB // 2):
            pair = pick(idx, slice(k * LANES, (k + 1) * LANES))
            p1[idx, 1 + 2 * k] = jnp.where(lo[0], p1[idx, 1 + 2 * k], swap_bf(pair))
            p1[idx, 2 + 2 * k] = jnp.where(lo[0], p1[idx, 2 + 2 * k], pair)
        seal(p1, idx, FB)

    @pl.loop(1, 8)
    def _(idx):
        def emit(lo_block, count, new):
            stems = stem2[idx, pl.ds(lo_block, count)]
            p2[idx, pl.ds(1 + lo_block, count)] = jnp.where(lo, stems, new)

        fine_gru(p1, idx, w_gru, in_grid(first + idx - 3, rows), emit)
        seal(p2, idx, FB)

    @pl.loop(2, 7)
    def _(idx):
        def emit(lo_block, count, new):
            p3[idx, pl.ds(1 + lo_block, count)] = jnp.where(lo, jnp.zeros_like(new), new)

        fine_gru(p2, idx, w_gru, in_grid(first + idx - 3, rows), emit)
        seal(p3, idx, FB)

    def lowered(src, p):
        acc = leaky(down_row(src, 3 + 2 * p, w_down)).astype(BF).astype(F32)
        return pack_forms(coarse_forms(acc[:, :LANES], acc[:, LANES:]))

    def put(ref, at, tiles):
        for k, tile in enumerate(tiles):
            base = at * ROW_TILES + k * PAIRS
            ref[base : base + PAIRS] = tile

    for p in range(2):
        tiles = lowered(p2, p)
        put(low_own, p, tiles)
        put(to_outer, p, tiles)
        put(to_inner, p, tiles)
    for p in range(2):
        tiles = lowered(p3, p)
        put(low_own, 2 + p, tiles)
        outward = upper if p == 0 else jnp.logical_not(upper)

        @pl.when(outward)
        def _():
            put(to_outer, 2, tiles)

        @pl.when(jnp.logical_not(outward))
        def _():
            put(to_inner, 2, tiles)

    for r in range(4):
        for k in range(FB // 2):
            state_out[r, k] = jnp.where(lo[0], swap_bf(p3[3 + r, 1 + 2 * k]), p3[3 + r, 2 + 2 * k])
    base = 3 * ROW_TILES
    for top, ref in ((upper, to_outer), (jnp.logical_not(upper), to_inner)):
        start = jnp.where(top, 0, 2)
        for r in range(2):
            ref[base + r * FB // 2 : base + (r + 1) * FB // 2] = state_out[start + r]


def zero_tail(acc):
    acc[:, 4 * LANES :] = jnp.zeros((CB * SUB, LANES), F32)


def packed_tiles(ref, at):
    return lambda i: ref[at * ROW_TILES + i * PAIRS : at * ROW_TILES + (i + 1) * PAIRS]


def coarse_encoder_body(
    where_ref, own, outer, inner, low_own, low_outer, low_inner, w_x_hbm, w_h_hbm,
    state_out, x1, x2, h0, h1, acc_x, acc_h, w_x, w_h, sems,
):
    fetch_h = pltpu.make_async_copy(w_h_hbm, w_h, sems.at[0])
    fetch_x = pltpu.make_async_copy(w_x_hbm, w_x, sems.at[1])
    fetch_h.start()
    fetch_x.start()
    upper = where_ref[0] == 0
    first = where_ref[1] * 2
    rows = where_ref[2] * 2
    zero_tail(acc_x)
    zero_tail(acc_h)

    def raw_tiles(get):
        def tiles(i):
            return jnp.stack([get(slice((3 * k + i) * LANES, (3 * k + i + 1) * LANES)) for k in range(CB // 2)])

        return tiles

    for idx in range(6):
        if 2 <= idx < 4:
            put_packed(h0, idx, raw_tiles(lambda lanes: own[2 + idx, :, lanes]))
            put_packed(x1, idx, packed_tiles(low_own, idx - 2))
            continue
        r = idx if idx < 2 else idx - 4
        first_ref, second_ref = (outer, inner) if idx < 2 else (inner, outer)
        put_packed(
            h0, idx, raw_tiles(lambda lanes: jnp.where(upper, first_ref[4 + r, :, lanes], second_ref[4 + r, :, lanes]))
        )
        low_a, low_b = (low_outer, low_inner) if idx < 2 else (low_inner, low_outer)
        put_packed(x1, idx, lambda i: jnp.where(upper, packed_tiles(low_a, r)(i), packed_tiles(low_b, r)(i)))
    put_packed(x2, 1, packed_tiles(low_own, 2))
    put_packed(x2, 2, packed_tiles(low_own, 3))
    put_packed(x2, 0, lambda i: jnp.where(upper, packed_tiles(low_outer, 2)(i), packed_tiles(low_inner, 2)(i)))
    put_packed(x2, 3, lambda i: jnp.where(upper, packed_tiles(low_inner, 2)(i), packed_tiles(low_outer, 2)(i)))

    fetch_h.wait()
    fetch_x.wait()

    @pl.loop(0, 4)
    def _(idx):
        forms = coarse_gru(x1, idx + 1, h0, idx + 1, w_x, w_h, acc_x, acc_h, in_grid(first + idx - 1, rows))
        put_forms(h1, idx, forms)

    @pl.loop(0, 2)
    def _(idx):
        forms = coarse_gru(x2, idx + 1, h1, idx + 1, w_x, w_h, acc_x, acc_h, in_grid(first + idx, rows))
        for k, tile in enumerate(pack_forms(forms)):
            state_out[pl.ds(idx * ROW_TILES + k * PAIRS, PAIRS)] = tile


def raise_pair(src, idx, weight):
    def tile(dr, dj, k):
        return src[idx + dr, 1 + dj : 1 + dj + CB, :, k * LANES : (k + 1) * LANES].reshape(CB * SUB, LANES)

    lo = low_half((CB * SUB, LANES))
    parts = []
    for dr in (0, 1):
        parts += [tile(dr, 0, 0), jnp.where(lo, tile(dr, 0, 1), tile(dr, 1, 2)), tile(dr, 1, 3)]
    return jnp.dot(jnp.concatenate(parts, axis=-1), weight[...], preferred_element_type=F32)


def forecaster_body(
    where_ref, c_own, c_outer, c_inner, c_third, f_own, f_outer, f_inner, w_h_hbm, w_up, w_gru, w_head,
    out, h2, s1, s2, pf1, pf2, states, acc_h, w_h, sem,
):
    fetch_h = pltpu.make_async_copy(w_h_hbm, w_h, sem)
    fetch_h.start()
    upper = where_ref[0] == 0
    first_c = where_ref[1] * 2
    rows_c = where_ref[2] * 2
    first_f = where_ref[1] * 4
    rows_f = where_ref[2] * 4
    lo = low_half((1, SUB, LANES))
    zero_tail(acc_h)

    put_packed(h2, 3, packed_tiles(c_own, 0))
    put_packed(h2, 4, packed_tiles(c_own, 1))

    def either(a, b):
        return lambda i: jnp.where(upper, a(i), b(i))

    put_packed(h2, 0, either(packed_tiles(c_outer, 0), packed_tiles(c_third, 0)))
    put_packed(h2, 1, either(packed_tiles(c_outer, 1), packed_tiles(c_inner, 0)))
    put_packed(h2, 2, either(packed_tiles(c_outer, 2), packed_tiles(c_inner, 1)))
    put_packed(h2, 5, either(packed_tiles(c_inner, 0), packed_tiles(c_outer, 0)))
    put_packed(h2, 6, either(packed_tiles(c_inner, 1), packed_tiles(c_outer, 1)))
    put_packed(h2, 7, either(packed_tiles(c_third, 0), packed_tiles(c_outer, 2)))

    base = 3 * ROW_TILES
    for idx in range(8):
        for k in range(FB // 2):
            if 2 <= idx < 6:
                pair = f_own[idx - 2, k]
            elif idx < 2:
                pair = jnp.where(upper, f_outer[base + idx * FB // 2 + k], f_inner[base + idx * FB // 2 + k])
            else:
                at = base + (idx - 6) * FB // 2 + k
                pair = jnp.where(upper, f_inner[at], f_outer[at])
            pf1[idx, 1 + 2 * k] = swap_bf(pair)
            pf1[idx, 2 + 2 * k] = pair

    fetch_h.wait()

    @pl.loop(0, 6)
    def _(idx):
        forms = coarse_gru(None, 0, h2, idx + 1, None, w_h, None, acc_h, in_grid(first_c + idx - 2, rows_c))
        put_forms(s1, idx, forms)

    @pl.loop(0, 4)
    def _(idx):
        forms = coarse_gru(None, 0, s1, idx + 1, None, w_h, None, acc_h, in_grid(first_c + idx - 1, rows_c))
        put_forms(s2, idx, forms)

    s2[4] = jnp.zeros(s2.shape[1:], BF)

    def raise_rows(src, idx, fine, at, coarse_row):
        acc = raise_pair(src, idx, w_up)
        acc = jnp.where(in_grid(coarse_row, rows_c), leaky(acc), 0.0)
        for half, row in enumerate(at):
            if row is None:
                continue
            tile = acc[:, half * LANES : (half + 1) * LANES]
            even = tile.astype(BF).reshape(CB, SUB, LANES)
            odd = swap_halves(tile).astype(BF).reshape(CB, SUB, LANES)
            both = jnp.stack([even, odd], axis=1).reshape(FB, SUB, LANES)
            fine[row, 1 : FB + 1] = jnp.where(lo, both, fine[row, 1 : FB + 1])

    @pl.loop(0, 4)
    def _(k):
        raise_rows(s1, k + 1, pf1, (2 * k, 2 * k + 1), first_c + k - 1)
        seal(pf1, 2 * k, FB)
        seal(pf1, 2 * k + 1, FB)

    @pl.loop(0, 6)
    def _(idx):
        def emit(lo_block, count, new):
            pf2[idx, pl.ds(1 + lo_block, count)] = new

        fine_gru(pf1, idx + 1, w_gru, in_grid(first_f + idx - 1, rows_f), emit)

    def head(step, ref, base):
        for t in range(4):
            lhs = jnp.concatenate(
                [ref[base : base + 4, 1 + 8 * t + k].reshape(4 * SUB, LANES) for k in range(8)], axis=-1
            )
            acc = jnp.dot(lhs, w_head[...], preferred_element_type=F32).astype(BF)
            out[step, :, :, t * LANES : (t + 1) * LANES] = acc.reshape(4, SUB, LANES)

    head(0, pf2, 1)

    raise_rows(s2, 0, pf2, (None, 0), first_c - 1)
    raise_rows(s2, 1, pf2, (1, 2), first_c)
    raise_rows(s2, 2, pf2, (3, 4), first_c + 1)
    raise_rows(s2, 3, pf2, (5, None), first_c + 2)
    for idx in range(6):
        seal(pf2, idx, FB)

    @pl.loop(0, 4)
    def _(idx):
        def emit(lo_block, count, new):
            states[idx, pl.ds(1 + lo_block, count)] = new

        fine_gru(pf2, idx + 1, w_gru, True, emit)

    head(1, states, 0)


def to_upper(x):
    return jnp.concatenate([jnp.zeros(x.shape, F32), x.astype(F32)], axis=-1).astype(BF)


def to_lower(x):
    return jnp.concatenate([x.astype(F32), jnp.zeros(x.shape, F32)], axis=-1).astype(BF)


def prepare_body(
    stem, enc_x, enc_h, down, up, fc_x, fc_h, head, w_stem, w_enc, w_down, w_up, w_fc, w_head
):
    for kx, kh, w in ((enc_x, enc_h, w_enc), (fc_x, fc_h, w_fc)):
        for k in range(9):
            at = k * LANES
            w[at : at + C1, :LANES] = kx[k, :, :LANES]
            w[at : at + C1, LANES:] = to_upper(kx[k, :, LANES:])
            w[at + C1 : at + LANES, :LANES] = kh[k, :, :LANES]
            w[at + C1 : at + LANES, LANES:] = to_lower(kh[k, :, LANES:])
    for k in range(9):
        at = k * LANES
        w_down[at : at + C1] = jnp.zeros((C1, 2 * LANES), BF)
        w_down[at + C1 : at + LANES, :LANES] = down[k, :, :LANES]
        w_down[at + C1 : at + LANES, LANES:] = to_lower(down[k, :, LANES:])

    def tap(a, b):
        return jnp.zeros((C2, C1), F32) if a is None else up[3 * a + b].astype(F32)

    none = (None, None)
    for g, taps in enumerate((
        ((1, 1), (1, 0), (0, 1), (0, 0)),
        (none, (1, 2), none, (0, 2)),
        (none, none, (2, 1), (2, 0)),
        (none, none, none, (2, 2)),
    )):
        for n in range(2):
            pair = jnp.concatenate([tap(*taps[2 * n]), tap(*taps[2 * n + 1])], axis=-1)
            w_up[g * C2 : (g + 1) * C2, n * LANES : (n + 1) * LANES] = pair.astype(BF)

    w_stem[...] = jnp.zeros(w_stem.shape, BF)
    w_head[...] = jnp.zeros(w_head.shape, BF)
    wide = to_lower(stem[...])
    for k in range(8):
        w_stem[k * PATCH : (k + 1) * PATCH, k * LANES : (k + 1) * LANES] = wide
        w_head[k * LANES + C1 : (k + 1) * LANES, k * PATCH : (k + 1) * PATCH] = head[...]


def call(body, name, args, outs, scratch):
    return pl.pallas_call(
        body,
        name=name,
        out_shape=[jax.ShapeDtypeStruct(s, BF) for s in outs],
        in_specs=[pl.BlockSpec(memory_space=space) for _, space in args],
        out_specs=[pl.BlockSpec(memory_space=pltpu.VMEM)] * len(outs),
        scratch_shapes=scratch,
        compiler_params=pltpu.CompilerParams(vmem_limit_bytes=24 * 1024 * 1024),
    )(*[arg for arg, _ in args])


def on_device(
    frames,
    start_fine,
    start_coarse,
    enc_stem,
    enc_fine_x,
    enc_fine_h,
    enc_down,
    enc_coarse_x,
    enc_coarse_h,
    fc_coarse_h,
    fc_up,
    fc_fine_x,
    fc_fine_h,
    fc_head,
):
    count = lax.axis_size(LINE)
    section = lax.axis_index("section")
    position = lax.axis_index(LINE)
    where = jnp.stack([section, position, jnp.int32(count)]).astype(jnp.int32)
    across = [(i, i + 1) for i in range(1, count - 1, 2)]
    across = across + [(b, a) for a, b in across]

    def outer_swap(x):
        return lax.ppermute(x, LINE, across)

    def inner_swap(x):
        return lax.ppermute(x, "section", [(0, 1), (1, 0)])

    fine = start_fine.reshape(4, SUB, FB * C1)
    patches = frames.reshape(FRAMES, 4, SUB, FB * PATCH)
    coarse = start_coarse.reshape(2, SUB, CB * C2)
    own = jnp.concatenate([fine, patches[0], patches[1]], axis=-1)
    own = jnp.concatenate([own, coarse], axis=0)
    outer, inner = outer_swap(own), inner_swap(own)

    def on_chip(*values):
        return [(value, pltpu.VMEM) for value in values]

    def in_hbm(*values):
        return [(value, pltpu.HBM) for value in values]

    def fine_buf(rows):
        return pltpu.VMEM((rows, FB + 2, SUB, LANES), BF)

    def coarse_buf(rows):
        return pltpu.VMEM((rows, CB + 2, SUB, 4 * LANES), BF)

    place = [(where, pltpu.SMEM)]
    acc_buf = pltpu.VMEM((CB * SUB, 5 * LANES), F32)
    flat = (9 * C2, 3 * C2)
    big = pltpu.VMEM(flat, BF)

    w_stem, w_enc, w_down, w_up, w_fc, w_head = call(
        prepare_body,
        "prepare",
        on_chip(
            enc_stem,
            enc_fine_x.reshape(9, C1, 3 * C1),
            enc_fine_h.reshape(9, C1, 3 * C1),
            enc_down.reshape(9, C1, C2),
            fc_up.reshape(9, C2, C1),
            fc_fine_x.reshape(9, C1, 3 * C1),
            fc_fine_h.reshape(9, C1, 3 * C1),
            fc_head,
        ),
        [
            (8 * PATCH, 8 * LANES),
            (9 * LANES, 2 * LANES),
            (9 * LANES, 2 * LANES),
            (4 * C2, 2 * LANES),
            (9 * LANES, 2 * LANES),
            (8 * LANES, 8 * PATCH),
        ],
        [],
    )
    halo = (3 * ROW_TILES + FB, SUB, LANES)
    state_f, low_own, to_outer, to_inner = call(
        fine_encoder_body,
        "fine_encoder",
        place + on_chip(own, outer, inner, w_stem, w_enc, w_down),
        [(4, FB // 2, SUB, LANES), (4 * ROW_TILES, SUB, LANES), halo, halo],
        [fine_buf(9), fine_buf(9), fine_buf(9), pltpu.VMEM((9, FB, SUB, LANES), BF)],
    )
    got_o, got_i = outer_swap(to_outer), inner_swap(to_inner)

    (state_c,) = call(
        coarse_encoder_body,
        "coarse_encoder",
        place
        + on_chip(own, outer, inner, low_own, got_o, got_i)
        + in_hbm(enc_coarse_x.reshape(flat), enc_coarse_h.reshape(flat)),
        [(2 * ROW_TILES, SUB, LANES)],
        [coarse_buf(6), coarse_buf(4), coarse_buf(6), coarse_buf(4), acc_buf, acc_buf, big, big,
         pltpu.SemaphoreType.DMA((2,))],
    )
    state_ci = inner_swap(state_c)
    near = jnp.where(section == 0, state_ci[:ROW_TILES], state_ci[ROW_TILES:])
    send = jnp.where(
        section == 0,
        jnp.concatenate([state_c, near], axis=0),
        jnp.concatenate([near, state_c], axis=0),
    )
    state_co = outer_swap(send)
    third = inner_swap(jnp.where(section == 0, state_co[2 * ROW_TILES :], state_co[:ROW_TILES]))

    (out,) = call(
        forecaster_body,
        "forecaster",
        place
        + on_chip(state_c, state_co, state_ci, third, state_f, got_o, got_i)
        + in_hbm(fc_coarse_h.reshape(flat))
        + on_chip(w_up, w_fc, w_head),
        [(HORIZON, 4, SUB, FB * PATCH)],
        [coarse_buf(8), coarse_buf(6), coarse_buf(5), fine_buf(8), fine_buf(6), fine_buf(4), acc_buf, big,
         pltpu.SemaphoreType.DMA],
    )
    return out.reshape(HORIZON, 4, COLS * PATCH)


def solution(mesh):
    line = ("groups", "tile", "section")
    return jax.shard_map(
        on_device,
        mesh=mesh,
        in_specs=(P(None, line, None), P(line, None), P(line, None)) + (P(),) * 11,
        out_specs=P(None, line, None),
        check_vma=False,
    )
```

```python
import jax
import jax.numpy as jnp
from jax import lax
from jax.experimental import pallas as pl
from jax.experimental.pallas import tpu as pltpu
from jax.sharding import PartitionSpec as P


C1 = 64
C2 = 192
PATCH = 16
FRAMES = 2
HORIZON = 2
COLS = 512
SUB = 16
FB = COLS // SUB
CB = COLS // 2 // SUB
LANES = 128
BF = jnp.bfloat16
F32 = jnp.float32
LINE = ("tile", "section")
PAIRS = CB // 2
ROW_TILES = 3 * PAIRS


def leaky(values):
    return jnp.where(values > 0, values, 0.2 * values)


def low_half(shape):
    return lax.broadcasted_iota(jnp.int32, shape, len(shape) - 1) < 64


def swap_halves(x):
    flat = x.reshape(-1, LANES)
    return pltpu.roll(flat, 64, 1).reshape(x.shape)


def swap_bf(x):
    return swap_halves(x.astype(F32)).astype(BF)


def sigmoid(x):
    return 0.5 * jnp.tanh(0.5 * x) + 0.5


def shift_sub(x, by):
    wide = x.astype(F32)
    row = lax.broadcasted_iota(jnp.int32, wide.shape, 0)
    if by > 0:
        moved = jnp.where(row == 0, 0.0, pltpu.roll(wide, 1, 0))
    else:
        moved = jnp.where(row == SUB - 1, 0.0, pltpu.roll(wide, SUB - 1, 0))
    return moved.astype(BF)


def seal(ref, idx, blocks):
    ref[idx, 0] = shift_sub(ref[idx, blocks], 1)
    ref[idx, blocks + 1] = shift_sub(ref[idx, 1], -1)


def fine_patches(ref, idx, lo, count):
    parts = [
        ref[idx + dr, pl.ds(lo + dj, count)].reshape(count * SUB, LANES)
        for dr in (-1, 0, 1)
        for dj in (0, 1, 2)
    ]
    return jnp.concatenate(parts, axis=-1)


def fine_gru(src, idx, weight, valid, emit):
    count = 16
    for lo in range(0, FB, count):
        acc = jnp.dot(fine_patches(src, idx, lo, count), weight[...], preferred_element_type=F32)
        gates = sigmoid(acc[:, :LANES])
        cand = acc[:, LANES:]
        cand = jnp.tanh(cand + swap_halves(gates * cand))
        old = src[idx, pl.ds(1 + lo, count)].reshape(count * SUB, LANES).astype(F32)
        new = (1.0 - gates) * cand + gates * old
        new = jnp.where(valid, new, 0.0).astype(BF)
        emit(lo, count, new.reshape(count, SUB, LANES))


def down_row(src, idx, weight):
    parts = []
    for dr in (-1, 0, 1):
        row = src[idx + dr].reshape(FB // 2 + 1, 2, SUB, LANES)
        for tap in (row[:CB, 0], row[:CB, 1], row[1:, 0]):
            parts.append(tap.reshape(CB * SUB, LANES))
    lhs = jnp.concatenate(parts, axis=-1)
    return jnp.dot(lhs, weight[...], preferred_element_type=F32)


def coarse_forms(t0, t1):
    lo = low_half(t0.shape)
    r0, r1 = swap_halves(t0), swap_halves(t1)
    return (
        t0.astype(BF),
        jnp.where(lo, t1, 0.0).astype(BF),
        jnp.where(lo, 0.0, r0).astype(BF),
        jnp.where(lo, r0, r1).astype(BF),
    )


def put_forms(ref, idx, forms):
    for k, tile in enumerate(forms):
        ref[idx, 1 : CB + 1, :, k * LANES : (k + 1) * LANES] = tile.reshape(CB, SUB, LANES)
    seal(ref, idx, CB)


def put_packed(ref, idx, tiles):
    t = [tiles(i).astype(F32) for i in range(3)]
    r = [swap_halves(x) for x in t]
    lo = low_half(t[0].shape)
    even = (t[0], jnp.where(lo, t[1], 0.0), jnp.where(lo, 0.0, r[0]), jnp.where(lo, r[0], r[1]))
    odd = (
        jnp.where(lo, r[1], r[2]),
        jnp.where(lo, r[2], 0.0),
        jnp.where(lo, 0.0, t[1]),
        t[2],
    )
    for k in range(4):
        both = jnp.stack([even[k].astype(BF), odd[k].astype(BF)], axis=1)
        ref[idx, 1 : CB + 1, :, k * LANES : (k + 1) * LANES] = both.reshape(CB, SUB, LANES)
    seal(ref, idx, CB)


def pack_forms(forms):
    f = [x.reshape(CB // 2, 2, SUB, LANES) for x in forms]
    lo = low_half((CB // 2, SUB, LANES))
    return (f[0][:, 0], jnp.where(lo, f[1][:, 0], f[2][:, 1]), f[3][:, 1])


def coarse_patches(ref, idx):
    def tile(dr, dj, k):
        return ref[idx + dr, dj : dj + CB, :, k * LANES : (k + 1) * LANES].reshape(CB * SUB, LANES)

    lo = low_half((CB * SUB, LANES))

    def aligned(dr):
        return [
            tile(dr, 0, 0),
            jnp.where(lo, tile(dr, 0, 1), tile(dr, 1, 2)),
            tile(dr, 1, 3),
            tile(dr, 2, 0),
        ]

    parts = aligned(-1)
    parts.append(jnp.where(lo, tile(-1, 2, 1), tile(0, 0, 2)))
    parts += [tile(0, 0, 3), tile(0, 1, 0), jnp.where(lo, tile(0, 1, 1), tile(0, 2, 2)), tile(0, 2, 3)]
    parts += aligned(1)
    parts.append(tile(1, 2, 1))
    return jnp.concatenate(parts, axis=-1)[:, : 9 * C2]


def coarse_gru(x_ref, x_idx, h_ref, h_idx, w_x, w_h, acc_x, acc_h, valid):
    width = 3 * C2
    if w_h is not None:
        acc_h[:, :width] = jnp.dot(coarse_patches(h_ref, h_idx), w_h[...], preferred_element_type=F32)
    if x_ref is not None:
        acc_x[:, :width] = jnp.dot(coarse_patches(x_ref, x_idx), w_x[...], preferred_element_type=F32)

    def part(ref, k):
        return ref[:, k * LANES : (k + 1) * LANES]

    gates = []
    for k in range(3):
        mixed = part(acc_h, k)
        if x_ref is not None:
            mixed = part(acc_x, k) + mixed
        gates.append(sigmoid(mixed))
    lo = low_half(gates[0].shape)
    g1, g2 = swap_halves(gates[1]), swap_halves(gates[2])
    update = (jnp.where(lo, g1, g2), g2)
    out = []
    for k in range(2):
        cand = gates[k] * part(acc_h, 3 + k)
        if x_ref is not None:
            cand = part(acc_x, 3 + k) + cand
        cand = jnp.tanh(cand)
        old = h_ref[h_idx, 1 : CB + 1, :, k * LANES : (k + 1) * LANES].reshape(CB * SUB, LANES).astype(F32)
        new = (1.0 - update[k]) * cand + update[k] * old
        out.append(jnp.where(valid, new, 0.0).astype(BF).astype(F32))
    return coarse_forms(out[0], out[1])


def in_grid(row, rows):
    return jnp.logical_and(row >= 0, row < rows)


def fine_encoder_body(
    where_ref, own, outer, inner, w_stem, w_gru, w_down,
    state_out, low_own, to_outer, to_inner, state_outer, state_inner, p1, p2, p3, stem2,
):
    upper = where_ref[0] == 0
    first = where_ref[1] * 4
    rows = where_ref[2] * 4
    lo = low_half((1, SUB, LANES))

    def pick(idx, lanes):
        if 3 <= idx < 7:
            return own[idx - 3, :, lanes]
        r = idx if idx < 3 else idx - 7
        a, b = outer[r, :, lanes], inner[r, :, lanes]
        return jnp.where(upper, a, b) if idx < 3 else jnp.where(upper, b, a)

    for frame in range(FRAMES):
        for t in range(4):
            at = FB * C1 + frame * FB * PATCH + t * LANES
            patches = jnp.concatenate([pick(idx, slice(at, at + LANES)) for idx in range(9)], axis=0)
            for half in range(2):
                acc = jnp.dot(patches, w_stem[:, half * 512 : half * 512 + 512], preferred_element_type=F32)
                acc = leaky(acc).astype(BF)
                for k in range(4):
                    block = acc[:, k * LANES : (k + 1) * LANES].reshape(9, SUB, LANES)
                    at = 8 * t + 4 * half + k
                    if frame == 0:
                        p1[:, 1 + at] = block
                    else:
                        stem2[:, at] = block
    for idx in range(9):
        for k in range(FB // 2):
            pair = pick(idx, slice(k * LANES, (k + 1) * LANES))
            p1[idx, 1 + 2 * k] = jnp.where(lo[0], p1[idx, 1 + 2 * k], swap_bf(pair))
            p1[idx, 2 + 2 * k] = jnp.where(lo[0], p1[idx, 2 + 2 * k], pair)
        seal(p1, idx, FB)

    @pl.loop(1, 8)
    def _(idx):
        def emit(lo_block, count, new):
            stems = stem2[idx, pl.ds(lo_block, count)]
            p2[idx, pl.ds(1 + lo_block, count)] = jnp.where(lo, stems, new)

        fine_gru(p1, idx, w_gru, in_grid(first + idx - 3, rows), emit)
        seal(p2, idx, FB)

    @pl.loop(2, 7)
    def _(idx):
        def emit(lo_block, count, new):
            p3[idx, pl.ds(1 + lo_block, count)] = jnp.where(lo, jnp.zeros_like(new), new)

        fine_gru(p2, idx, w_gru, in_grid(first + idx - 3, rows), emit)
        seal(p3, idx, FB)

    def lowered(src, p):
        acc = leaky(down_row(src, 3 + 2 * p, w_down)).astype(BF).astype(F32)
        return pack_forms(coarse_forms(acc[:, :LANES], acc[:, LANES:]))

    def put(ref, at, tiles):
        for k, tile in enumerate(tiles):
            base = at * ROW_TILES + k * PAIRS
            ref[base : base + PAIRS] = tile

    for p in range(2):
        tiles = lowered(p2, p)
        put(low_own, p, tiles)
        put(to_outer, p, tiles)
        put(to_inner, p, tiles)
    for p in range(2):
        tiles = lowered(p3, p)
        put(low_own, 2 + p, tiles)
        outward = upper if p == 0 else jnp.logical_not(upper)

        @pl.when(outward)
        def _():
            put(to_outer, 2, tiles)

        @pl.when(jnp.logical_not(outward))
        def _():
            put(to_inner, 2, tiles)

    for r in range(4):
        for k in range(FB // 2):
            state_out[r, k] = jnp.where(lo[0], swap_bf(p3[3 + r, 1 + 2 * k]), p3[3 + r, 2 + 2 * k])
    for top, ref in ((upper, state_outer), (jnp.logical_not(upper), state_inner)):
        start = jnp.where(top, 0, 2)
        for r in range(2):
            ref[r] = state_out[start + r]


def zero_tail(acc):
    acc[:, 4 * LANES :] = jnp.zeros((CB * SUB, LANES), F32)


def packed_tiles(ref, at):
    return lambda i: ref[at * ROW_TILES + i * PAIRS : at * ROW_TILES + (i + 1) * PAIRS]


def raw_tiles(get):
    def tiles(i):
        return jnp.stack([get(slice((3 * k + i) * LANES, (3 * k + i + 1) * LANES)) for k in range(PAIRS)])

    return tiles


def coarse_state_body(where_ref, own, outer, inner, w_h, acc_out, h_out, h0):
    upper = where_ref[0] == 0
    for idx in range(6):
        if 2 <= idx < 4:
            put_packed(h0, idx, raw_tiles(lambda lanes: own[idx - 2, :, lanes]))
            continue
        r = idx if idx < 2 else idx - 4
        a, b = (outer, inner) if idx < 2 else (inner, outer)
        put_packed(h0, idx, raw_tiles(lambda lanes: jnp.where(upper, a[r, :, lanes], b[r, :, lanes])))

    @pl.loop(0, 4)
    def _(idx):
        acc_out[idx, :, : 3 * C2] = jnp.dot(coarse_patches(h0, idx + 1), w_h[...], preferred_element_type=F32)
        acc_out[idx, :, 4 * LANES + C1 :] = jnp.zeros((CB * SUB, C1), F32)
        h_out[idx] = h0[idx + 1]


def coarse_encoder_body(
    where_ref, low_own, low_outer, low_inner, acc_first, h_first, w_x, w_h,
    state_out, x1, x2, h1, acc_x, acc_h,
):
    upper = where_ref[0] == 0
    first = where_ref[1] * 2
    rows = where_ref[2] * 2
    zero_tail(acc_x)
    zero_tail(acc_h)

    for idx in range(6):
        if 2 <= idx < 4:
            put_packed(x1, idx, packed_tiles(low_own, idx - 2))
            continue
        r = idx if idx < 2 else idx - 4
        a, b = (low_outer, low_inner) if idx < 2 else (low_inner, low_outer)
        put_packed(x1, idx, lambda i: jnp.where(upper, packed_tiles(a, r)(i), packed_tiles(b, r)(i)))
    put_packed(x2, 1, packed_tiles(low_own, 2))
    put_packed(x2, 2, packed_tiles(low_own, 3))
    put_packed(x2, 0, lambda i: jnp.where(upper, packed_tiles(low_outer, 2)(i), packed_tiles(low_inner, 2)(i)))
    put_packed(x2, 3, lambda i: jnp.where(upper, packed_tiles(low_inner, 2)(i), packed_tiles(low_outer, 2)(i)))

    @pl.loop(0, 4)
    def _(idx):
        forms = coarse_gru(
            x1, idx + 1, h_first, idx, w_x, None, acc_x, acc_first.at[idx], in_grid(first + idx - 1, rows)
        )
        put_forms(h1, idx, forms)

    @pl.loop(0, 2)
    def _(idx):
        forms = coarse_gru(x2, idx + 1, h1, idx + 1, w_x, w_h, acc_x, acc_h, in_grid(first + idx, rows))
        for k, tile in enumerate(pack_forms(forms)):
            state_out[pl.ds(idx * ROW_TILES + k * PAIRS, PAIRS)] = tile


def raise_pair(src, idx, weight):
    def tile(dr, dj, k):
        return src[idx + dr, 1 + dj : 1 + dj + CB, :, k * LANES : (k + 1) * LANES].reshape(CB * SUB, LANES)

    lo = low_half((CB * SUB, LANES))
    parts = []
    for dr in (0, 1):
        parts += [tile(dr, 0, 0), jnp.where(lo, tile(dr, 0, 1), tile(dr, 1, 2)), tile(dr, 1, 3)]
    return jnp.dot(jnp.concatenate(parts, axis=-1), weight[...], preferred_element_type=F32)


def forecaster_body(
    where_ref, c_own, c_outer, c_inner, c_third, f_own, f_outer, f_inner, w_h, w_up, w_gru, w_head,
    out, h2, s1, s2, pf1, pf2, states, acc_h,
):
    upper = where_ref[0] == 0
    first_c = where_ref[1] * 2
    rows_c = where_ref[2] * 2
    first_f = where_ref[1] * 4
    rows_f = where_ref[2] * 4
    lo = low_half((1, SUB, LANES))
    zero_tail(acc_h)

    put_packed(h2, 3, packed_tiles(c_own, 0))
    put_packed(h2, 4, packed_tiles(c_own, 1))

    def either(a, b):
        return lambda i: jnp.where(upper, a(i), b(i))

    put_packed(h2, 0, either(packed_tiles(c_outer, 0), packed_tiles(c_third, 0)))
    put_packed(h2, 1, either(packed_tiles(c_outer, 1), packed_tiles(c_inner, 0)))
    put_packed(h2, 2, either(packed_tiles(c_outer, 2), packed_tiles(c_inner, 1)))
    put_packed(h2, 5, either(packed_tiles(c_inner, 0), packed_tiles(c_outer, 0)))
    put_packed(h2, 6, either(packed_tiles(c_inner, 1), packed_tiles(c_outer, 1)))
    put_packed(h2, 7, either(packed_tiles(c_third, 0), packed_tiles(c_outer, 2)))

    for idx in range(8):
        for k in range(FB // 2):
            if 2 <= idx < 6:
                pair = f_own[idx - 2, k]
            elif idx < 2:
                pair = jnp.where(upper, f_outer[idx, k], f_inner[idx, k])
            else:
                pair = jnp.where(upper, f_inner[idx - 6, k], f_outer[idx - 6, k])
            pf1[idx, 1 + 2 * k] = swap_bf(pair)
            pf1[idx, 2 + 2 * k] = pair

    @pl.loop(0, 6)
    def _(idx):
        forms = coarse_gru(None, 0, h2, idx + 1, None, w_h, None, acc_h, in_grid(first_c + idx - 2, rows_c))
        put_forms(s1, idx, forms)

    @pl.loop(0, 4)
    def _(idx):
        forms = coarse_gru(None, 0, s1, idx + 1, None, w_h, None, acc_h, in_grid(first_c + idx - 1, rows_c))
        put_forms(s2, idx, forms)

    s2[4] = jnp.zeros(s2.shape[1:], BF)

    def raise_rows(src, idx, fine, at, coarse_row):
        acc = raise_pair(src, idx, w_up)
        acc = jnp.where(in_grid(coarse_row, rows_c), leaky(acc), 0.0)
        for half, row in enumerate(at):
            if row is None:
                continue
            tile = acc[:, half * LANES : (half + 1) * LANES]
            even = tile.astype(BF).reshape(CB, SUB, LANES)
            odd = swap_halves(tile).astype(BF).reshape(CB, SUB, LANES)
            both = jnp.stack([even, odd], axis=1).reshape(FB, SUB, LANES)
            fine[row, 1 : FB + 1] = jnp.where(lo, both, fine[row, 1 : FB + 1])

    @pl.loop(0, 4)
    def _(k):
        raise_rows(s1, k + 1, pf1, (2 * k, 2 * k + 1), first_c + k - 1)
        seal(pf1, 2 * k, FB)
        seal(pf1, 2 * k + 1, FB)

    @pl.loop(0, 6)
    def _(idx):
        def emit(lo_block, count, new):
            pf2[idx, pl.ds(1 + lo_block, count)] = new

        fine_gru(pf1, idx + 1, w_gru, in_grid(first_f + idx - 1, rows_f), emit)

    def head(step, ref, base):
        for t in range(4):
            lhs = jnp.concatenate(
                [ref[base : base + 4, 1 + 8 * t + k].reshape(4 * SUB, LANES) for k in range(8)], axis=-1
            )
            acc = jnp.dot(lhs, w_head[...], preferred_element_type=F32).astype(BF)
            out[step, :, :, t * LANES : (t + 1) * LANES] = acc.reshape(4, SUB, LANES)

    head(0, pf2, 1)

    raise_rows(s2, 0, pf2, (None, 0), first_c - 1)
    raise_rows(s2, 1, pf2, (1, 2), first_c)
    raise_rows(s2, 2, pf2, (3, 4), first_c + 1)
    raise_rows(s2, 3, pf2, (5, None), first_c + 2)
    for idx in range(6):
        seal(pf2, idx, FB)

    @pl.loop(0, 4)
    def _(idx):
        def emit(lo_block, count, new):
            states[idx, pl.ds(1 + lo_block, count)] = new

        fine_gru(pf2, idx + 1, w_gru, True, emit)

    head(1, states, 0)


def to_upper(x):
    return jnp.concatenate([jnp.zeros(x.shape, F32), x.astype(F32)], axis=-1).astype(BF)


def to_lower(x):
    return jnp.concatenate([x.astype(F32), jnp.zeros(x.shape, F32)], axis=-1).astype(BF)


def prepare_body(
    stem, enc_x, enc_h, down, up, fc_x, fc_h, head, w_stem, w_enc, w_down, w_up, w_fc, w_head
):
    for kx, kh, w in ((enc_x, enc_h, w_enc), (fc_x, fc_h, w_fc)):
        for k in range(9):
            at = k * LANES
            w[at : at + C1, :LANES] = kx[k, :, :LANES]
            w[at : at + C1, LANES:] = to_upper(kx[k, :, LANES:])
            w[at + C1 : at + LANES, :LANES] = kh[k, :, :LANES]
            w[at + C1 : at + LANES, LANES:] = to_lower(kh[k, :, LANES:])
    for k in range(9):
        at = k * LANES
        w_down[at : at + C1] = jnp.zeros((C1, 2 * LANES), BF)
        w_down[at + C1 : at + LANES, :LANES] = down[k, :, :LANES]
        w_down[at + C1 : at + LANES, LANES:] = to_lower(down[k, :, LANES:])

    def tap(a, b):
        return jnp.zeros((C2, C1), F32) if a is None else up[3 * a + b].astype(F32)

    none = (None, None)
    for g, taps in enumerate((
        ((1, 1), (1, 0), (0, 1), (0, 0)),
        (none, (1, 2), none, (0, 2)),
        (none, none, (2, 1), (2, 0)),
        (none, none, none, (2, 2)),
    )):
        for n in range(2):
            pair = jnp.concatenate([tap(*taps[2 * n]), tap(*taps[2 * n + 1])], axis=-1)
            w_up[g * C2 : (g + 1) * C2, n * LANES : (n + 1) * LANES] = pair.astype(BF)

    w_stem[...] = jnp.zeros(w_stem.shape, BF)
    w_head[...] = jnp.zeros(w_head.shape, BF)
    wide = to_lower(stem[...])
    for k in range(8):
        w_stem[k * PATCH : (k + 1) * PATCH, k * LANES : (k + 1) * LANES] = wide
        w_head[k * LANES + C1 : (k + 1) * LANES, k * PATCH : (k + 1) * PATCH] = head[...]


def call(body, args, outs, scratch):
    return pl.pallas_call(
        body,
        out_shape=[s if isinstance(s, jax.ShapeDtypeStruct) else jax.ShapeDtypeStruct(s, BF) for s in outs],
        in_specs=[pl.BlockSpec(memory_space=space) for _, space in args],
        out_specs=[pl.BlockSpec(memory_space=pltpu.VMEM)] * len(outs),
        scratch_shapes=scratch,
        compiler_params=pltpu.CompilerParams(vmem_limit_bytes=24 * 1024 * 1024),
    )(*[arg for arg, _ in args])


def on_device(
    frames,
    start_fine,
    start_coarse,
    enc_stem,
    enc_fine_x,
    enc_fine_h,
    enc_down,
    enc_coarse_x,
    enc_coarse_h,
    fc_coarse_h,
    fc_up,
    fc_fine_x,
    fc_fine_h,
    fc_head,
):
    count = lax.axis_size(LINE)
    section = lax.axis_index("section")
    position = lax.axis_index(LINE)
    where = jnp.stack([section, position, jnp.int32(count)]).astype(jnp.int32)
    across = [(i, i + 1) for i in range(1, count - 1, 2)]
    across = across + [(b, a) for a, b in across]

    def outer_swap(x):
        return lax.ppermute(x, LINE, across)

    def inner_swap(x):
        return lax.ppermute(x, "section", [(0, 1), (1, 0)])

    fine = start_fine.reshape(4, SUB, FB * C1)
    patches = frames.reshape(FRAMES, 4, SUB, FB * PATCH)
    coarse = start_coarse.reshape(2, SUB, CB * C2)
    own = jnp.concatenate([fine, patches[0], patches[1]], axis=-1)
    outer = outer_swap(lax.dynamic_slice_in_dim(own, section, 3, 0))
    inner = inner_swap(lax.dynamic_slice_in_dim(own, 1 - section, 3, 0))

    def on_chip(*values):
        return [(value, pltpu.VMEM) for value in values]

    def fine_buf(rows):
        return pltpu.VMEM((rows, FB + 2, SUB, LANES), BF)

    def coarse_buf(rows):
        return pltpu.VMEM((rows, CB + 2, SUB, 4 * LANES), BF)

    place = [(where, pltpu.SMEM)]
    acc_buf = pltpu.VMEM((CB * SUB, 5 * LANES), F32)
    flat = (9 * C2, 3 * C2)

    w_stem, w_enc, w_down, w_up, w_fc, w_head = call(
        prepare_body,
        on_chip(
            enc_stem,
            enc_fine_x.reshape(9, C1, 3 * C1),
            enc_fine_h.reshape(9, C1, 3 * C1),
            enc_down.reshape(9, C1, C2),
            fc_up.reshape(9, C2, C1),
            fc_fine_x.reshape(9, C1, 3 * C1),
            fc_fine_h.reshape(9, C1, 3 * C1),
            fc_head,
        ),
        [
            (8 * PATCH, 8 * LANES),
            (9 * LANES, 2 * LANES),
            (9 * LANES, 2 * LANES),
            (4 * C2, 2 * LANES),
            (9 * LANES, 2 * LANES),
            (8 * LANES, 8 * PATCH),
        ],
        [],
    )
    coarse_o, coarse_i = outer_swap(coarse), inner_swap(coarse)

    halo = (3 * ROW_TILES, SUB, LANES)
    edge = (2, FB // 2, SUB, LANES)
    state_f, low_own, to_outer, to_inner, state_fo, state_fi = call(
        fine_encoder_body,
        place + on_chip(own, outer, inner, w_stem, w_enc, w_down),
        [(4, FB // 2, SUB, LANES), (4 * ROW_TILES, SUB, LANES), halo, halo, edge, edge],
        [fine_buf(9), fine_buf(9), fine_buf(9), pltpu.VMEM((9, FB, SUB, LANES), BF)],
    )
    got_o, got_i = outer_swap(to_outer), inner_swap(to_inner)

    acc_first, h_first = call(
        coarse_state_body,
        place + on_chip(coarse, coarse_o, coarse_i, enc_coarse_h.reshape(flat)),
        [jax.ShapeDtypeStruct((4, CB * SUB, 5 * LANES), F32), (4, CB + 2, SUB, 4 * LANES)],
        [coarse_buf(6)],
    )
    state_fo, state_fi = outer_swap(state_fo), inner_swap(state_fi)

    (state_c,) = call(
        coarse_encoder_body,
        place
        + on_chip(low_own, got_o, got_i, acc_first, h_first, enc_coarse_x.reshape(flat), enc_coarse_h.reshape(flat)),
        [(2 * ROW_TILES, SUB, LANES)],
        [coarse_buf(6), coarse_buf(4), coarse_buf(4), acc_buf, acc_buf],
    )
    state_ci = inner_swap(state_c)
    near = jnp.where(section == 0, state_ci[:ROW_TILES], state_ci[ROW_TILES:])
    send = jnp.where(
        section == 0,
        jnp.concatenate([state_c, near], axis=0),
        jnp.concatenate([near, state_c], axis=0),
    )
    state_co = outer_swap(send)
    third = inner_swap(jnp.where(section == 0, state_co[2 * ROW_TILES :], state_co[:ROW_TILES]))

    (out,) = call(
        forecaster_body,
        place
        + on_chip(state_c, state_co, state_ci, third, state_f, state_fo, state_fi, fc_coarse_h.reshape(flat))
        + on_chip(w_up, w_fc, w_head),
        [(HORIZON, 4, SUB, FB * PATCH)],
        [coarse_buf(8), coarse_buf(6), coarse_buf(5), fine_buf(8), fine_buf(6), fine_buf(4), acc_buf],
    )
    return out.reshape(HORIZON, 4, COLS * PATCH)


def solution(mesh):
    line = ("groups", "tile", "section")
    return jax.shard_map(
        on_device,
        mesh=mesh,
        in_specs=(P(None, line, None), P(line, None), P(line, None)) + (P(),) * 11,
        out_specs=P(None, line, None),
        check_vma=False,
    )
```

```python
import jax
import jax.numpy as jnp
from jax import lax
from jax.experimental import pallas as pl
from jax.experimental.pallas import tpu as pltpu
from jax.sharding import PartitionSpec as P


C1 = 64
C2 = 192
PATCH = 16
FRAMES = 2
HORIZON = 2
COLS = 512
SUB = 16
FB = COLS // SUB
CB = COLS // 2 // SUB
LANES = 128
BF = jnp.bfloat16
F32 = jnp.float32
LINE = ("tile", "section")
PAIRS = CB // 2
ROW_TILES = 3 * PAIRS


def leaky(values):
    return jnp.where(values > 0, values, 0.2 * values)


def low_half(shape):
    return lax.broadcasted_iota(jnp.int32, shape, len(shape) - 1) < 64


def swap_halves(x):
    flat = x.reshape(-1, LANES)
    return pltpu.roll(flat, 64, 1).reshape(x.shape)


def swap_bf(x):
    return swap_halves(x.astype(F32)).astype(BF)


def sigmoid(x):
    return 0.5 * jnp.tanh(0.5 * x) + 0.5


def shift_sub(x, by):
    wide = x.astype(F32)
    row = lax.broadcasted_iota(jnp.int32, wide.shape, 0)
    if by > 0:
        moved = jnp.where(row == 0, 0.0, pltpu.roll(wide, 1, 0))
    else:
        moved = jnp.where(row == SUB - 1, 0.0, pltpu.roll(wide, SUB - 1, 0))
    return moved.astype(BF)


def seal(ref, idx, blocks):
    ref[idx, 0] = shift_sub(ref[idx, blocks], 1)
    ref[idx, blocks + 1] = shift_sub(ref[idx, 1], -1)


def fine_patches(ref, idx, lo, count):
    parts = [
        ref[idx + dr, pl.ds(lo + dj, count)].reshape(count * SUB, LANES)
        for dr in (-1, 0, 1)
        for dj in (0, 1, 2)
    ]
    return jnp.concatenate(parts, axis=-1)


def fine_gru(src, idx, weight, valid, emit):
    count = 16
    for lo in range(0, FB, count):
        acc = jnp.dot(fine_patches(src, idx, lo, count), weight[...], preferred_element_type=F32)
        gates = sigmoid(acc[:, :LANES])
        cand = acc[:, LANES:]
        cand = jnp.tanh(cand + swap_halves(gates * cand))
        old = src[idx, pl.ds(1 + lo, count)].reshape(count * SUB, LANES).astype(F32)
        new = (1.0 - gates) * cand + gates * old
        new = jnp.where(valid, new, 0.0).astype(BF)
        emit(lo, count, new.reshape(count, SUB, LANES))


def down_row(src, idx, weight):
    parts = []
    for dr in (-1, 0, 1):
        row = src[idx + dr].reshape(FB // 2 + 1, 2, SUB, LANES)
        for tap in (row[:CB, 0], row[:CB, 1], row[1:, 0]):
            parts.append(tap.reshape(CB * SUB, LANES))
    lhs = jnp.concatenate(parts, axis=-1)
    return jnp.dot(lhs, weight[...], preferred_element_type=F32)


def coarse_forms(t0, t1):
    lo = low_half(t0.shape)
    r0, r1 = swap_halves(t0), swap_halves(t1)
    return (
        t0.astype(BF),
        jnp.where(lo, t1, 0.0).astype(BF),
        jnp.where(lo, 0.0, r0).astype(BF),
        jnp.where(lo, r0, r1).astype(BF),
    )


def put_forms(ref, idx, forms):
    for k, tile in enumerate(forms):
        ref[idx, 1 : CB + 1, :, k * LANES : (k + 1) * LANES] = tile.reshape(CB, SUB, LANES)
    seal(ref, idx, CB)


def put_packed(ref, idx, tiles):
    t = [tiles(i).astype(F32) for i in range(3)]
    r = [swap_halves(x) for x in t]
    lo = low_half(t[0].shape)
    even = (t[0], jnp.where(lo, t[1], 0.0), jnp.where(lo, 0.0, r[0]), jnp.where(lo, r[0], r[1]))
    odd = (
        jnp.where(lo, r[1], r[2]),
        jnp.where(lo, r[2], 0.0),
        jnp.where(lo, 0.0, t[1]),
        t[2],
    )
    for k in range(4):
        both = jnp.stack([even[k].astype(BF), odd[k].astype(BF)], axis=1)
        ref[idx, 1 : CB + 1, :, k * LANES : (k + 1) * LANES] = both.reshape(CB, SUB, LANES)
    seal(ref, idx, CB)


def pack_forms(forms):
    f = [x.reshape(CB // 2, 2, SUB, LANES) for x in forms]
    lo = low_half((CB // 2, SUB, LANES))
    return (f[0][:, 0], jnp.where(lo, f[1][:, 0], f[2][:, 1]), f[3][:, 1])


def coarse_patches(ref, idx):
    def tile(dr, dj, k):
        return ref[idx + dr, dj : dj + CB, :, k * LANES : (k + 1) * LANES].reshape(CB * SUB, LANES)

    lo = low_half((CB * SUB, LANES))

    def aligned(dr):
        return [
            tile(dr, 0, 0),
            jnp.where(lo, tile(dr, 0, 1), tile(dr, 1, 2)),
            tile(dr, 1, 3),
            tile(dr, 2, 0),
        ]

    parts = aligned(-1)
    parts.append(jnp.where(lo, tile(-1, 2, 1), tile(0, 0, 2)))
    parts += [tile(0, 0, 3), tile(0, 1, 0), jnp.where(lo, tile(0, 1, 1), tile(0, 2, 2)), tile(0, 2, 3)]
    parts += aligned(1)
    parts.append(tile(1, 2, 1))
    return jnp.concatenate(parts, axis=-1)[:, : 9 * C2]


def coarse_gru(x_ref, x_idx, h_ref, h_idx, w_x, w_h, acc_x, acc_h, valid):
    width = 3 * C2
    if w_h is not None:
        acc_h[:, :width] = jnp.dot(coarse_patches(h_ref, h_idx), w_h[...], preferred_element_type=F32)
    if x_ref is not None:
        acc_x[:, :width] = jnp.dot(coarse_patches(x_ref, x_idx), w_x[...], preferred_element_type=F32)

    def part(ref, k):
        return ref[:, k * LANES : (k + 1) * LANES]

    gates = []
    for k in range(3):
        mixed = part(acc_h, k)
        if x_ref is not None:
            mixed = part(acc_x, k) + mixed
        gates.append(sigmoid(mixed))
    lo = low_half(gates[0].shape)
    g1, g2 = swap_halves(gates[1]), swap_halves(gates[2])
    update = (jnp.where(lo, g1, g2), g2)
    out = []
    for k in range(2):
        cand = gates[k] * part(acc_h, 3 + k)
        if x_ref is not None:
            cand = part(acc_x, 3 + k) + cand
        cand = jnp.tanh(cand)
        old = h_ref[h_idx, 1 : CB + 1, :, k * LANES : (k + 1) * LANES].reshape(CB * SUB, LANES).astype(F32)
        new = (1.0 - update[k]) * cand + update[k] * old
        out.append(jnp.where(valid, new, 0.0).astype(BF).astype(F32))
    return coarse_forms(out[0], out[1])


def place(per_device):
    upper = lax.axis_index("section") == 0
    line = lax.axis_index("tile") * lax.axis_size("section") + lax.axis_index("section")
    return upper, line * per_device, lax.axis_size(LINE) * per_device


def in_grid(row, rows):
    return jnp.logical_and(row >= 0, row < rows)


def pack_body(fine, first, second, own, to_outer, to_inner):
    upper, _, _ = place(4)
    for r in range(4):
        own[r, :, : FB * C1] = fine[r]
        own[r, :, FB * C1 : FB * (C1 + PATCH)] = first[r]
        own[r, :, FB * (C1 + PATCH) :] = second[r]
    for r in range(3):
        to_outer[r] = jnp.where(upper, own[r], own[r + 1])
        to_inner[r] = jnp.where(upper, own[r + 1], own[r])


def fine_encoder_body(
    own, outer, inner, w_stem, w_gru, w_down,
    state_out, low_own, to_outer, to_inner, state_outer, state_inner, p1, p2, p3, stem2,
):
    upper, first, rows = place(4)
    lo = low_half((1, SUB, LANES))

    def pick(idx, lanes):
        if 3 <= idx < 7:
            return own[idx - 3, :, lanes]
        r = idx if idx < 3 else idx - 7
        a, b = outer[r, :, lanes], inner[r, :, lanes]
        return jnp.where(upper, a, b) if idx < 3 else jnp.where(upper, b, a)

    for frame in range(FRAMES):
        for t in range(4):
            at = FB * C1 + frame * FB * PATCH + t * LANES
            patches = jnp.concatenate([pick(idx, slice(at, at + LANES)) for idx in range(9)], axis=0)
            for half in range(2):
                acc = jnp.dot(patches, w_stem[:, half * 512 : half * 512 + 512], preferred_element_type=F32)
                acc = leaky(acc).astype(BF)
                for k in range(4):
                    block = acc[:, k * LANES : (k + 1) * LANES].reshape(9, SUB, LANES)
                    at = 8 * t + 4 * half + k
                    if frame == 0:
                        p1[:, 1 + at] = block
                    else:
                        stem2[:, at] = block
    for idx in range(9):
        for k in range(FB // 2):
            pair = pick(idx, slice(k * LANES, (k + 1) * LANES))
            p1[idx, 1 + 2 * k] = jnp.where(lo[0], p1[idx, 1 + 2 * k], swap_bf(pair))
            p1[idx, 2 + 2 * k] = jnp.where(lo[0], p1[idx, 2 + 2 * k], pair)
        seal(p1, idx, FB)

    @pl.loop(1, 8)
    def _(idx):
        def emit(lo_block, count, new):
            stems = stem2[idx, pl.ds(lo_block, count)]
            p2[idx, pl.ds(1 + lo_block, count)] = jnp.where(lo, stems, new)

        fine_gru(p1, idx, w_gru, in_grid(first + idx - 3, rows), emit)
        seal(p2, idx, FB)

    @pl.loop(2, 7)
    def _(idx):
        def emit(lo_block, count, new):
            p3[idx, pl.ds(1 + lo_block, count)] = jnp.where(lo, jnp.zeros_like(new), new)

        fine_gru(p2, idx, w_gru, in_grid(first + idx - 3, rows), emit)
        seal(p3, idx, FB)

    def lowered(src, p):
        acc = leaky(down_row(src, 3 + 2 * p, w_down)).astype(BF).astype(F32)
        return pack_forms(coarse_forms(acc[:, :LANES], acc[:, LANES:]))

    def put(ref, at, tiles):
        for k, tile in enumerate(tiles):
            base = at * ROW_TILES + k * PAIRS
            ref[base : base + PAIRS] = tile

    for p in range(2):
        tiles = lowered(p2, p)
        put(low_own, p, tiles)
        put(to_outer, p, tiles)
        put(to_inner, p, tiles)
    for p in range(2):
        tiles = lowered(p3, p)
        put(low_own, 2 + p, tiles)
        outward = upper if p == 0 else jnp.logical_not(upper)

        @pl.when(outward)
        def _():
            put(to_outer, 2, tiles)

        @pl.when(jnp.logical_not(outward))
        def _():
            put(to_inner, 2, tiles)

    for r in range(4):
        for k in range(FB // 2):
            state_out[r, k] = jnp.where(lo[0], swap_bf(p3[3 + r, 1 + 2 * k]), p3[3 + r, 2 + 2 * k])
    for top, ref in ((upper, state_outer), (jnp.logical_not(upper), state_inner)):
        start = jnp.where(top, 0, 2)
        for r in range(2):
            ref[r] = state_out[start + r]


def zero_tail(acc):
    acc[:, 4 * LANES :] = jnp.zeros((CB * SUB, LANES), F32)


def packed_tiles(ref, at):
    return lambda i: ref[at * ROW_TILES + i * PAIRS : at * ROW_TILES + (i + 1) * PAIRS]


def raw_tiles(get):
    def tiles(i):
        return jnp.stack([get(slice((3 * k + i) * LANES, (3 * k + i + 1) * LANES)) for k in range(PAIRS)])

    return tiles


def coarse_state_body(own, outer, inner, w_h, acc_out, h_out, h0):
    upper, _, _ = place(2)
    for idx in range(6):
        if 2 <= idx < 4:
            put_packed(h0, idx, raw_tiles(lambda lanes: own[idx - 2, :, lanes]))
            continue
        r = idx if idx < 2 else idx - 4
        a, b = (outer, inner) if idx < 2 else (inner, outer)
        put_packed(h0, idx, raw_tiles(lambda lanes: jnp.where(upper, a[r, :, lanes], b[r, :, lanes])))

    @pl.loop(0, 4)
    def _(idx):
        acc_out[idx, :, : 3 * C2] = jnp.dot(coarse_patches(h0, idx + 1), w_h[...], preferred_element_type=F32)
        acc_out[idx, :, 4 * LANES + C1 :] = jnp.zeros((CB * SUB, C1), F32)
        h_out[idx] = h0[idx + 1]


def coarse_encoder_body(
    low_own, low_outer, low_inner, acc_first, h_first, w_x, w_h,
    state_out, x1, x2, h1, acc_x, acc_h,
):
    upper, first, rows = place(2)
    zero_tail(acc_x)
    zero_tail(acc_h)

    for idx in range(6):
        if 2 <= idx < 4:
            put_packed(x1, idx, packed_tiles(low_own, idx - 2))
            continue
        r = idx if idx < 2 else idx - 4
        a, b = (low_outer, low_inner) if idx < 2 else (low_inner, low_outer)
        put_packed(x1, idx, lambda i: jnp.where(upper, packed_tiles(a, r)(i), packed_tiles(b, r)(i)))
    put_packed(x2, 1, packed_tiles(low_own, 2))
    put_packed(x2, 2, packed_tiles(low_own, 3))
    put_packed(x2, 0, lambda i: jnp.where(upper, packed_tiles(low_outer, 2)(i), packed_tiles(low_inner, 2)(i)))
    put_packed(x2, 3, lambda i: jnp.where(upper, packed_tiles(low_inner, 2)(i), packed_tiles(low_outer, 2)(i)))

    @pl.loop(0, 4)
    def _(idx):
        forms = coarse_gru(
            x1, idx + 1, h_first, idx, w_x, None, acc_x, acc_first.at[idx], in_grid(first + idx - 1, rows)
        )
        put_forms(h1, idx, forms)

    @pl.loop(0, 2)
    def _(idx):
        forms = coarse_gru(x2, idx + 1, h1, idx + 1, w_x, w_h, acc_x, acc_h, in_grid(first + idx, rows))
        slot = jnp.where(upper, idx, 1 - idx)
        for k, tile in enumerate(pack_forms(forms)):
            state_out[pl.ds(slot * ROW_TILES + k * PAIRS, PAIRS)] = tile


def raise_pair(src, idx, weight):
    def tile(dr, dj, k):
        return src[idx + dr, 1 + dj : 1 + dj + CB, :, k * LANES : (k + 1) * LANES].reshape(CB * SUB, LANES)

    lo = low_half((CB * SUB, LANES))
    parts = []
    for dr in (0, 1):
        parts += [tile(dr, 0, 0), jnp.where(lo, tile(dr, 0, 1), tile(dr, 1, 2)), tile(dr, 1, 3)]
    return jnp.dot(jnp.concatenate(parts, axis=-1), weight[...], preferred_element_type=F32)


def forecaster_body(
    c_own, c_outer, c_inner, c_third, f_own, f_outer, f_inner, w_h, w_up, w_gru, w_head,
    out, h2, s1, s2, pf1, pf2, states, acc_h,
):
    upper, first_c, rows_c = place(2)
    _, first_f, rows_f = place(4)
    lo = low_half((1, SUB, LANES))
    zero_tail(acc_h)

    def either(a, i, b, j):
        return lambda t: jnp.where(upper, packed_tiles(a, i)(t), packed_tiles(b, j)(t))

    put_packed(h2, 0, either(c_outer, 2, c_third, 0))
    put_packed(h2, 1, either(c_outer, 1, c_inner, 0))
    put_packed(h2, 2, either(c_outer, 0, c_inner, 1))
    put_packed(h2, 3, either(c_own, 0, c_own, 1))
    put_packed(h2, 4, either(c_own, 1, c_own, 0))
    put_packed(h2, 5, either(c_inner, 1, c_outer, 0))
    put_packed(h2, 6, either(c_inner, 0, c_outer, 1))
    put_packed(h2, 7, either(c_third, 0, c_outer, 2))

    for idx in range(8):
        for k in range(FB // 2):
            if 2 <= idx < 6:
                pair = f_own[idx - 2, k]
            elif idx < 2:
                pair = jnp.where(upper, f_outer[idx, k], f_inner[idx, k])
            else:
                pair = jnp.where(upper, f_inner[idx - 6, k], f_outer[idx - 6, k])
            pf1[idx, 1 + 2 * k] = swap_bf(pair)
            pf1[idx, 2 + 2 * k] = pair

    @pl.loop(0, 6)
    def _(idx):
        forms = coarse_gru(None, 0, h2, idx + 1, None, w_h, None, acc_h, in_grid(first_c + idx - 2, rows_c))
        put_forms(s1, idx, forms)

    @pl.loop(0, 4)
    def _(idx):
        forms = coarse_gru(None, 0, s1, idx + 1, None, w_h, None, acc_h, in_grid(first_c + idx - 1, rows_c))
        put_forms(s2, idx, forms)

    s2[4] = jnp.zeros(s2.shape[1:], BF)

    def raise_rows(src, idx, fine, at, coarse_row):
        acc = raise_pair(src, idx, w_up)
        acc = jnp.where(in_grid(coarse_row, rows_c), leaky(acc), 0.0)
        for half, row in enumerate(at):
            if row is None:
                continue
            tile = acc[:, half * LANES : (half + 1) * LANES]
            even = tile.astype(BF).reshape(CB, SUB, LANES)
            odd = swap_halves(tile).astype(BF).reshape(CB, SUB, LANES)
            both = jnp.stack([even, odd], axis=1).reshape(FB, SUB, LANES)
            fine[row, 1 : FB + 1] = jnp.where(lo, both, fine[row, 1 : FB + 1])

    @pl.loop(0, 4)
    def _(k):
        raise_rows(s1, k + 1, pf1, (2 * k, 2 * k + 1), first_c + k - 1)
        seal(pf1, 2 * k, FB)
        seal(pf1, 2 * k + 1, FB)

    @pl.loop(0, 6)
    def _(idx):
        def emit(lo_block, count, new):
            pf2[idx, pl.ds(1 + lo_block, count)] = new

        fine_gru(pf1, idx + 1, w_gru, in_grid(first_f + idx - 1, rows_f), emit)

    def head(step, ref, base):
        for t in range(4):
            lhs = jnp.concatenate(
                [ref[base : base + 4, 1 + 8 * t + k].reshape(4 * SUB, LANES) for k in range(8)], axis=-1
            )
            acc = jnp.dot(lhs, w_head[...], preferred_element_type=F32).astype(BF)
            out[step, :, :, t * LANES : (t + 1) * LANES] = acc.reshape(4, SUB, LANES)

    head(0, pf2, 1)

    raise_rows(s2, 0, pf2, (None, 0), first_c - 1)
    raise_rows(s2, 1, pf2, (1, 2), first_c)
    raise_rows(s2, 2, pf2, (3, 4), first_c + 1)
    raise_rows(s2, 3, pf2, (5, None), first_c + 2)
    for idx in range(6):
        seal(pf2, idx, FB)

    @pl.loop(0, 4)
    def _(idx):
        def emit(lo_block, count, new):
            states[idx, pl.ds(1 + lo_block, count)] = new

        fine_gru(pf2, idx + 1, w_gru, True, emit)

    head(1, states, 0)


def to_upper(x):
    return jnp.concatenate([jnp.zeros(x.shape, F32), x.astype(F32)], axis=-1).astype(BF)


def to_lower(x):
    return jnp.concatenate([x.astype(F32), jnp.zeros(x.shape, F32)], axis=-1).astype(BF)


def fetch_all(given, copies, sems):
    fetches = [pltpu.make_async_copy(src, dst, sems.at[i]) for i, (src, dst) in enumerate(zip(given, copies))]
    for fetch in fetches:
        fetch.start()
    for fetch in fetches:
        fetch.wait()


def arrange_gru(kx, kh, w):
    for k in range(9):
        at = k * LANES
        w[at : at + C1, :LANES] = kx[k, :, :LANES]
        w[at : at + C1, LANES:] = to_upper(kx[k, :, LANES:])
        w[at + C1 : at + LANES, :LANES] = kh[k, :, :LANES]
        w[at + C1 : at + LANES, LANES:] = to_lower(kh[k, :, LANES:])


def prepare_encoder_body(*refs):
    given, (w_stem, w_enc, w_down), copies, sems = refs[:4], refs[4:7], refs[7:11], refs[11]
    fetch_all(given, copies, sems)
    stem, enc_x, enc_h, down = copies
    arrange_gru(enc_x, enc_h, w_enc)
    for k in range(9):
        at = k * LANES
        w_down[at : at + C1] = jnp.zeros((C1, 2 * LANES), BF)
        w_down[at + C1 : at + LANES, :LANES] = down[k, :, :LANES]
        w_down[at + C1 : at + LANES, LANES:] = to_lower(down[k, :, LANES:])
    w_stem[...] = jnp.zeros(w_stem.shape, BF)
    wide = to_lower(stem[...])
    for k in range(8):
        w_stem[k * PATCH : (k + 1) * PATCH, k * LANES : (k + 1) * LANES] = wide


def prepare_forecaster_body(*refs):
    given, (w_up, w_fc, w_head), copies, sems = refs[:4], refs[4:7], refs[7:11], refs[11]
    fetch_all(given, copies, sems)
    up, fc_x, fc_h, head = copies
    arrange_gru(fc_x, fc_h, w_fc)

    def tap(a, b):
        return jnp.zeros((C2, C1), F32) if a is None else up[3 * a + b].astype(F32).T

    none = (None, None)
    for g, taps in enumerate((
        ((1, 1), (1, 0), (0, 1), (0, 0)),
        (none, (1, 2), none, (0, 2)),
        (none, none, (2, 1), (2, 0)),
        (none, none, none, (2, 2)),
    )):
        for n in range(2):
            pair = jnp.concatenate([tap(*taps[2 * n]), tap(*taps[2 * n + 1])], axis=-1)
            w_up[g * C2 : (g + 1) * C2, n * LANES : (n + 1) * LANES] = pair.astype(BF)

    w_head[...] = jnp.zeros(w_head.shape, BF)
    tall = head[...].astype(F32).T.astype(BF)
    for k in range(8):
        w_head[k * LANES + C1 : (k + 1) * LANES, k * PATCH : (k + 1) * PATCH] = tall


def call(body, args, outs, scratch):
    return pl.pallas_call(
        body,
        out_shape=[s if isinstance(s, jax.ShapeDtypeStruct) else jax.ShapeDtypeStruct(s, BF) for s in outs],
        in_specs=[pl.BlockSpec(memory_space=space) for _, space in args],
        out_specs=[pl.BlockSpec(memory_space=pltpu.VMEM)] * len(outs),
        scratch_shapes=scratch,
        compiler_params=pltpu.CompilerParams(vmem_limit_bytes=24 * 1024 * 1024),
    )(*[arg for arg, _ in args])


def on_device(
    frames,
    start_fine,
    start_coarse,
    enc_stem,
    enc_fine_x,
    enc_fine_h,
    enc_down,
    enc_coarse_x,
    enc_coarse_h,
    fc_coarse_h,
    fc_up,
    fc_fine_x,
    fc_fine_h,
    fc_head,
):
    count = lax.axis_size(LINE)
    across = [(i, i + 1) for i in range(1, count - 1, 2)]
    across = across + [(b, a) for a, b in across]

    def outer_swap(x):
        return lax.ppermute(x, LINE, across)

    def inner_swap(x):
        return lax.ppermute(x, "section", [(0, 1), (1, 0)])

    fine = start_fine.reshape(4, SUB, FB * C1)
    patches = frames.reshape(FRAMES, 4, SUB, FB * PATCH)
    coarse = start_coarse.reshape(2, SUB, CB * C2)

    def on_chip(*values):
        return [(value, pltpu.VMEM) for value in values]

    def fine_buf(rows):
        return pltpu.VMEM((rows, FB + 2, SUB, LANES), BF)

    def coarse_buf(rows):
        return pltpu.VMEM((rows, CB + 2, SUB, 4 * LANES), BF)

    rows = (3, SUB, FB * (C1 + FRAMES * PATCH))
    own, to_outer, to_inner = call(pack_body, on_chip(fine, patches[0], patches[1]), [(4,) + rows[1:], rows, rows], [])
    outer, inner = outer_swap(to_outer), inner_swap(to_inner)

    acc_buf = pltpu.VMEM((CB * SUB, 5 * LANES), F32)
    flat = (9 * C2, 3 * C2)

    def prepare(body, values, outs):
        scratch = [pltpu.VMEM(value.shape, BF) for value in values]
        return call(
            body, [(value, pl.ANY) for value in values], outs, scratch + [pltpu.SemaphoreType.DMA((len(values),))]
        )

    kernel = (9, C1, 3 * C1)
    wide = (9 * LANES, 2 * LANES)
    w_stem, w_enc, w_down = prepare(
        prepare_encoder_body,
        [enc_stem, enc_fine_x.reshape(kernel), enc_fine_h.reshape(kernel), enc_down.reshape(kernel)],
        [(8 * PATCH, 8 * LANES), wide, wide],
    )
    w_up, w_fc, w_head = prepare(
        prepare_forecaster_body,
        [jnp.swapaxes(fc_up.reshape(9, C2, C1), 1, 2), fc_fine_x.reshape(kernel), fc_fine_h.reshape(kernel), fc_head.T],
        [(4 * C2, 2 * LANES), wide, (8 * LANES, 8 * PATCH)],
    )
    coarse_o, coarse_i = outer_swap(coarse), inner_swap(coarse)

    halo = (3 * ROW_TILES, SUB, LANES)
    edge = (2, FB // 2, SUB, LANES)
    state_f, low_own, to_outer, to_inner, state_fo, state_fi = call(
        fine_encoder_body,
        on_chip(own, outer, inner, w_stem, w_enc, w_down),
        [(4, FB // 2, SUB, LANES), (4 * ROW_TILES, SUB, LANES), halo, halo, edge, edge],
        [fine_buf(9), fine_buf(9), fine_buf(9), pltpu.VMEM((9, FB, SUB, LANES), BF)],
    )
    got_o, got_i = outer_swap(to_outer), inner_swap(to_inner)

    acc_first, h_first = call(
        coarse_state_body,
        on_chip(coarse, coarse_o, coarse_i, enc_coarse_h.reshape(flat)),
        [jax.ShapeDtypeStruct((4, CB * SUB, 5 * LANES), F32), (4, CB + 2, SUB, 4 * LANES)],
        [coarse_buf(6)],
    )
    state_fo, state_fi = outer_swap(state_fo), inner_swap(state_fi)

    (state_c,) = call(
        coarse_encoder_body,
        on_chip(low_own, got_o, got_i, acc_first, h_first, enc_coarse_x.reshape(flat), enc_coarse_h.reshape(flat)),
        [(2 * ROW_TILES, SUB, LANES)],
        [coarse_buf(6), coarse_buf(4), coarse_buf(4), acc_buf, acc_buf],
    )
    state_ci = inner_swap(state_c)
    state_co = outer_swap(jnp.concatenate([state_c, state_ci[ROW_TILES:]], axis=0))
    third = inner_swap(state_co[:ROW_TILES])

    (out,) = call(
        forecaster_body,
        on_chip(state_c, state_co, state_ci, third, state_f, state_fo, state_fi, fc_coarse_h.reshape(flat))
        + on_chip(w_up, w_fc, w_head),
        [(HORIZON, 4, SUB, FB * PATCH)],
        [coarse_buf(8), coarse_buf(6), coarse_buf(5), fine_buf(8), fine_buf(6), fine_buf(4), acc_buf],
    )
    return out.reshape(HORIZON, 4, COLS * PATCH)


def solution(mesh):
    line = ("groups", "tile", "section")
    return jax.shard_map(
        on_device,
        mesh=mesh,
        in_specs=(P(None, line, None), P(line, None), P(line, None)) + (P(),) * 11,
        out_specs=P(None, line, None),
        check_vma=False,
    )
```

```python
import jax
import jax.numpy as jnp
from jax import lax
from jax.experimental import pallas as pl
from jax.experimental.pallas import tpu as pltpu
from jax.sharding import PartitionSpec as P


C1 = 64
C2 = 192
PATCH = 16
FRAMES = 2
HORIZON = 2
COLS = 512
SUB = 16
FB = COLS // SUB
CB = COLS // 2 // SUB
LANES = 128
BF = jnp.bfloat16
F32 = jnp.float32
LINE = ("tile", "section")
PAIRS = CB // 2
ROW_TILES = 3 * PAIRS


def leaky(values):
    return jnp.where(values > 0, values, 0.2 * values)


def low_half(shape):
    return lax.broadcasted_iota(jnp.int32, shape, len(shape) - 1) < 64


def swap_halves(x):
    flat = x.reshape(-1, LANES)
    return pltpu.roll(flat, 64, 1).reshape(x.shape)


def swap_bf(x):
    return swap_halves(x.astype(F32)).astype(BF)


def sigmoid(x):
    return 0.5 * jnp.tanh(0.5 * x) + 0.5


def shift_sub(x, by):
    wide = x.astype(F32)
    row = lax.broadcasted_iota(jnp.int32, wide.shape, 0)
    if by > 0:
        moved = jnp.where(row == 0, 0.0, pltpu.roll(wide, 1, 0))
    else:
        moved = jnp.where(row == SUB - 1, 0.0, pltpu.roll(wide, SUB - 1, 0))
    return moved.astype(BF)


def seal(ref, idx, blocks):
    ref[idx, 0] = shift_sub(ref[idx, blocks], 1)
    ref[idx, blocks + 1] = shift_sub(ref[idx, 1], -1)


def fine_patches(ref, idx, lo, count):
    parts = [
        ref[idx + dr, pl.ds(lo + dj, count)].reshape(count * SUB, LANES)
        for dr in (-1, 0, 1)
        for dj in (0, 1, 2)
    ]
    return jnp.concatenate(parts, axis=-1)


def fine_gru(src, idx, weight, valid, emit):
    count = 16
    for lo in range(0, FB, count):
        acc = jnp.dot(fine_patches(src, idx, lo, count), weight[...], preferred_element_type=F32)
        gates = sigmoid(acc[:, :LANES])
        cand = acc[:, LANES:]
        cand = jnp.tanh(cand + swap_halves(gates * cand))
        old = src[idx, pl.ds(1 + lo, count)].reshape(count * SUB, LANES).astype(F32)
        new = (1.0 - gates) * cand + gates * old
        new = jnp.where(valid, new, 0.0).astype(BF)
        emit(lo, count, new.reshape(count, SUB, LANES))


def down_row(src, idx, weight):
    parts = []
    for dr in (-1, 0, 1):
        row = src[idx + dr].reshape(FB // 2 + 1, 2, SUB, LANES)
        for tap in (row[:CB, 0], row[:CB, 1], row[1:, 0]):
            parts.append(tap.reshape(CB * SUB, LANES))
    lhs = jnp.concatenate(parts, axis=-1)
    return jnp.dot(lhs, weight[...], preferred_element_type=F32)


def coarse_forms(t0, t1):
    lo = low_half(t0.shape)
    r0, r1 = swap_halves(t0), swap_halves(t1)
    return (
        t0.astype(BF),
        jnp.where(lo, t1, 0.0).astype(BF),
        jnp.where(lo, 0.0, r0).astype(BF),
        jnp.where(lo, r0, r1).astype(BF),
    )


def put_forms(ref, idx, forms):
    for k, tile in enumerate(forms):
        ref[idx, 1 : CB + 1, :, k * LANES : (k + 1) * LANES] = tile.reshape(CB, SUB, LANES)
    seal(ref, idx, CB)


def put_packed(ref, idx, tiles):
    t = [tiles(i).astype(F32) for i in range(3)]
    r = [swap_halves(x) for x in t]
    lo = low_half(t[0].shape)
    even = (t[0], jnp.where(lo, t[1], 0.0), jnp.where(lo, 0.0, r[0]), jnp.where(lo, r[0], r[1]))
    odd = (
        jnp.where(lo, r[1], r[2]),
        jnp.where(lo, r[2], 0.0),
        jnp.where(lo, 0.0, t[1]),
        t[2],
    )
    for k in range(4):
        both = jnp.stack([even[k].astype(BF), odd[k].astype(BF)], axis=1)
        ref[idx, 1 : CB + 1, :, k * LANES : (k + 1) * LANES] = both.reshape(CB, SUB, LANES)
    seal(ref, idx, CB)


def pack_forms(forms):
    f = [x.reshape(CB // 2, 2, SUB, LANES) for x in forms]
    lo = low_half((CB // 2, SUB, LANES))
    return (f[0][:, 0], jnp.where(lo, f[1][:, 0], f[2][:, 1]), f[3][:, 1])


def coarse_patches(ref, idx):
    def tile(dr, dj, k):
        return ref[idx + dr, dj : dj + CB, :, k * LANES : (k + 1) * LANES].reshape(CB * SUB, LANES)

    lo = low_half((CB * SUB, LANES))

    def aligned(dr):
        return [
            tile(dr, 0, 0),
            jnp.where(lo, tile(dr, 0, 1), tile(dr, 1, 2)),
            tile(dr, 1, 3),
            tile(dr, 2, 0),
        ]

    parts = aligned(-1)
    parts.append(jnp.where(lo, tile(-1, 2, 1), tile(0, 0, 2)))
    parts += [tile(0, 0, 3), tile(0, 1, 0), jnp.where(lo, tile(0, 1, 1), tile(0, 2, 2)), tile(0, 2, 3)]
    parts += aligned(1)
    parts.append(tile(1, 2, 1))
    return jnp.concatenate(parts, axis=-1)[:, : 9 * C2]


def coarse_gru(x_ref, x_idx, h_ref, h_idx, w_x, w_h, acc_x, acc_h, valid):
    width = 3 * C2
    if w_h is not None:
        acc_h[:, :width] = jnp.dot(coarse_patches(h_ref, h_idx), w_h[...], preferred_element_type=F32)
    if x_ref is not None:
        acc_x[:, :width] = jnp.dot(coarse_patches(x_ref, x_idx), w_x[...], preferred_element_type=F32)

    def part(ref, k):
        return ref[:, k * LANES : (k + 1) * LANES]

    gates = []
    for k in range(3):
        mixed = part(acc_h, k)
        if x_ref is not None:
            mixed = part(acc_x, k) + mixed
        gates.append(sigmoid(mixed))
    lo = low_half(gates[0].shape)
    g1, g2 = swap_halves(gates[1]), swap_halves(gates[2])
    update = (jnp.where(lo, g1, g2), g2)
    out = []
    for k in range(2):
        cand = gates[k] * part(acc_h, 3 + k)
        if x_ref is not None:
            cand = part(acc_x, 3 + k) + cand
        cand = jnp.tanh(cand)
        old = h_ref[h_idx, 1 : CB + 1, :, k * LANES : (k + 1) * LANES].reshape(CB * SUB, LANES).astype(F32)
        new = (1.0 - update[k]) * cand + update[k] * old
        out.append(jnp.where(valid, new, 0.0).astype(BF).astype(F32))
    return coarse_forms(out[0], out[1])


def place(per_device):
    upper = lax.axis_index("section") == 0
    line = lax.axis_index("tile") * lax.axis_size("section") + lax.axis_index("section")
    return upper, line * per_device, lax.axis_size(LINE) * per_device


def in_grid(row, rows):
    return jnp.logical_and(row >= 0, row < rows)


def pack_body(fine, first, second, own, to_outer, to_inner):
    upper, _, _ = place(4)
    for r in range(4):
        own[r, :, : FB * C1] = fine[r]
        own[r, :, FB * C1 : FB * (C1 + PATCH)] = first[r]
        own[r, :, FB * (C1 + PATCH) :] = second[r]
    for r in range(3):
        to_outer[r] = jnp.where(upper, own[r], own[r + 1])
        to_inner[r] = jnp.where(upper, own[r + 1], own[r])


def fine_encoder_body(
    own, outer, inner, w_stem, w_gru, w_down,
    state_out, low_own, to_outer, to_inner, state_outer, state_inner, p1, p2, p3, stem2,
):
    upper, first, rows = place(4)
    lo = low_half((1, SUB, LANES))

    def pick(idx, lanes):
        if 3 <= idx < 7:
            return own[idx - 3, :, lanes]
        r = idx if idx < 3 else idx - 7
        a, b = outer[r, :, lanes], inner[r, :, lanes]
        return jnp.where(upper, a, b) if idx < 3 else jnp.where(upper, b, a)

    for frame in range(FRAMES):
        for t in range(4):
            at = FB * C1 + frame * FB * PATCH + t * LANES
            patches = jnp.concatenate([pick(idx, slice(at, at + LANES)) for idx in range(9)], axis=0)
            for half in range(2):
                acc = jnp.dot(patches, w_stem[:, half * 512 : half * 512 + 512], preferred_element_type=F32)
                acc = leaky(acc).astype(BF)
                for k in range(4):
                    block = acc[:, k * LANES : (k + 1) * LANES].reshape(9, SUB, LANES)
                    at = 8 * t + 4 * half + k
                    if frame == 0:
                        p1[:, 1 + at] = block
                    else:
                        stem2[:, at] = block
    for idx in range(9):
        for k in range(FB // 2):
            pair = pick(idx, slice(k * LANES, (k + 1) * LANES))
            p1[idx, 1 + 2 * k] = jnp.where(lo[0], p1[idx, 1 + 2 * k], swap_bf(pair))
            p1[idx, 2 + 2 * k] = jnp.where(lo[0], p1[idx, 2 + 2 * k], pair)
        seal(p1, idx, FB)

    for idx in range(1, 8):
        def emit(lo_block, count, new):
            stems = stem2[idx, pl.ds(lo_block, count)]
            p2[idx, pl.ds(1 + lo_block, count)] = jnp.where(lo, stems, new)

        fine_gru(p1, idx, w_gru, in_grid(first + idx - 3, rows), emit)
        seal(p2, idx, FB)

    for idx in range(2, 7):
        def emit(lo_block, count, new):
            p3[idx, pl.ds(1 + lo_block, count)] = jnp.where(lo, jnp.zeros_like(new), new)

        fine_gru(p2, idx, w_gru, in_grid(first + idx - 3, rows), emit)
        seal(p3, idx, FB)

    def lowered(src, p):
        acc = leaky(down_row(src, 3 + 2 * p, w_down)).astype(BF).astype(F32)
        return pack_forms(coarse_forms(acc[:, :LANES], acc[:, LANES:]))

    def put(ref, at, tiles):
        for k, tile in enumerate(tiles):
            base = at * ROW_TILES + k * PAIRS
            ref[base : base + PAIRS] = tile

    for p in range(2):
        tiles = lowered(p2, p)
        put(low_own, p, tiles)
        put(to_outer, p, tiles)
        put(to_inner, p, tiles)
    for p in range(2):
        tiles = lowered(p3, p)
        put(low_own, 2 + p, tiles)
        outward = upper if p == 0 else jnp.logical_not(upper)

        @pl.when(outward)
        def _():
            put(to_outer, 2, tiles)

        @pl.when(jnp.logical_not(outward))
        def _():
            put(to_inner, 2, tiles)

    for r in range(4):
        for k in range(FB // 2):
            state_out[r, k] = jnp.where(lo[0], swap_bf(p3[3 + r, 1 + 2 * k]), p3[3 + r, 2 + 2 * k])
    for top, ref in ((upper, state_outer), (jnp.logical_not(upper), state_inner)):
        start = jnp.where(top, 0, 2)
        for r in range(2):
            ref[r] = state_out[start + r]


def zero_tail(acc):
    acc[:, 4 * LANES :] = jnp.zeros((CB * SUB, LANES), F32)


def packed_tiles(ref, at):
    return lambda i: ref[at * ROW_TILES + i * PAIRS : at * ROW_TILES + (i + 1) * PAIRS]


def raw_tiles(get):
    def tiles(i):
        return jnp.stack([get(slice((3 * k + i) * LANES, (3 * k + i + 1) * LANES)) for k in range(PAIRS)])

    return tiles


def coarse_state_body(own, outer, inner, w_h, acc_out, h_out, h0):
    upper, _, _ = place(2)
    for idx in range(6):
        if 2 <= idx < 4:
            put_packed(h0, idx, raw_tiles(lambda lanes: own[idx - 2, :, lanes]))
            continue
        r = idx if idx < 2 else idx - 4
        a, b = (outer, inner) if idx < 2 else (inner, outer)
        put_packed(h0, idx, raw_tiles(lambda lanes: jnp.where(upper, a[r, :, lanes], b[r, :, lanes])))

    for idx in range(0, 4):
        acc_out[idx, :, : 3 * C2] = jnp.dot(coarse_patches(h0, idx + 1), w_h[...], preferred_element_type=F32)
        acc_out[idx, :, 4 * LANES + C1 :] = jnp.zeros((CB * SUB, C1), F32)
        h_out[idx] = h0[idx + 1]


def put_row(ref, forms):
    for k, tile in enumerate(pack_forms(forms)):
        ref[k * PAIRS : (k + 1) * PAIRS] = tile


def coarse_encoder_body(
    low_own, low_outer, low_inner, acc_first, h_first, w_x, w_h, near, h1, x2, x1, acc_x, acc_h,
):
    upper, first, rows = place(2)
    zero_tail(acc_x)
    zero_tail(acc_h)

    for idx in range(6):
        if 2 <= idx < 4:
            put_packed(x1, idx, packed_tiles(low_own, idx - 2))
            continue
        r = idx if idx < 2 else idx - 4
        a, b = (low_outer, low_inner) if idx < 2 else (low_inner, low_outer)
        put_packed(x1, idx, lambda i: jnp.where(upper, packed_tiles(a, r)(i), packed_tiles(b, r)(i)))
    put_packed(x2, 1, packed_tiles(low_own, 2))
    put_packed(x2, 2, packed_tiles(low_own, 3))
    put_packed(x2, 0, lambda i: jnp.where(upper, packed_tiles(low_outer, 2)(i), packed_tiles(low_inner, 2)(i)))
    put_packed(x2, 3, lambda i: jnp.where(upper, packed_tiles(low_inner, 2)(i), packed_tiles(low_outer, 2)(i)))

    for idx in range(4):
        forms = coarse_gru(
            x1, idx + 1, h_first, idx, w_x, None, acc_x, acc_first.at[idx], in_grid(first + idx - 1, rows)
        )
        put_forms(h1, idx, forms)

    idx = jnp.where(upper, 1, 0)
    put_row(near, coarse_gru(x2, idx + 1, h1, idx + 1, w_x, w_h, acc_x, acc_h, True))


def coarse_rest_body(h1, x2, w_x, w_h, far, acc_x, acc_h):
    upper, _, _ = place(2)
    zero_tail(acc_x)
    zero_tail(acc_h)
    idx = jnp.where(upper, 0, 1)
    put_row(far, coarse_gru(x2, idx + 1, h1, idx + 1, w_x, w_h, acc_x, acc_h, True))


def raise_pair(src, idx, weight):
    def tile(dr, dj, k):
        return src[idx + dr, 1 + dj : 1 + dj + CB, :, k * LANES : (k + 1) * LANES].reshape(CB * SUB, LANES)

    lo = low_half((CB * SUB, LANES))
    parts = []
    for dr in (0, 1):
        parts += [tile(dr, 0, 0), jnp.where(lo, tile(dr, 0, 1), tile(dr, 1, 2)), tile(dr, 1, 3)]
    return jnp.dot(jnp.concatenate(parts, axis=-1), weight[...], preferred_element_type=F32)


def either(upper, a, i, b, j):
    return lambda t: jnp.where(upper, packed_tiles(a, i)(t), packed_tiles(b, j)(t))


def forecast_start_body(far, near, outer, in_far, in_near, w_h, s1, h2, acc_h):
    upper, first, rows = place(2)
    zero_tail(acc_h)
    put_packed(h2, 0, packed_tiles(outer, 2))
    put_packed(h2, 1, either(upper, outer, 1, in_far, 0))
    put_packed(h2, 2, either(upper, outer, 0, in_near, 0))
    put_packed(h2, 3, either(upper, far, 0, near, 0))
    put_packed(h2, 4, either(upper, near, 0, far, 0))
    put_packed(h2, 5, either(upper, in_near, 0, outer, 0))
    put_packed(h2, 6, either(upper, in_far, 0, outer, 1))
    put_packed(h2, 7, packed_tiles(outer, 2))

    shift = jnp.where(upper, 0, 1)
    for k in range(5):
        idx = k + shift
        forms = coarse_gru(None, 0, h2, idx + 1, None, w_h, None, acc_h, in_grid(first + idx - 2, rows))
        put_forms(s1, idx, forms)


def forecaster_body(
    s1_given, in_far, in_near, third, f_own, f_outer, f_inner, w_h, w_up, w_gru, w_head,
    out, s1, h2, s2, pf1, pf2, states, acc_h,
):
    upper, first_c, rows_c = place(2)
    _, first_f, rows_f = place(4)
    lo = low_half((1, SUB, LANES))
    zero_tail(acc_h)

    put_packed(h2, 0, either(upper, in_near, 0, third, 0))
    put_packed(h2, 1, packed_tiles(in_far, 0))
    put_packed(h2, 2, either(upper, third, 0, in_near, 0))
    last = jnp.where(upper, 5, 0)
    put_forms(
        s1, last, coarse_gru(None, 0, h2, 1, None, w_h, None, acc_h, in_grid(first_c + last - 2, rows_c))
    )

    for idx in range(8):
        for k in range(FB // 2):
            if 2 <= idx < 6:
                pair = f_own[idx - 2, k]
            elif idx < 2:
                pair = jnp.where(upper, f_outer[idx, k], f_inner[idx, k])
            else:
                pair = jnp.where(upper, f_inner[idx - 6, k], f_outer[idx - 6, k])
            pf1[idx, 1 + 2 * k] = swap_bf(pair)
            pf1[idx, 2 + 2 * k] = pair

    for idx in range(0, 4):
        forms = coarse_gru(None, 0, s1, idx + 1, None, w_h, None, acc_h, in_grid(first_c + idx - 1, rows_c))
        put_forms(s2, idx, forms)

    s2[4] = jnp.zeros(s2.shape[1:], BF)

    def raise_rows(src, idx, fine, at, coarse_row):
        acc = raise_pair(src, idx, w_up)
        acc = jnp.where(in_grid(coarse_row, rows_c), leaky(acc), 0.0)
        for half, row in enumerate(at):
            if row is None:
                continue
            tile = acc[:, half * LANES : (half + 1) * LANES]
            even = tile.astype(BF).reshape(CB, SUB, LANES)
            odd = swap_halves(tile).astype(BF).reshape(CB, SUB, LANES)
            both = jnp.stack([even, odd], axis=1).reshape(FB, SUB, LANES)
            fine[row, 1 : FB + 1] = jnp.where(lo, both, fine[row, 1 : FB + 1])

    for k in range(0, 4):
        raise_rows(s1, k + 1, pf1, (2 * k, 2 * k + 1), first_c + k - 1)
        seal(pf1, 2 * k, FB)
        seal(pf1, 2 * k + 1, FB)

    for idx in range(0, 6):
        def emit(lo_block, count, new):
            pf2[idx, pl.ds(1 + lo_block, count)] = new

        fine_gru(pf1, idx + 1, w_gru, in_grid(first_f + idx - 1, rows_f), emit)

    def head(step, ref, base):
        for t in range(4):
            lhs = jnp.concatenate(
                [ref[base : base + 4, 1 + 8 * t + k].reshape(4 * SUB, LANES) for k in range(8)], axis=-1
            )
            acc = jnp.dot(lhs, w_head[...], preferred_element_type=F32).astype(BF)
            out[step, :, :, t * LANES : (t + 1) * LANES] = acc.reshape(4, SUB, LANES)

    head(0, pf2, 1)

    raise_rows(s2, 0, pf2, (None, 0), first_c - 1)
    raise_rows(s2, 1, pf2, (1, 2), first_c)
    raise_rows(s2, 2, pf2, (3, 4), first_c + 1)
    raise_rows(s2, 3, pf2, (5, None), first_c + 2)
    for idx in range(6):
        seal(pf2, idx, FB)

    for idx in range(0, 4):
        def emit(lo_block, count, new):
            states[idx, pl.ds(1 + lo_block, count)] = new

        fine_gru(pf2, idx + 1, w_gru, True, emit)

    head(1, states, 0)


def to_upper(x):
    return jnp.concatenate([jnp.zeros(x.shape, F32), x.astype(F32)], axis=-1).astype(BF)


def to_lower(x):
    return jnp.concatenate([x.astype(F32), jnp.zeros(x.shape, F32)], axis=-1).astype(BF)


def fetch_all(given, copies, sems):
    fetches = [pltpu.make_async_copy(src, dst, sems.at[i]) for i, (src, dst) in enumerate(zip(given, copies))]
    for fetch in fetches:
        fetch.start()
    for fetch in fetches:
        fetch.wait()


def arrange_gru(kx, kh, w):
    for k in range(9):
        at = k * LANES
        w[at : at + C1, :LANES] = kx[k, :, :LANES]
        w[at : at + C1, LANES:] = to_upper(kx[k, :, LANES:])
        w[at + C1 : at + LANES, :LANES] = kh[k, :, :LANES]
        w[at + C1 : at + LANES, LANES:] = to_lower(kh[k, :, LANES:])


def prepare_encoder_body(*refs):
    given, (w_stem, w_enc, w_down), copies, sems = refs[:4], refs[4:7], refs[7:11], refs[11]
    fetch_all(given, copies, sems)
    stem, enc_x, enc_h, down = copies
    arrange_gru(enc_x, enc_h, w_enc)
    for k in range(9):
        at = k * LANES
        w_down[at : at + C1] = jnp.zeros((C1, 2 * LANES), BF)
        w_down[at + C1 : at + LANES, :LANES] = down[k, :, :LANES]
        w_down[at + C1 : at + LANES, LANES:] = to_lower(down[k, :, LANES:])
    w_stem[...] = jnp.zeros(w_stem.shape, BF)
    wide = to_lower(stem[...])
    for k in range(8):
        w_stem[k * PATCH : (k + 1) * PATCH, k * LANES : (k + 1) * LANES] = wide


def prepare_forecaster_body(*refs):
    given, (w_up, w_fc, w_head), copies, sems = refs[:4], refs[4:7], refs[7:11], refs[11]
    fetch_all(given, copies, sems)
    up, fc_x, fc_h, head = copies
    arrange_gru(fc_x, fc_h, w_fc)

    def tap(a, b):
        return jnp.zeros((C2, C1), F32) if a is None else up[3 * a + b].astype(F32).T

    none = (None, None)
    for g, taps in enumerate((
        ((1, 1), (1, 0), (0, 1), (0, 0)),
        (none, (1, 2), none, (0, 2)),
        (none, none, (2, 1), (2, 0)),
        (none, none, none, (2, 2)),
    )):
        for n in range(2):
            pair = jnp.concatenate([tap(*taps[2 * n]), tap(*taps[2 * n + 1])], axis=-1)
            w_up[g * C2 : (g + 1) * C2, n * LANES : (n + 1) * LANES] = pair.astype(BF)

    w_head[...] = jnp.zeros(w_head.shape, BF)
    tall = head[...].astype(F32).T.astype(BF)
    for k in range(8):
        w_head[k * LANES + C1 : (k + 1) * LANES, k * PATCH : (k + 1) * PATCH] = tall


def call(body, args, outs, scratch, aliases={}):
    return pl.pallas_call(
        body,
        out_shape=[s if isinstance(s, jax.ShapeDtypeStruct) else jax.ShapeDtypeStruct(s, BF) for s in outs],
        in_specs=[pl.BlockSpec(memory_space=space) for _, space in args],
        out_specs=[pl.BlockSpec(memory_space=pltpu.VMEM)] * len(outs),
        scratch_shapes=scratch,
        input_output_aliases=aliases,
        compiler_params=pltpu.CompilerParams(vmem_limit_bytes=24 * 1024 * 1024),
    )(*[arg for arg, _ in args])


def on_device(
    frames,
    start_fine,
    start_coarse,
    enc_stem,
    enc_fine_x,
    enc_fine_h,
    enc_down,
    enc_coarse_x,
    enc_coarse_h,
    fc_coarse_h,
    fc_up,
    fc_fine_x,
    fc_fine_h,
    fc_head,
):
    count = lax.axis_size(LINE)
    across = [(i, i + 1) for i in range(1, count - 1, 2)]
    across = across + [(b, a) for a, b in across]

    def outer_swap(x):
        return lax.ppermute(x, LINE, across)

    def inner_swap(x):
        return lax.ppermute(x, "section", [(0, 1), (1, 0)])

    fine = start_fine.reshape(4, SUB, FB * C1)
    patches = frames.reshape(FRAMES, 4, SUB, FB * PATCH)
    coarse = start_coarse.reshape(2, SUB, CB * C2)

    def on_chip(*values):
        return [(value, pltpu.VMEM) for value in values]

    def fine_buf(rows):
        return pltpu.VMEM((rows, FB + 2, SUB, LANES), BF)

    def coarse_buf(rows):
        return pltpu.VMEM((rows, CB + 2, SUB, 4 * LANES), BF)

    rows = (3, SUB, FB * (C1 + FRAMES * PATCH))
    own, to_outer, to_inner = call(pack_body, on_chip(fine, patches[0], patches[1]), [(4,) + rows[1:], rows, rows], [])
    outer, inner = outer_swap(to_outer), inner_swap(to_inner)

    acc_buf = pltpu.VMEM((CB * SUB, 5 * LANES), F32)
    flat = (9 * C2, 3 * C2)

    def prepare(body, values, outs):
        scratch = [pltpu.VMEM(value.shape, BF) for value in values]
        return call(
            body, [(value, pl.ANY) for value in values], outs, scratch + [pltpu.SemaphoreType.DMA((len(values),))]
        )

    kernel = (9, C1, 3 * C1)
    wide = (9 * LANES, 2 * LANES)
    w_stem, w_enc, w_down = prepare(
        prepare_encoder_body,
        [enc_stem, enc_fine_x.reshape(kernel), enc_fine_h.reshape(kernel), enc_down.reshape(kernel)],
        [(8 * PATCH, 8 * LANES), wide, wide],
    )
    w_up, w_fc, w_head = prepare(
        prepare_forecaster_body,
        [jnp.swapaxes(fc_up.reshape(9, C2, C1), 1, 2), fc_fine_x.reshape(kernel), fc_fine_h.reshape(kernel), fc_head.T],
        [(4 * C2, 2 * LANES), wide, (8 * LANES, 8 * PATCH)],
    )
    coarse_o, coarse_i = outer_swap(coarse), inner_swap(coarse)

    halo = (3 * ROW_TILES, SUB, LANES)
    edge = (2, FB // 2, SUB, LANES)
    state_f, low_own, to_outer, to_inner, state_fo, state_fi = call(
        fine_encoder_body,
        on_chip(own, outer, inner, w_stem, w_enc, w_down),
        [(4, FB // 2, SUB, LANES), (4 * ROW_TILES, SUB, LANES), halo, halo, edge, edge],
        [fine_buf(9), fine_buf(9), fine_buf(9), pltpu.VMEM((9, FB, SUB, LANES), BF)],
    )
    got_o, got_i = outer_swap(to_outer), inner_swap(to_inner)

    acc_first, h_first = call(
        coarse_state_body,
        on_chip(coarse, coarse_o, coarse_i, enc_coarse_h.reshape(flat)),
        [jax.ShapeDtypeStruct((4, CB * SUB, 5 * LANES), F32), (4, CB + 2, SUB, 4 * LANES)],
        [coarse_buf(6)],
    )
    state_fo, state_fi = outer_swap(state_fo), inner_swap(state_fi)

    w_x, w_h = enc_coarse_x.reshape(flat), enc_coarse_h.reshape(flat)
    four = (4, CB + 2, SUB, 4 * LANES)
    near, h1, x2 = call(
        coarse_encoder_body,
        on_chip(low_own, got_o, got_i, acc_first, h_first, w_x, w_h),
        [(ROW_TILES, SUB, LANES), four, four],
        [coarse_buf(6), acc_buf, acc_buf],
    )
    in_near = inner_swap(near)
    (far,) = call(coarse_rest_body, on_chip(h1, x2, w_x, w_h), [(ROW_TILES, SUB, LANES)], [acc_buf, acc_buf])
    in_far = inner_swap(far)
    state_co = outer_swap(jnp.concatenate([far, near, in_near], axis=0))
    third = inner_swap(state_co[:ROW_TILES])

    w_f = fc_coarse_h.reshape(flat)
    (s1,) = call(
        forecast_start_body,
        on_chip(far, near, state_co, in_far, in_near, w_f),
        [(6, CB + 2, SUB, 4 * LANES)],
        [coarse_buf(8), acc_buf],
    )
    out, _ = call(
        forecaster_body,
        on_chip(s1, in_far, in_near, third, state_f, state_fo, state_fi, w_f, w_up, w_fc, w_head),
        [(HORIZON, 4, SUB, FB * PATCH), (6, CB + 2, SUB, 4 * LANES)],
        [coarse_buf(3), coarse_buf(5), fine_buf(8), fine_buf(6), fine_buf(4), acc_buf],
        {0: 1},
    )
    return out.reshape(HORIZON, 4, COLS * PATCH)


def solution(mesh):
    line = ("groups", "tile", "section")
    return jax.shard_map(
        on_device,
        mesh=mesh,
        in_specs=(P(None, line, None), P(line, None), P(line, None)) + (P(),) * 11,
        out_specs=P(None, line, None),
        check_vma=False,
    )
```

```python
import jax
import jax.numpy as jnp
from jax import lax
from jax.experimental import pallas as pl
from jax.experimental.pallas import tpu as pltpu
from jax.sharding import PartitionSpec as P


C1 = 64
C2 = 192
PATCH = 16
FRAMES = 2
HORIZON = 2
COLS = 512
SUB = 16
FB = COLS // SUB
CB = COLS // 2 // SUB
LANES = 128
BF = jnp.bfloat16
F32 = jnp.float32
LINE = ("tile", "section")
PAIRS = CB // 2
ROW_TILES = 3 * PAIRS


def leaky(values):
    return jnp.where(values > 0, values, 0.2 * values)


def low_half(shape):
    return lax.broadcasted_iota(jnp.int32, shape, len(shape) - 1) < 64


def swap_halves(x):
    flat = x.reshape(-1, LANES)
    return pltpu.roll(flat, 64, 1).reshape(x.shape)


def swap_bf(x):
    return swap_halves(x.astype(F32)).astype(BF)


def sigmoid(x):
    return 0.5 * jnp.tanh(0.5 * x) + 0.5


def shift_sub(x, by):
    wide = x.astype(F32)
    row = lax.broadcasted_iota(jnp.int32, wide.shape, 0)
    if by > 0:
        moved = jnp.where(row == 0, 0.0, pltpu.roll(wide, 1, 0))
    else:
        moved = jnp.where(row == SUB - 1, 0.0, pltpu.roll(wide, SUB - 1, 0))
    return moved.astype(BF)


def seal(ref, idx, blocks):
    ref[idx, 0] = shift_sub(ref[idx, blocks], 1)
    ref[idx, blocks + 1] = shift_sub(ref[idx, 1], -1)


def row_of(src, idx):
    if isinstance(src, list):
        ref, at = src[idx]
        return ref.at[at]
    return src.at[idx]


def fine_patches(src, idx, lo, count):
    parts = [
        row_of(src, idx + dr)[pl.ds(lo + dj, count)].reshape(count * SUB, LANES)
        for dr in (-1, 0, 1)
        for dj in (0, 1, 2)
    ]
    return jnp.concatenate(parts, axis=-1)


def fine_gru(src, idx, weight, valid, emit):
    count = 16
    for lo in range(0, FB, count):
        acc = jnp.dot(fine_patches(src, idx, lo, count), weight[...], preferred_element_type=F32)
        gates = sigmoid(acc[:, :LANES])
        cand = acc[:, LANES:]
        cand = jnp.tanh(cand + swap_halves(gates * cand))
        old = row_of(src, idx)[pl.ds(1 + lo, count)].reshape(count * SUB, LANES).astype(F32)
        new = (1.0 - gates) * cand + gates * old
        new = jnp.where(valid, new, 0.0).astype(BF)
        emit(lo, count, new.reshape(count, SUB, LANES))


def down_row(src, idx, weight):
    parts = []
    for dr in (-1, 0, 1):
        row = row_of(src, idx + dr)[...].reshape(FB // 2 + 1, 2, SUB, LANES)
        for tap in (row[:CB, 0], row[:CB, 1], row[1:, 0]):
            parts.append(tap.reshape(CB * SUB, LANES))
    lhs = jnp.concatenate(parts, axis=-1)
    return jnp.dot(lhs, weight[...], preferred_element_type=F32)


def coarse_forms(t0, t1):
    lo = low_half(t0.shape)
    r0, r1 = swap_halves(t0), swap_halves(t1)
    return (
        t0.astype(BF),
        jnp.where(lo, t1, 0.0).astype(BF),
        jnp.where(lo, 0.0, r0).astype(BF),
        jnp.where(lo, r0, r1).astype(BF),
    )


def put_forms(ref, idx, forms):
    for k, tile in enumerate(forms):
        ref[idx, 1 : CB + 1, :, k * LANES : (k + 1) * LANES] = tile.reshape(CB, SUB, LANES)
    seal(ref, idx, CB)


def put_packed(ref, idx, tiles):
    t = [tiles(i).astype(F32) for i in range(3)]
    r = [swap_halves(x) for x in t]
    lo = low_half(t[0].shape)
    even = (t[0], jnp.where(lo, t[1], 0.0), jnp.where(lo, 0.0, r[0]), jnp.where(lo, r[0], r[1]))
    odd = (
        jnp.where(lo, r[1], r[2]),
        jnp.where(lo, r[2], 0.0),
        jnp.where(lo, 0.0, t[1]),
        t[2],
    )
    for k in range(4):
        both = jnp.stack([even[k].astype(BF), odd[k].astype(BF)], axis=1)
        ref[idx, 1 : CB + 1, :, k * LANES : (k + 1) * LANES] = both.reshape(CB, SUB, LANES)
    seal(ref, idx, CB)


def pack_forms(forms):
    f = [x.reshape(CB // 2, 2, SUB, LANES) for x in forms]
    lo = low_half((CB // 2, SUB, LANES))
    return (f[0][:, 0], jnp.where(lo, f[1][:, 0], f[2][:, 1]), f[3][:, 1])


def coarse_patches(ref, idx):
    def tile(dr, dj, k):
        return ref[idx + dr, dj : dj + CB, :, k * LANES : (k + 1) * LANES].reshape(CB * SUB, LANES)

    lo = low_half((CB * SUB, LANES))

    def aligned(dr):
        return [
            tile(dr, 0, 0),
            jnp.where(lo, tile(dr, 0, 1), tile(dr, 1, 2)),
            tile(dr, 1, 3),
            tile(dr, 2, 0),
        ]

    parts = aligned(-1)
    parts.append(jnp.where(lo, tile(-1, 2, 1), tile(0, 0, 2)))
    parts += [tile(0, 0, 3), tile(0, 1, 0), jnp.where(lo, tile(0, 1, 1), tile(0, 2, 2)), tile(0, 2, 3)]
    parts += aligned(1)
    parts.append(tile(1, 2, 1))
    return jnp.concatenate(parts, axis=-1)[:, : 9 * C2]


def coarse_gru(x_ref, x_idx, h_ref, h_idx, w_x, w_h, acc_x, acc_h, valid):
    width = 3 * C2
    if w_h is not None:
        acc_h[:, :width] = jnp.dot(coarse_patches(h_ref, h_idx), w_h[...], preferred_element_type=F32)
    if x_ref is not None:
        acc_x[:, :width] = jnp.dot(coarse_patches(x_ref, x_idx), w_x[...], preferred_element_type=F32)

    def part(ref, k):
        return ref[:, k * LANES : (k + 1) * LANES]

    gates = []
    for k in range(3):
        mixed = part(acc_h, k)
        if x_ref is not None:
            mixed = part(acc_x, k) + mixed
        gates.append(sigmoid(mixed))
    lo = low_half(gates[0].shape)
    g1, g2 = swap_halves(gates[1]), swap_halves(gates[2])
    update = (jnp.where(lo, g1, g2), g2)
    out = []
    for k in range(2):
        cand = gates[k] * part(acc_h, 3 + k)
        if x_ref is not None:
            cand = part(acc_x, 3 + k) + cand
        cand = jnp.tanh(cand)
        old = h_ref[h_idx, 1 : CB + 1, :, k * LANES : (k + 1) * LANES].reshape(CB * SUB, LANES).astype(F32)
        new = (1.0 - update[k]) * cand + update[k] * old
        out.append(jnp.where(valid, new, 0.0).astype(BF).astype(F32))
    return coarse_forms(out[0], out[1])


def place(per_device):
    upper = lax.axis_index("section") == 0
    line = lax.axis_index("tile") * lax.axis_size("section") + lax.axis_index("section")
    return upper, line * per_device, lax.axis_size(LINE) * per_device


def in_grid(row, rows):
    return jnp.logical_and(row >= 0, row < rows)


def pack_body(fine, first, second, own, to_outer, to_inner):
    upper, _, _ = place(4)
    for r in range(4):
        own[r, :, : FB * C1] = fine[r]
        own[r, :, FB * C1 : FB * (C1 + PATCH)] = first[r]
        own[r, :, FB * (C1 + PATCH) :] = second[r]
    for r in range(3):
        to_outer[r] = jnp.where(upper, own[r], own[r + 1])
        to_inner[r] = jnp.where(upper, own[r + 1], own[r])


def fill_fine(get, count, w_stem, p1, stem2):
    lo = low_half((SUB, LANES))
    for frame in range(FRAMES):
        for t in range(4):
            at = FB * C1 + frame * FB * PATCH + t * LANES
            patches = jnp.concatenate([get(r, slice(at, at + LANES)) for r in range(count)], axis=0)
            for half in range(2):
                acc = jnp.dot(patches, w_stem[:, half * 512 : half * 512 + 512], preferred_element_type=F32)
                acc = leaky(acc).astype(BF)
                for k in range(4):
                    block = acc[:, k * LANES : (k + 1) * LANES].reshape(count, SUB, LANES)
                    at_block = 8 * t + 4 * half + k
                    if frame == 0:
                        p1[:, 1 + at_block] = block
                    else:
                        stem2[:, at_block] = block
    for r in range(count):
        for k in range(FB // 2):
            pair = get(r, slice(k * LANES, (k + 1) * LANES))
            p1[r, 1 + 2 * k] = jnp.where(lo, p1[r, 1 + 2 * k], swap_bf(pair))
            p1[r, 2 + 2 * k] = jnp.where(lo, p1[r, 2 + 2 * k], pair)
        seal(p1, r, FB)


def first_fine(src, idx, w_gru, valid, stems, dst, at):
    lo = low_half((1, SUB, LANES))

    def emit(lo_block, count, new):
        dst[at, pl.ds(1 + lo_block, count)] = jnp.where(lo, stems[pl.ds(lo_block, count)], new)

    fine_gru(src, idx, w_gru, valid, emit)
    seal(dst, at, FB)


def fine_own_body(own, w_stem, w_gru, p1, stem2, inside):
    fill_fine(lambda r, lanes: own[r, :, lanes], 4, w_stem, p1, stem2)
    for r in range(2):
        first_fine(p1, 1 + r, w_gru, True, stem2.at[1 + r], inside, r)


def fine_encoder_body(
    p1_own, stem2_own, inside, outer, inner, w_stem, w_gru, w_down,
    state_out, low_own, to_outer, to_inner, state_outer, state_inner, p1_halo, stem2_halo, p2_rest, p3,
):
    upper, first, rows = place(4)
    lo = low_half((1, SUB, LANES))

    def get(r, lanes):
        above = r < 3
        at = r if above else r - 3
        a, b = outer[at, :, lanes], inner[at, :, lanes]
        return jnp.where(upper, a, b) if above else jnp.where(upper, b, a)

    fill_fine(get, 5, w_stem, p1_halo, stem2_halo)
    p1 = [(p1_halo, r) for r in range(3)] + [(p1_own, r) for r in range(4)] + [(p1_halo, r) for r in (3, 4)]
    stem2 = [(stem2_halo, r) for r in range(3)] + [(stem2_own, r) for r in range(4)] + [(stem2_halo, 3)]
    p2 = [None] + [(p2_rest, r) for r in range(3)] + [(inside, 0), (inside, 1), (p2_rest, 3), (p2_rest, 4)]
    for idx in (1, 2, 3, 6, 7):
        dst, at = p2[idx]
        first_fine(p1, idx, w_gru, in_grid(first + idx - 3, rows), row_of(stem2, idx), dst, at)

    for idx in range(2, 7):
        def emit(lo_block, count, new):
            p3[idx, pl.ds(1 + lo_block, count)] = jnp.where(lo, jnp.zeros_like(new), new)

        fine_gru(p2, idx, w_gru, in_grid(first + idx - 3, rows), emit)
        seal(p3, idx, FB)

    def lowered(src, p):
        acc = leaky(down_row(src, 3 + 2 * p, w_down)).astype(BF).astype(F32)
        return pack_forms(coarse_forms(acc[:, :LANES], acc[:, LANES:]))

    def put(ref, at, tiles):
        for k, tile in enumerate(tiles):
            base = at * ROW_TILES + k * PAIRS
            ref[base : base + PAIRS] = tile

    for p in range(2):
        tiles = lowered(p2, p)
        put(low_own, p, tiles)
        put(to_outer, p, tiles)
        put(to_inner, p, tiles)
    for p in range(2):
        tiles = lowered(p3, p)
        put(low_own, 2 + p, tiles)
        outward = upper if p == 0 else jnp.logical_not(upper)

        @pl.when(outward)
        def _():
            put(to_outer, 2, tiles)

        @pl.when(jnp.logical_not(outward))
        def _():
            put(to_inner, 2, tiles)

    for r in range(4):
        for k in range(FB // 2):
            state_out[r, k] = jnp.where(lo[0], swap_bf(p3[3 + r, 1 + 2 * k]), p3[3 + r, 2 + 2 * k])
    for top, ref in ((upper, state_outer), (jnp.logical_not(upper), state_inner)):
        start = jnp.where(top, 0, 2)
        for r in range(2):
            ref[r] = state_out[start + r]


def zero_tail(acc):
    acc[:, 4 * LANES :] = jnp.zeros((CB * SUB, LANES), F32)


def packed_tiles(ref, at):
    return lambda i: ref[at * ROW_TILES + i * PAIRS : at * ROW_TILES + (i + 1) * PAIRS]


def raw_tiles(get):
    def tiles(i):
        return jnp.stack([get(slice((3 * k + i) * LANES, (3 * k + i + 1) * LANES)) for k in range(PAIRS)])

    return tiles


def coarse_state_body(own, outer, inner, w_h, acc_out, h_out, h0):
    upper, _, _ = place(2)
    for idx in range(6):
        if 2 <= idx < 4:
            put_packed(h0, idx, raw_tiles(lambda lanes: own[idx - 2, :, lanes]))
            continue
        r = idx if idx < 2 else idx - 4
        a, b = (outer, inner) if idx < 2 else (inner, outer)
        put_packed(h0, idx, raw_tiles(lambda lanes: jnp.where(upper, a[r, :, lanes], b[r, :, lanes])))

    for idx in range(0, 4):
        acc_out[idx, :, : 3 * C2] = jnp.dot(coarse_patches(h0, idx + 1), w_h[...], preferred_element_type=F32)
        acc_out[idx, :, 4 * LANES + C1 :] = jnp.zeros((CB * SUB, C1), F32)
        h_out[idx] = h0[idx + 1]


def put_row(ref, forms):
    for k, tile in enumerate(pack_forms(forms)):
        ref[k * PAIRS : (k + 1) * PAIRS] = tile


def coarse_encoder_body(
    low_own, low_outer, low_inner, acc_first, h_first, w_x, w_h, near, h1, x2, x1, acc_x, acc_h,
):
    upper, first, rows = place(2)
    zero_tail(acc_x)
    zero_tail(acc_h)

    for idx in range(6):
        if 2 <= idx < 4:
            put_packed(x1, idx, packed_tiles(low_own, idx - 2))
            continue
        r = idx if idx < 2 else idx - 4
        a, b = (low_outer, low_inner) if idx < 2 else (low_inner, low_outer)
        put_packed(x1, idx, lambda i: jnp.where(upper, packed_tiles(a, r)(i), packed_tiles(b, r)(i)))
    put_packed(x2, 1, packed_tiles(low_own, 2))
    put_packed(x2, 2, packed_tiles(low_own, 3))
    put_packed(x2, 0, lambda i: jnp.where(upper, packed_tiles(low_outer, 2)(i), packed_tiles(low_inner, 2)(i)))
    put_packed(x2, 3, lambda i: jnp.where(upper, packed_tiles(low_inner, 2)(i), packed_tiles(low_outer, 2)(i)))

    for idx in range(4):
        forms = coarse_gru(
            x1, idx + 1, h_first, idx, w_x, None, acc_x, acc_first.at[idx], in_grid(first + idx - 1, rows)
        )
        put_forms(h1, idx, forms)

    idx = jnp.where(upper, 1, 0)
    put_row(near, coarse_gru(x2, idx + 1, h1, idx + 1, w_x, w_h, acc_x, acc_h, True))


def coarse_rest_body(h1, x2, w_x, w_h, far, acc_x, acc_h):
    upper, _, _ = place(2)
    zero_tail(acc_x)
    zero_tail(acc_h)
    idx = jnp.where(upper, 0, 1)
    put_row(far, coarse_gru(x2, idx + 1, h1, idx + 1, w_x, w_h, acc_x, acc_h, True))


def raise_pair(src, idx, weight):
    def tile(dr, dj, k):
        return src[idx + dr, 1 + dj : 1 + dj + CB, :, k * LANES : (k + 1) * LANES].reshape(CB * SUB, LANES)

    lo = low_half((CB * SUB, LANES))
    parts = []
    for dr in (0, 1):
        parts += [tile(dr, 0, 0), jnp.where(lo, tile(dr, 0, 1), tile(dr, 1, 2)), tile(dr, 1, 3)]
    return jnp.dot(jnp.concatenate(parts, axis=-1), weight[...], preferred_element_type=F32)


def either(upper, a, i, b, j):
    return lambda t: jnp.where(upper, packed_tiles(a, i)(t), packed_tiles(b, j)(t))


def forecast_inner_body(far, near, in_far, in_near, w_h, s1, h2, acc_h):
    upper, first, rows = place(2)
    zero_tail(acc_h)
    put_packed(h2, 0, either(upper, far, 0, in_far, 0))
    put_packed(h2, 1, either(upper, near, 0, in_near, 0))
    put_packed(h2, 2, either(upper, in_near, 0, near, 0))
    put_packed(h2, 3, either(upper, in_far, 0, far, 0))
    at = jnp.where(upper, 3, 1)
    for k in range(2):
        forms = coarse_gru(None, 0, h2, k + 1, None, w_h, None, acc_h, in_grid(first + at + k - 2, rows))
        put_forms(s1, at + k, forms)


def forecast_outer_body(s1_given, far, near, outer, w_h, s1, h2, acc_h):
    upper, first, rows = place(2)
    zero_tail(acc_h)
    put_packed(h2, 0, either(upper, outer, 2, near, 0))
    put_packed(h2, 1, either(upper, outer, 1, far, 0))
    put_packed(h2, 2, packed_tiles(outer, 0))
    put_packed(h2, 3, either(upper, far, 0, outer, 1))
    put_packed(h2, 4, either(upper, near, 0, outer, 2))
    at = jnp.where(upper, 0, 3)
    for k in range(3):
        forms = coarse_gru(None, 0, h2, k + 1, None, w_h, None, acc_h, in_grid(first + at + k - 2, rows))
        put_forms(s1, at + k, forms)


def forecaster_body(
    s1_given, in_far, in_near, third, f_own, f_outer, f_inner, w_h, w_up, w_gru, w_head,
    out, s1, h2, s2, pf1, pf2, states, acc_h,
):
    upper, first_c, rows_c = place(2)
    _, first_f, rows_f = place(4)
    lo = low_half((1, SUB, LANES))
    zero_tail(acc_h)

    put_packed(h2, 0, either(upper, in_near, 0, third, 0))
    put_packed(h2, 1, packed_tiles(in_far, 0))
    put_packed(h2, 2, either(upper, third, 0, in_near, 0))
    last = jnp.where(upper, 5, 0)
    put_forms(
        s1, last, coarse_gru(None, 0, h2, 1, None, w_h, None, acc_h, in_grid(first_c + last - 2, rows_c))
    )

    for idx in range(8):
        for k in range(FB // 2):
            if 2 <= idx < 6:
                pair = f_own[idx - 2, k]
            elif idx < 2:
                pair = jnp.where(upper, f_outer[idx, k], f_inner[idx, k])
            else:
                pair = jnp.where(upper, f_inner[idx - 6, k], f_outer[idx - 6, k])
            pf1[idx, 1 + 2 * k] = swap_bf(pair)
            pf1[idx, 2 + 2 * k] = pair

    for idx in range(0, 4):
        forms = coarse_gru(None, 0, s1, idx + 1, None, w_h, None, acc_h, in_grid(first_c + idx - 1, rows_c))
        put_forms(s2, idx, forms)

    s2[4] = jnp.zeros(s2.shape[1:], BF)

    def raise_rows(src, idx, fine, at, coarse_row):
        acc = raise_pair(src, idx, w_up)
        acc = jnp.where(in_grid(coarse_row, rows_c), leaky(acc), 0.0)
        for half, row in enumerate(at):
            if row is None:
                continue
            tile = acc[:, half * LANES : (half + 1) * LANES]
            even = tile.astype(BF).reshape(CB, SUB, LANES)
            odd = swap_halves(tile).astype(BF).reshape(CB, SUB, LANES)
            both = jnp.stack([even, odd], axis=1).reshape(FB, SUB, LANES)
            fine[row, 1 : FB + 1] = jnp.where(lo, both, fine[row, 1 : FB + 1])

    for k in range(0, 4):
        raise_rows(s1, k + 1, pf1, (2 * k, 2 * k + 1), first_c + k - 1)
        seal(pf1, 2 * k, FB)
        seal(pf1, 2 * k + 1, FB)

    for idx in range(0, 6):
        def emit(lo_block, count, new):
            pf2[idx, pl.ds(1 + lo_block, count)] = new

        fine_gru(pf1, idx + 1, w_gru, in_grid(first_f + idx - 1, rows_f), emit)

    def head(step, ref, base):
        for t in range(4):
            lhs = jnp.concatenate(
                [ref[base : base + 4, 1 + 8 * t + k].reshape(4 * SUB, LANES) for k in range(8)], axis=-1
            )
            acc = jnp.dot(lhs, w_head[...], preferred_element_type=F32).astype(BF)
            out[step, :, :, t * LANES : (t + 1) * LANES] = acc.reshape(4, SUB, LANES)

    head(0, pf2, 1)

    raise_rows(s2, 0, pf2, (None, 0), first_c - 1)
    raise_rows(s2, 1, pf2, (1, 2), first_c)
    raise_rows(s2, 2, pf2, (3, 4), first_c + 1)
    raise_rows(s2, 3, pf2, (5, None), first_c + 2)
    for idx in range(6):
        seal(pf2, idx, FB)

    for idx in range(0, 4):
        def emit(lo_block, count, new):
            states[idx, pl.ds(1 + lo_block, count)] = new

        fine_gru(pf2, idx + 1, w_gru, True, emit)

    head(1, states, 0)


def to_upper(x):
    return jnp.concatenate([jnp.zeros(x.shape, F32), x.astype(F32)], axis=-1).astype(BF)


def to_lower(x):
    return jnp.concatenate([x.astype(F32), jnp.zeros(x.shape, F32)], axis=-1).astype(BF)


def fetch_all(given, copies, sems):
    fetches = [pltpu.make_async_copy(src, dst, sems.at[i]) for i, (src, dst) in enumerate(zip(given, copies))]
    for fetch in fetches:
        fetch.start()
    for fetch in fetches:
        fetch.wait()


def arrange_gru(kx, kh, w):
    for k in range(9):
        at = k * LANES
        w[at : at + C1, :LANES] = kx[k, :, :LANES]
        w[at : at + C1, LANES:] = to_upper(kx[k, :, LANES:])
        w[at + C1 : at + LANES, :LANES] = kh[k, :, :LANES]
        w[at + C1 : at + LANES, LANES:] = to_lower(kh[k, :, LANES:])


def prepare_encoder_body(*refs):
    given, (w_stem, w_enc, w_down), copies, sems = refs[:4], refs[4:7], refs[7:11], refs[11]
    fetch_all(given, copies, sems)
    stem, enc_x, enc_h, down = copies
    arrange_gru(enc_x, enc_h, w_enc)
    for k in range(9):
        at = k * LANES
        w_down[at : at + C1] = jnp.zeros((C1, 2 * LANES), BF)
        w_down[at + C1 : at + LANES, :LANES] = down[k, :, :LANES]
        w_down[at + C1 : at + LANES, LANES:] = to_lower(down[k, :, LANES:])
    w_stem[...] = jnp.zeros(w_stem.shape, BF)
    wide = to_lower(stem[...])
    for k in range(8):
        w_stem[k * PATCH : (k + 1) * PATCH, k * LANES : (k + 1) * LANES] = wide


def prepare_forecaster_body(*refs):
    given, (w_up, w_fc, w_head), copies, sems = refs[:4], refs[4:7], refs[7:11], refs[11]
    fetch_all(given, copies, sems)
    up, fc_x, fc_h, head = copies
    arrange_gru(fc_x, fc_h, w_fc)

    def tap(a, b):
        return jnp.zeros((C2, C1), F32) if a is None else up[3 * a + b].astype(F32).T

    none = (None, None)
    for g, taps in enumerate((
        ((1, 1), (1, 0), (0, 1), (0, 0)),
        (none, (1, 2), none, (0, 2)),
        (none, none, (2, 1), (2, 0)),
        (none, none, none, (2, 2)),
    )):
        for n in range(2):
            pair = jnp.concatenate([tap(*taps[2 * n]), tap(*taps[2 * n + 1])], axis=-1)
            w_up[g * C2 : (g + 1) * C2, n * LANES : (n + 1) * LANES] = pair.astype(BF)

    w_head[...] = jnp.zeros(w_head.shape, BF)
    tall = head[...].astype(F32).T.astype(BF)
    for k in range(8):
        w_head[k * LANES + C1 : (k + 1) * LANES, k * PATCH : (k + 1) * PATCH] = tall


def call(body, args, outs, scratch, aliases={}):
    return pl.pallas_call(
        body,
        out_shape=[s if isinstance(s, jax.ShapeDtypeStruct) else jax.ShapeDtypeStruct(s, BF) for s in outs],
        in_specs=[pl.BlockSpec(memory_space=space) for _, space in args],
        out_specs=[pl.BlockSpec(memory_space=pltpu.VMEM)] * len(outs),
        scratch_shapes=scratch,
        input_output_aliases=aliases,
        compiler_params=pltpu.CompilerParams(vmem_limit_bytes=24 * 1024 * 1024),
    )(*[arg for arg, _ in args])


def on_device(
    frames,
    start_fine,
    start_coarse,
    enc_stem,
    enc_fine_x,
    enc_fine_h,
    enc_down,
    enc_coarse_x,
    enc_coarse_h,
    fc_coarse_h,
    fc_up,
    fc_fine_x,
    fc_fine_h,
    fc_head,
):
    count = lax.axis_size(LINE)
    across = [(i, i + 1) for i in range(1, count - 1, 2)]
    across = across + [(b, a) for a, b in across]

    def outer_swap(x):
        return lax.ppermute(x, LINE, across)

    def inner_swap(x):
        return lax.ppermute(x, "section", [(0, 1), (1, 0)])

    fine = start_fine.reshape(4, SUB, FB * C1)
    patches = frames.reshape(FRAMES, 4, SUB, FB * PATCH)
    coarse = start_coarse.reshape(2, SUB, CB * C2)

    def on_chip(*values):
        return [(value, pltpu.VMEM) for value in values]

    def fine_buf(rows):
        return pltpu.VMEM((rows, FB + 2, SUB, LANES), BF)

    def coarse_buf(rows):
        return pltpu.VMEM((rows, CB + 2, SUB, 4 * LANES), BF)

    rows = (3, SUB, FB * (C1 + FRAMES * PATCH))
    own, to_outer, to_inner = call(pack_body, on_chip(fine, patches[0], patches[1]), [(4,) + rows[1:], rows, rows], [])
    outer, inner = outer_swap(to_outer), inner_swap(to_inner)

    acc_buf = pltpu.VMEM((CB * SUB, 5 * LANES), F32)
    flat = (9 * C2, 3 * C2)

    def prepare(body, values, outs):
        scratch = [pltpu.VMEM(value.shape, BF) for value in values]
        return call(
            body, [(value, pl.ANY) for value in values], outs, scratch + [pltpu.SemaphoreType.DMA((len(values),))]
        )

    kernel = (9, C1, 3 * C1)
    wide = (9 * LANES, 2 * LANES)
    w_stem, w_enc, w_down = prepare(
        prepare_encoder_body,
        [enc_stem, enc_fine_x.reshape(kernel), enc_fine_h.reshape(kernel), enc_down.reshape(kernel)],
        [(8 * PATCH, 8 * LANES), wide, wide],
    )
    w_up, w_fc, w_head = prepare(
        prepare_forecaster_body,
        [jnp.swapaxes(fc_up.reshape(9, C2, C1), 1, 2), fc_fine_x.reshape(kernel), fc_fine_h.reshape(kernel), fc_head.T],
        [(4 * C2, 2 * LANES), wide, (8 * LANES, 8 * PATCH)],
    )
    coarse_o, coarse_i = outer_swap(coarse), inner_swap(coarse)

    halo = (3 * ROW_TILES, SUB, LANES)
    edge = (2, FB // 2, SUB, LANES)

    def fine_shape(count, blocks=FB + 2):
        return (count, blocks, SUB, LANES)

    p1_own, stem2_own, inside = call(
        fine_own_body, on_chip(own, w_stem, w_enc), [fine_shape(4), fine_shape(4, FB), fine_shape(2)], []
    )
    state_f, low_own, to_outer, to_inner, state_fo, state_fi = call(
        fine_encoder_body,
        on_chip(p1_own, stem2_own, inside, outer, inner, w_stem, w_enc, w_down),
        [(4, FB // 2, SUB, LANES), (4 * ROW_TILES, SUB, LANES), halo, halo, edge, edge],
        [fine_buf(5), pltpu.VMEM(fine_shape(5, FB), BF), fine_buf(5), fine_buf(9)],
    )
    got_o, got_i = outer_swap(to_outer), inner_swap(to_inner)

    acc_first, h_first = call(
        coarse_state_body,
        on_chip(coarse, coarse_o, coarse_i, enc_coarse_h.reshape(flat)),
        [jax.ShapeDtypeStruct((4, CB * SUB, 5 * LANES), F32), (4, CB + 2, SUB, 4 * LANES)],
        [coarse_buf(6)],
    )
    state_fo, state_fi = outer_swap(state_fo), inner_swap(state_fi)

    w_x, w_h = enc_coarse_x.reshape(flat), enc_coarse_h.reshape(flat)
    four = (4, CB + 2, SUB, 4 * LANES)
    near, h1, x2 = call(
        coarse_encoder_body,
        on_chip(low_own, got_o, got_i, acc_first, h_first, w_x, w_h),
        [(ROW_TILES, SUB, LANES), four, four],
        [coarse_buf(6), acc_buf, acc_buf],
    )
    in_near = inner_swap(near)
    (far,) = call(coarse_rest_body, on_chip(h1, x2, w_x, w_h), [(ROW_TILES, SUB, LANES)], [acc_buf, acc_buf])
    in_far = inner_swap(far)
    state_co = outer_swap(jnp.concatenate([far, near, in_near], axis=0))
    third = inner_swap(state_co[:ROW_TILES])

    w_f = fc_coarse_h.reshape(flat)
    (s1,) = call(
        forecast_inner_body,
        on_chip(far, near, in_far, in_near, w_f),
        [(6, CB + 2, SUB, 4 * LANES)],
        [coarse_buf(4), acc_buf],
    )
    (s1,) = call(
        forecast_outer_body,
        on_chip(s1, far, near, state_co, w_f),
        [(6, CB + 2, SUB, 4 * LANES)],
        [coarse_buf(5), acc_buf],
        {0: 0},
    )
    out, _ = call(
        forecaster_body,
        on_chip(s1, in_far, in_near, third, state_f, state_fo, state_fi, w_f, w_up, w_fc, w_head),
        [(HORIZON, 4, SUB, FB * PATCH), (6, CB + 2, SUB, 4 * LANES)],
        [coarse_buf(3), coarse_buf(5), fine_buf(8), fine_buf(6), fine_buf(4), acc_buf],
        {0: 1},
    )
    return out.reshape(HORIZON, 4, COLS * PATCH)


def solution(mesh):
    line = ("groups", "tile", "section")
    return jax.shard_map(
        on_device,
        mesh=mesh,
        in_specs=(P(None, line, None), P(line, None), P(line, None)) + (P(),) * 11,
        out_specs=P(None, line, None),
        check_vma=False,
    )
```

```python
import jax
import jax.numpy as jnp
from jax import lax
from jax.experimental import pallas as pl
from jax.experimental.pallas import tpu as pltpu
from jax.sharding import PartitionSpec as P


C1 = 64
C2 = 192
PATCH = 16
FRAMES = 2
HORIZON = 2
COLS = 512
SUB = 16
FB = COLS // SUB
CB = COLS // 2 // SUB
LANES = 128
BF = jnp.bfloat16
F32 = jnp.float32
LINE = ("tile", "section")
PAIRS = CB // 2
ROW_TILES = 3 * PAIRS


def leaky(values):
    return jnp.where(values > 0, values, 0.2 * values)


def low_half(shape):
    return lax.broadcasted_iota(jnp.int32, shape, len(shape) - 1) < 64


def swap_halves(x):
    flat = x.reshape(-1, LANES)
    return pltpu.roll(flat, 64, 1).reshape(x.shape)


def swap_bf(x):
    return swap_halves(x.astype(F32)).astype(BF)


def sigmoid(x):
    return 0.5 * jnp.tanh(0.5 * x) + 0.5


def shift_sub(x, by):
    wide = x.astype(F32)
    row = lax.broadcasted_iota(jnp.int32, wide.shape, 0)
    if by > 0:
        moved = jnp.where(row == 0, 0.0, pltpu.roll(wide, 1, 0))
    else:
        moved = jnp.where(row == SUB - 1, 0.0, pltpu.roll(wide, SUB - 1, 0))
    return moved.astype(BF)


def seal(ref, idx, blocks):
    ref[idx, 0] = shift_sub(ref[idx, blocks], 1)
    ref[idx, blocks + 1] = shift_sub(ref[idx, 1], -1)


def row_of(src, idx):
    if isinstance(src, list):
        ref, at = src[idx]
        return ref.at[at]
    return src.at[idx]


def fine_patches(src, idx, lo, count):
    parts = [
        row_of(src, idx + dr)[pl.ds(lo + dj, count)].reshape(count * SUB, LANES)
        for dr in (-1, 0, 1)
        for dj in (0, 1, 2)
    ]
    return jnp.concatenate(parts, axis=-1)


def fine_gru(src, idx, weight, valid, emit):
    count = 16
    for lo in range(0, FB, count):
        acc = jnp.dot(fine_patches(src, idx, lo, count), weight[...], preferred_element_type=F32)
        gates = sigmoid(acc[:, :LANES])
        cand = acc[:, LANES:]
        cand = jnp.tanh(cand + swap_halves(gates * cand))
        old = row_of(src, idx)[pl.ds(1 + lo, count)].reshape(count * SUB, LANES).astype(F32)
        new = (1.0 - gates) * cand + gates * old
        new = jnp.where(valid, new, 0.0).astype(BF)
        emit(lo, count, new.reshape(count, SUB, LANES))


def down_row(src, idx, weight):
    parts = []
    for dr in (-1, 0, 1):
        row = row_of(src, idx + dr)[...].reshape(FB // 2 + 1, 2, SUB, LANES)
        for tap in (row[:CB, 0], row[:CB, 1], row[1:, 0]):
            parts.append(tap.reshape(CB * SUB, LANES))
    lhs = jnp.concatenate(parts, axis=-1)
    return jnp.dot(lhs, weight[...], preferred_element_type=F32)


def coarse_forms(t0, t1):
    lo = low_half(t0.shape)
    r0, r1 = swap_halves(t0), swap_halves(t1)
    return (
        t0.astype(BF),
        jnp.where(lo, t1, 0.0).astype(BF),
        jnp.where(lo, 0.0, r0).astype(BF),
        jnp.where(lo, r0, r1).astype(BF),
    )


def put_forms(ref, idx, forms):
    for k, tile in enumerate(forms):
        ref[idx, 1 : CB + 1, :, k * LANES : (k + 1) * LANES] = tile.reshape(CB, SUB, LANES)
    seal(ref, idx, CB)


def put_packed(ref, idx, tiles):
    t = [tiles(i).astype(F32) for i in range(3)]
    r = [swap_halves(x) for x in t]
    lo = low_half(t[0].shape)
    even = (t[0], jnp.where(lo, t[1], 0.0), jnp.where(lo, 0.0, r[0]), jnp.where(lo, r[0], r[1]))
    odd = (
        jnp.where(lo, r[1], r[2]),
        jnp.where(lo, r[2], 0.0),
        jnp.where(lo, 0.0, t[1]),
        t[2],
    )
    for k in range(4):
        both = jnp.stack([even[k].astype(BF), odd[k].astype(BF)], axis=1)
        ref[idx, 1 : CB + 1, :, k * LANES : (k + 1) * LANES] = both.reshape(CB, SUB, LANES)
    seal(ref, idx, CB)


def pack_forms(forms):
    f = [x.reshape(CB // 2, 2, SUB, LANES) for x in forms]
    lo = low_half((CB // 2, SUB, LANES))
    return (f[0][:, 0], jnp.where(lo, f[1][:, 0], f[2][:, 1]), f[3][:, 1])


def coarse_patches(ref, idx):
    def tile(dr, dj, k):
        return ref[idx + dr, dj : dj + CB, :, k * LANES : (k + 1) * LANES].reshape(CB * SUB, LANES)

    lo = low_half((CB * SUB, LANES))

    def aligned(dr):
        return [
            tile(dr, 0, 0),
            jnp.where(lo, tile(dr, 0, 1), tile(dr, 1, 2)),
            tile(dr, 1, 3),
            tile(dr, 2, 0),
        ]

    parts = aligned(-1)
    parts.append(jnp.where(lo, tile(-1, 2, 1), tile(0, 0, 2)))
    parts += [tile(0, 0, 3), tile(0, 1, 0), jnp.where(lo, tile(0, 1, 1), tile(0, 2, 2)), tile(0, 2, 3)]
    parts += aligned(1)
    parts.append(tile(1, 2, 1))
    return jnp.concatenate(parts, axis=-1)[:, : 9 * C2]


def coarse_gru(x_ref, x_idx, h_ref, h_idx, w_x, w_h, acc_x, acc_h, valid):
    width = 3 * C2
    if w_h is not None:
        acc_h[:, :width] = jnp.dot(coarse_patches(h_ref, h_idx), w_h[...], preferred_element_type=F32)
    if x_ref is not None:
        acc_x[:, :width] = jnp.dot(coarse_patches(x_ref, x_idx), w_x[...], preferred_element_type=F32)

    def part(ref, k):
        return ref[:, k * LANES : (k + 1) * LANES]

    gates = []
    for k in range(3):
        mixed = part(acc_h, k)
        if x_ref is not None:
            mixed = part(acc_x, k) + mixed
        gates.append(sigmoid(mixed))
    lo = low_half(gates[0].shape)
    g1, g2 = swap_halves(gates[1]), swap_halves(gates[2])
    update = (jnp.where(lo, g1, g2), g2)
    out = []
    for k in range(2):
        cand = gates[k] * part(acc_h, 3 + k)
        if x_ref is not None:
            cand = part(acc_x, 3 + k) + cand
        cand = jnp.tanh(cand)
        old = h_ref[h_idx, 1 : CB + 1, :, k * LANES : (k + 1) * LANES].reshape(CB * SUB, LANES).astype(F32)
        new = (1.0 - update[k]) * cand + update[k] * old
        out.append(jnp.where(valid, new, 0.0).astype(BF).astype(F32))
    return coarse_forms(out[0], out[1])


def place(per_device):
    upper = lax.axis_index("section") == 0
    line = lax.axis_index("tile") * lax.axis_size("section") + lax.axis_index("section")
    return upper, line * per_device, lax.axis_size(LINE) * per_device


def in_grid(row, rows):
    return jnp.logical_and(row >= 0, row < rows)


def pack_body(fine, first, second, own, to_outer, to_inner):
    upper, _, _ = place(4)
    for r in range(4):
        own[r, :, : FB * C1] = fine[r]
        own[r, :, FB * C1 : FB * (C1 + PATCH)] = first[r]
        own[r, :, FB * (C1 + PATCH) :] = second[r]
    for r in range(3):
        to_outer[r] = jnp.where(upper, own[r], own[r + 1])
        to_inner[r] = jnp.where(upper, own[r + 1], own[r])


def fill_fine(get, count, w_stem, p1, stem2):
    lo = low_half((SUB, LANES))
    for frame in range(FRAMES):
        for t in range(4):
            at = FB * C1 + frame * FB * PATCH + t * LANES
            patches = jnp.concatenate([get(r, slice(at, at + LANES)) for r in range(count)], axis=0)
            for half in range(2):
                acc = jnp.dot(patches, w_stem[:, half * 512 : half * 512 + 512], preferred_element_type=F32)
                acc = leaky(acc).astype(BF)
                for k in range(4):
                    block = acc[:, k * LANES : (k + 1) * LANES].reshape(count, SUB, LANES)
                    at_block = 8 * t + 4 * half + k
                    if frame == 0:
                        p1[:, 1 + at_block] = block
                    else:
                        stem2[:, at_block] = block
    for r in range(count):
        for k in range(FB // 2):
            pair = get(r, slice(k * LANES, (k + 1) * LANES))
            p1[r, 1 + 2 * k] = jnp.where(lo, p1[r, 1 + 2 * k], swap_bf(pair))
            p1[r, 2 + 2 * k] = jnp.where(lo, p1[r, 2 + 2 * k], pair)
        seal(p1, r, FB)


def first_fine(src, idx, w_gru, valid, stems, dst, at):
    lo = low_half((1, SUB, LANES))

    def emit(lo_block, count, new):
        dst[at, pl.ds(1 + lo_block, count)] = jnp.where(lo, stems[pl.ds(lo_block, count)], new)

    fine_gru(src, idx, w_gru, valid, emit)
    seal(dst, at, FB)


def fine_own_body(own, w_stem, w_gru, p1, stem2, inside):
    fill_fine(lambda r, lanes: own[r, :, lanes], 4, w_stem, p1, stem2)
    for r in range(2):
        first_fine(p1, 1 + r, w_gru, True, stem2.at[1 + r], inside, r)


def fine_encoder_body(
    p1_own, stem2_own, inside, outer, inner, w_stem, w_gru, w_down,
    state_out, low_own, to_outer, to_inner, second_outer, second_inner, state_outer, state_inner,
    p1_halo, stem2_halo, p2_rest, p3,
):
    upper, first, rows = place(4)
    lo = low_half((1, SUB, LANES))

    def get(r, lanes):
        above = r < 3
        at = r if above else r - 3
        a, b = outer[at, :, lanes], inner[at, :, lanes]
        return jnp.where(upper, a, b) if above else jnp.where(upper, b, a)

    fill_fine(get, 5, w_stem, p1_halo, stem2_halo)
    p1 = [(p1_halo, r) for r in range(3)] + [(p1_own, r) for r in range(4)] + [(p1_halo, r) for r in (3, 4)]
    stem2 = [(stem2_halo, r) for r in range(3)] + [(stem2_own, r) for r in range(4)] + [(stem2_halo, 3)]
    p2 = [None] + [(p2_rest, r) for r in range(3)] + [(inside, 0), (inside, 1), (p2_rest, 3), (p2_rest, 4)]
    for idx in (1, 2, 3, 6, 7):
        dst, at = p2[idx]
        first_fine(p1, idx, w_gru, in_grid(first + idx - 3, rows), row_of(stem2, idx), dst, at)

    for idx in range(2, 7):
        def emit(lo_block, count, new):
            p3[idx, pl.ds(1 + lo_block, count)] = jnp.where(lo, jnp.zeros_like(new), new)

        fine_gru(p2, idx, w_gru, in_grid(first + idx - 3, rows), emit)
        seal(p3, idx, FB)

    def lowered(src, p):
        acc = leaky(down_row(src, 3 + 2 * p, w_down)).astype(BF).astype(F32)
        return pack_forms(coarse_forms(acc[:, :LANES], acc[:, LANES:]))

    def put(ref, at, tiles):
        for k, tile in enumerate(tiles):
            base = at * ROW_TILES + k * PAIRS
            ref[base : base + PAIRS] = tile

    for p in range(2):
        tiles = lowered(p2, p)
        put(low_own, p, tiles)
        put(to_outer, p, tiles)
        put(to_inner, p, tiles)
    for p in range(2):
        tiles = lowered(p3, p)
        put(low_own, 2 + p, tiles)
        outward = upper if p == 0 else jnp.logical_not(upper)

        @pl.when(outward)
        def _():
            put(second_outer, 0, tiles)

        @pl.when(jnp.logical_not(outward))
        def _():
            put(second_inner, 0, tiles)

    for r in range(4):
        for k in range(FB // 2):
            state_out[r, k] = jnp.where(lo[0], swap_bf(p3[3 + r, 1 + 2 * k]), p3[3 + r, 2 + 2 * k])
    for top, ref in ((upper, state_outer), (jnp.logical_not(upper), state_inner)):
        start = jnp.where(top, 0, 2)
        for r in range(2):
            ref[r] = state_out[start + r]


def zero_tail(acc):
    acc[:, 4 * LANES :] = jnp.zeros((CB * SUB, LANES), F32)


def packed_tiles(ref, at):
    return lambda i: ref[at * ROW_TILES + i * PAIRS : at * ROW_TILES + (i + 1) * PAIRS]


def raw_tiles(get):
    def tiles(i):
        return jnp.stack([get(slice((3 * k + i) * LANES, (3 * k + i + 1) * LANES)) for k in range(PAIRS)])

    return tiles


def coarse_state_body(own, outer, inner, w_h, acc_out, h_out, h0):
    upper, _, _ = place(2)
    for idx in range(6):
        if 2 <= idx < 4:
            put_packed(h0, idx, raw_tiles(lambda lanes: own[idx - 2, :, lanes]))
            continue
        r = idx if idx < 2 else idx - 4
        a, b = (outer, inner) if idx < 2 else (inner, outer)
        put_packed(h0, idx, raw_tiles(lambda lanes: jnp.where(upper, a[r, :, lanes], b[r, :, lanes])))

    for idx in range(0, 4):
        acc_out[idx, :, : 3 * C2] = jnp.dot(coarse_patches(h0, idx + 1), w_h[...], preferred_element_type=F32)
        acc_out[idx, :, 4 * LANES + C1 :] = jnp.zeros((CB * SUB, C1), F32)
        h_out[idx] = h0[idx + 1]


def put_row(ref, forms):
    for k, tile in enumerate(pack_forms(forms)):
        ref[k * PAIRS : (k + 1) * PAIRS] = tile


def coarse_encoder_body(low_own, low_outer, low_inner, acc_first, h_first, w_x, h1, x1, acc_x):
    upper, first, rows = place(2)
    zero_tail(acc_x)
    for idx in range(6):
        if 2 <= idx < 4:
            put_packed(x1, idx, packed_tiles(low_own, idx - 2))
            continue
        r = idx if idx < 2 else idx - 4
        a, b = (low_outer, low_inner) if idx < 2 else (low_inner, low_outer)
        put_packed(x1, idx, either(upper, a, r, b, r))
    for idx in range(4):
        forms = coarse_gru(
            x1, idx + 1, h_first, idx, w_x, None, acc_x, acc_first.at[idx], in_grid(first + idx - 1, rows)
        )
        put_forms(h1, idx, forms)


def coarse_near_body(low_own, second_outer, second_inner, h1, w_x, w_h, near, x2, acc_x, acc_h):
    upper, _, _ = place(2)
    zero_tail(acc_x)
    zero_tail(acc_h)
    put_packed(x2, 0, either(upper, second_outer, 0, second_inner, 0))
    put_packed(x2, 1, packed_tiles(low_own, 2))
    put_packed(x2, 2, packed_tiles(low_own, 3))
    put_packed(x2, 3, either(upper, second_inner, 0, second_outer, 0))
    idx = jnp.where(upper, 1, 0)
    put_row(near, coarse_gru(x2, idx + 1, h1, idx + 1, w_x, w_h, acc_x, acc_h, True))


def coarse_rest_body(h1, x2, w_x, w_h, far, acc_x, acc_h):
    upper, _, _ = place(2)
    zero_tail(acc_x)
    zero_tail(acc_h)
    idx = jnp.where(upper, 0, 1)
    put_row(far, coarse_gru(x2, idx + 1, h1, idx + 1, w_x, w_h, acc_x, acc_h, True))


def raise_pair(src, idx, weight):
    def tile(dr, dj, k):
        return src[idx + dr, 1 + dj : 1 + dj + CB, :, k * LANES : (k + 1) * LANES].reshape(CB * SUB, LANES)

    lo = low_half((CB * SUB, LANES))
    parts = []
    for dr in (0, 1):
        parts += [tile(dr, 0, 0), jnp.where(lo, tile(dr, 0, 1), tile(dr, 1, 2)), tile(dr, 1, 3)]
    return jnp.dot(jnp.concatenate(parts, axis=-1), weight[...], preferred_element_type=F32)


def either(upper, a, i, b, j):
    return lambda t: jnp.where(upper, packed_tiles(a, i)(t), packed_tiles(b, j)(t))


def forecast_inner_body(far, near, in_far, in_near, w_h, s1, h2, acc_h):
    upper, first, rows = place(2)
    zero_tail(acc_h)
    put_packed(h2, 0, either(upper, far, 0, in_far, 0))
    put_packed(h2, 1, either(upper, near, 0, in_near, 0))
    put_packed(h2, 2, either(upper, in_near, 0, near, 0))
    put_packed(h2, 3, either(upper, in_far, 0, far, 0))
    at = jnp.where(upper, 3, 1)
    for k in range(2):
        forms = coarse_gru(None, 0, h2, k + 1, None, w_h, None, acc_h, in_grid(first + at + k - 2, rows))
        put_forms(s1, at + k, forms)


def forecast_outer_body(s1_given, far, near, outer, w_h, s1, h2, acc_h):
    upper, first, rows = place(2)
    zero_tail(acc_h)
    put_packed(h2, 0, either(upper, outer, 2, near, 0))
    put_packed(h2, 1, either(upper, outer, 1, far, 0))
    put_packed(h2, 2, packed_tiles(outer, 0))
    put_packed(h2, 3, either(upper, far, 0, outer, 1))
    put_packed(h2, 4, either(upper, near, 0, outer, 2))
    at = jnp.where(upper, 0, 3)
    for k in range(3):
        forms = coarse_gru(None, 0, h2, k + 1, None, w_h, None, acc_h, in_grid(first + at + k - 2, rows))
        put_forms(s1, at + k, forms)


def forecaster_body(
    s1_given, in_far, in_near, third, f_own, f_outer, f_inner, w_h, w_up, w_gru, w_head,
    out, s1, h2, s2, pf1, pf2, states, acc_h,
):
    upper, first_c, rows_c = place(2)
    _, first_f, rows_f = place(4)
    lo = low_half((1, SUB, LANES))
    zero_tail(acc_h)

    put_packed(h2, 0, either(upper, in_near, 0, third, 0))
    put_packed(h2, 1, packed_tiles(in_far, 0))
    put_packed(h2, 2, either(upper, third, 0, in_near, 0))
    last = jnp.where(upper, 5, 0)
    put_forms(
        s1, last, coarse_gru(None, 0, h2, 1, None, w_h, None, acc_h, in_grid(first_c + last - 2, rows_c))
    )

    for idx in range(8):
        for k in range(FB // 2):
            if 2 <= idx < 6:
                pair = f_own[idx - 2, k]
            elif idx < 2:
                pair = jnp.where(upper, f_outer[idx, k], f_inner[idx, k])
            else:
                pair = jnp.where(upper, f_inner[idx - 6, k], f_outer[idx - 6, k])
            pf1[idx, 1 + 2 * k] = swap_bf(pair)
            pf1[idx, 2 + 2 * k] = pair

    for idx in range(0, 4):
        forms = coarse_gru(None, 0, s1, idx + 1, None, w_h, None, acc_h, in_grid(first_c + idx - 1, rows_c))
        put_forms(s2, idx, forms)

    s2[4] = jnp.zeros(s2.shape[1:], BF)

    def raise_rows(src, idx, fine, at, coarse_row):
        acc = raise_pair(src, idx, w_up)
        acc = jnp.where(in_grid(coarse_row, rows_c), leaky(acc), 0.0)
        for half, row in enumerate(at):
            if row is None:
                continue
            tile = acc[:, half * LANES : (half + 1) * LANES]
            even = tile.astype(BF).reshape(CB, SUB, LANES)
            odd = swap_halves(tile).astype(BF).reshape(CB, SUB, LANES)
            both = jnp.stack([even, odd], axis=1).reshape(FB, SUB, LANES)
            fine[row, 1 : FB + 1] = jnp.where(lo, both, fine[row, 1 : FB + 1])

    for k in range(0, 4):
        raise_rows(s1, k + 1, pf1, (2 * k, 2 * k + 1), first_c + k - 1)
        seal(pf1, 2 * k, FB)
        seal(pf1, 2 * k + 1, FB)

    for idx in range(0, 6):
        def emit(lo_block, count, new):
            pf2[idx, pl.ds(1 + lo_block, count)] = new

        fine_gru(pf1, idx + 1, w_gru, in_grid(first_f + idx - 1, rows_f), emit)

    def head(step, ref, base):
        for t in range(4):
            lhs = jnp.concatenate(
                [ref[base : base + 4, 1 + 8 * t + k].reshape(4 * SUB, LANES) for k in range(8)], axis=-1
            )
            acc = jnp.dot(lhs, w_head[...], preferred_element_type=F32).astype(BF)
            out[step, :, :, t * LANES : (t + 1) * LANES] = acc.reshape(4, SUB, LANES)

    head(0, pf2, 1)

    raise_rows(s2, 0, pf2, (None, 0), first_c - 1)
    raise_rows(s2, 1, pf2, (1, 2), first_c)
    raise_rows(s2, 2, pf2, (3, 4), first_c + 1)
    raise_rows(s2, 3, pf2, (5, None), first_c + 2)
    for idx in range(6):
        seal(pf2, idx, FB)

    for idx in range(0, 4):
        def emit(lo_block, count, new):
            states[idx, pl.ds(1 + lo_block, count)] = new

        fine_gru(pf2, idx + 1, w_gru, True, emit)

    head(1, states, 0)


def to_upper(x):
    return jnp.concatenate([jnp.zeros(x.shape, F32), x.astype(F32)], axis=-1).astype(BF)


def to_lower(x):
    return jnp.concatenate([x.astype(F32), jnp.zeros(x.shape, F32)], axis=-1).astype(BF)


def fetch_all(given, copies, sems):
    fetches = [pltpu.make_async_copy(src, dst, sems.at[i]) for i, (src, dst) in enumerate(zip(given, copies))]
    for fetch in fetches:
        fetch.start()
    for fetch in fetches:
        fetch.wait()


def arrange_gru(kx, kh, w):
    for k in range(9):
        at = k * LANES
        w[at : at + C1, :LANES] = kx[k, :, :LANES]
        w[at : at + C1, LANES:] = to_upper(kx[k, :, LANES:])
        w[at + C1 : at + LANES, :LANES] = kh[k, :, :LANES]
        w[at + C1 : at + LANES, LANES:] = to_lower(kh[k, :, LANES:])


def prepare_encoder_body(*refs):
    given, (w_stem, w_enc, w_down), copies, sems = refs[:4], refs[4:7], refs[7:11], refs[11]
    fetch_all(given, copies, sems)
    stem, enc_x, enc_h, down = copies
    arrange_gru(enc_x, enc_h, w_enc)
    for k in range(9):
        at = k * LANES
        w_down[at : at + C1] = jnp.zeros((C1, 2 * LANES), BF)
        w_down[at + C1 : at + LANES, :LANES] = down[k, :, :LANES]
        w_down[at + C1 : at + LANES, LANES:] = to_lower(down[k, :, LANES:])
    w_stem[...] = jnp.zeros(w_stem.shape, BF)
    wide = to_lower(stem[...])
    for k in range(8):
        w_stem[k * PATCH : (k + 1) * PATCH, k * LANES : (k + 1) * LANES] = wide


def prepare_forecaster_body(*refs):
    given, (w_up, w_fc, w_head), copies, sems = refs[:4], refs[4:7], refs[7:11], refs[11]
    fetch_all(given, copies, sems)
    up, fc_x, fc_h, head = copies
    arrange_gru(fc_x, fc_h, w_fc)

    def tap(a, b):
        return jnp.zeros((C2, C1), F32) if a is None else up[3 * a + b].astype(F32).T

    none = (None, None)
    for g, taps in enumerate((
        ((1, 1), (1, 0), (0, 1), (0, 0)),
        (none, (1, 2), none, (0, 2)),
        (none, none, (2, 1), (2, 0)),
        (none, none, none, (2, 2)),
    )):
        for n in range(2):
            pair = jnp.concatenate([tap(*taps[2 * n]), tap(*taps[2 * n + 1])], axis=-1)
            w_up[g * C2 : (g + 1) * C2, n * LANES : (n + 1) * LANES] = pair.astype(BF)

    w_head[...] = jnp.zeros(w_head.shape, BF)
    tall = head[...].astype(F32).T.astype(BF)
    for k in range(8):
        w_head[k * LANES + C1 : (k + 1) * LANES, k * PATCH : (k + 1) * PATCH] = tall


def call(body, args, outs, scratch, aliases={}):
    return pl.pallas_call(
        body,
        out_shape=[s if isinstance(s, jax.ShapeDtypeStruct) else jax.ShapeDtypeStruct(s, BF) for s in outs],
        in_specs=[pl.BlockSpec(memory_space=space) for _, space in args],
        out_specs=[pl.BlockSpec(memory_space=pltpu.VMEM)] * len(outs),
        scratch_shapes=scratch,
        input_output_aliases=aliases,
        compiler_params=pltpu.CompilerParams(vmem_limit_bytes=24 * 1024 * 1024),
    )(*[arg for arg, _ in args])


def on_device(
    frames,
    start_fine,
    start_coarse,
    enc_stem,
    enc_fine_x,
    enc_fine_h,
    enc_down,
    enc_coarse_x,
    enc_coarse_h,
    fc_coarse_h,
    fc_up,
    fc_fine_x,
    fc_fine_h,
    fc_head,
):
    count = lax.axis_size(LINE)
    across = [(i, i + 1) for i in range(1, count - 1, 2)]
    across = across + [(b, a) for a, b in across]

    def outer_swap(x):
        return lax.ppermute(x, LINE, across)

    def inner_swap(x):
        return lax.ppermute(x, "section", [(0, 1), (1, 0)])

    fine = start_fine.reshape(4, SUB, FB * C1)
    patches = frames.reshape(FRAMES, 4, SUB, FB * PATCH)
    coarse = start_coarse.reshape(2, SUB, CB * C2)

    def on_chip(*values):
        return [(value, pltpu.VMEM) for value in values]

    def fine_buf(rows):
        return pltpu.VMEM((rows, FB + 2, SUB, LANES), BF)

    def coarse_buf(rows):
        return pltpu.VMEM((rows, CB + 2, SUB, 4 * LANES), BF)

    rows = (3, SUB, FB * (C1 + FRAMES * PATCH))
    own, to_outer, to_inner = call(pack_body, on_chip(fine, patches[0], patches[1]), [(4,) + rows[1:], rows, rows], [])
    outer, inner = outer_swap(to_outer), inner_swap(to_inner)

    acc_buf = pltpu.VMEM((CB * SUB, 5 * LANES), F32)
    flat = (9 * C2, 3 * C2)

    def prepare(body, values, outs):
        scratch = [pltpu.VMEM(value.shape, BF) for value in values]
        return call(
            body, [(value, pl.ANY) for value in values], outs, scratch + [pltpu.SemaphoreType.DMA((len(values),))]
        )

    kernel = (9, C1, 3 * C1)
    wide = (9 * LANES, 2 * LANES)
    w_stem, w_enc, w_down = prepare(
        prepare_encoder_body,
        [enc_stem, enc_fine_x.reshape(kernel), enc_fine_h.reshape(kernel), enc_down.reshape(kernel)],
        [(8 * PATCH, 8 * LANES), wide, wide],
    )
    w_up, w_fc, w_head = prepare(
        prepare_forecaster_body,
        [jnp.swapaxes(fc_up.reshape(9, C2, C1), 1, 2), fc_fine_x.reshape(kernel), fc_fine_h.reshape(kernel), fc_head.T],
        [(4 * C2, 2 * LANES), wide, (8 * LANES, 8 * PATCH)],
    )
    coarse_o, coarse_i = outer_swap(coarse), inner_swap(coarse)

    halo = (2 * ROW_TILES, SUB, LANES)
    row = (ROW_TILES, SUB, LANES)
    edge = (2, FB // 2, SUB, LANES)

    def fine_shape(count, blocks=FB + 2):
        return (count, blocks, SUB, LANES)

    p1_own, stem2_own, inside = call(
        fine_own_body, on_chip(own, w_stem, w_enc), [fine_shape(4), fine_shape(4, FB), fine_shape(2)], []
    )
    state_f, low_own, to_outer, to_inner, second_o, second_i, state_fo, state_fi = call(
        fine_encoder_body,
        on_chip(p1_own, stem2_own, inside, outer, inner, w_stem, w_enc, w_down),
        [(4, FB // 2, SUB, LANES), (4 * ROW_TILES, SUB, LANES), halo, halo, row, row, edge, edge],
        [fine_buf(5), pltpu.VMEM(fine_shape(5, FB), BF), fine_buf(5), fine_buf(9)],
    )
    got_o, got_i = outer_swap(to_outer), inner_swap(to_inner)
    second_o, second_i = outer_swap(second_o), inner_swap(second_i)

    acc_first, h_first = call(
        coarse_state_body,
        on_chip(coarse, coarse_o, coarse_i, enc_coarse_h.reshape(flat)),
        [jax.ShapeDtypeStruct((4, CB * SUB, 5 * LANES), F32), (4, CB + 2, SUB, 4 * LANES)],
        [coarse_buf(6)],
    )
    state_fo, state_fi = outer_swap(state_fo), inner_swap(state_fi)

    w_x, w_h = enc_coarse_x.reshape(flat), enc_coarse_h.reshape(flat)
    four = (4, CB + 2, SUB, 4 * LANES)
    (h1,) = call(
        coarse_encoder_body, on_chip(low_own, got_o, got_i, acc_first, h_first, w_x), [four], [coarse_buf(6), acc_buf]
    )
    near, x2 = call(
        coarse_near_body, on_chip(low_own, second_o, second_i, h1, w_x, w_h), [row, four], [acc_buf, acc_buf]
    )
    in_near = inner_swap(near)
    (far,) = call(coarse_rest_body, on_chip(h1, x2, w_x, w_h), [(ROW_TILES, SUB, LANES)], [acc_buf, acc_buf])
    in_far = inner_swap(far)
    state_co = outer_swap(jnp.concatenate([far, near, in_near], axis=0))
    third = inner_swap(state_co[:ROW_TILES])

    w_f = fc_coarse_h.reshape(flat)
    (s1,) = call(
        forecast_inner_body,
        on_chip(far, near, in_far, in_near, w_f),
        [(6, CB + 2, SUB, 4 * LANES)],
        [coarse_buf(4), acc_buf],
    )
    (s1,) = call(
        forecast_outer_body,
        on_chip(s1, far, near, state_co, w_f),
        [(6, CB + 2, SUB, 4 * LANES)],
        [coarse_buf(5), acc_buf],
        {0: 0},
    )
    out, _ = call(
        forecaster_body,
        on_chip(s1, in_far, in_near, third, state_f, state_fo, state_fi, w_f, w_up, w_fc, w_head),
        [(HORIZON, 4, SUB, FB * PATCH), (6, CB + 2, SUB, 4 * LANES)],
        [coarse_buf(3), coarse_buf(5), fine_buf(8), fine_buf(6), fine_buf(4), acc_buf],
        {0: 1},
    )
    return out.reshape(HORIZON, 4, COLS * PATCH)


def solution(mesh):
    line = ("groups", "tile", "section")
    return jax.shard_map(
        on_device,
        mesh=mesh,
        in_specs=(P(None, line, None), P(line, None), P(line, None)) + (P(),) * 11,
        out_specs=P(None, line, None),
        check_vma=False,
    )
```

```python
import jax
import jax.numpy as jnp
from jax import lax
from jax.experimental import pallas as pl
from jax.experimental.pallas import tpu as pltpu
from jax.sharding import PartitionSpec as P


C1 = 64
C2 = 192
PATCH = 16
FRAMES = 2
HORIZON = 2
COLS = 512
SUB = 16
FB = COLS // SUB
CB = COLS // 2 // SUB
LANES = 128
BF = jnp.bfloat16
F32 = jnp.float32
LINE = ("tile", "section")
PAIRS = CB // 2
ROW_TILES = 3 * PAIRS


def leaky(values):
    return jnp.where(values > 0, values, 0.2 * values)


def low_half(shape):
    return lax.broadcasted_iota(jnp.int32, shape, len(shape) - 1) < 64


def swap_halves(x):
    flat = x.reshape(-1, LANES)
    return pltpu.roll(flat, 64, 1).reshape(x.shape)


def swap_bf(x):
    return swap_halves(x.astype(F32)).astype(BF)


def sigmoid(x):
    return 0.5 * jnp.tanh(0.5 * x) + 0.5


def shift_sub(x, by):
    wide = x.astype(F32)
    row = lax.broadcasted_iota(jnp.int32, wide.shape, 0)
    if by > 0:
        moved = jnp.where(row == 0, 0.0, pltpu.roll(wide, 1, 0))
    else:
        moved = jnp.where(row == SUB - 1, 0.0, pltpu.roll(wide, SUB - 1, 0))
    return moved.astype(BF)


def seal(ref, idx, blocks):
    ref[idx, 0] = shift_sub(ref[idx, blocks], 1)
    ref[idx, blocks + 1] = shift_sub(ref[idx, 1], -1)


def row_of(src, idx):
    if isinstance(src, list):
        ref, at = src[idx]
        return ref.at[at]
    return src.at[idx]


def fine_patches(src, idx, lo, count):
    parts = [
        row_of(src, idx + dr)[pl.ds(lo + dj, count)].reshape(count * SUB, LANES)
        for dr in (-1, 0, 1)
        for dj in (0, 1, 2)
    ]
    return jnp.concatenate(parts, axis=-1)


def fine_gru(src, idx, weight, valid, emit):
    count = 16
    for lo in range(0, FB, count):
        acc = jnp.dot(fine_patches(src, idx, lo, count), weight[...], preferred_element_type=F32)
        gates = sigmoid(acc[:, :LANES])
        cand = acc[:, LANES:]
        cand = jnp.tanh(cand + swap_halves(gates * cand))
        old = row_of(src, idx)[pl.ds(1 + lo, count)].reshape(count * SUB, LANES).astype(F32)
        new = (1.0 - gates) * cand + gates * old
        new = jnp.where(valid, new, 0.0).astype(BF)
        emit(lo, count, new.reshape(count, SUB, LANES))


def down_row(src, idx, weight):
    parts = []
    for dr in (-1, 0, 1):
        row = row_of(src, idx + dr)[...].reshape(FB // 2 + 1, 2, SUB, LANES)
        for tap in (row[:CB, 0], row[:CB, 1], row[1:, 0]):
            parts.append(tap.reshape(CB * SUB, LANES))
    lhs = jnp.concatenate(parts, axis=-1)
    return jnp.dot(lhs, weight[...], preferred_element_type=F32)


def coarse_forms(t0, t1):
    lo = low_half(t0.shape)
    r0, r1 = swap_halves(t0), swap_halves(t1)
    return (
        t0.astype(BF),
        jnp.where(lo, t1, 0.0).astype(BF),
        jnp.where(lo, 0.0, r0).astype(BF),
        jnp.where(lo, r0, r1).astype(BF),
    )


def put_forms(ref, idx, forms):
    for k, tile in enumerate(forms):
        ref[idx, 1 : CB + 1, :, k * LANES : (k + 1) * LANES] = tile.reshape(CB, SUB, LANES)
    seal(ref, idx, CB)


def put_packed(ref, idx, tiles):
    t = [tiles(i).astype(F32) for i in range(3)]
    r = [swap_halves(x) for x in t]
    lo = low_half(t[0].shape)
    even = (t[0], jnp.where(lo, t[1], 0.0), jnp.where(lo, 0.0, r[0]), jnp.where(lo, r[0], r[1]))
    odd = (
        jnp.where(lo, r[1], r[2]),
        jnp.where(lo, r[2], 0.0),
        jnp.where(lo, 0.0, t[1]),
        t[2],
    )
    for k in range(4):
        both = jnp.stack([even[k].astype(BF), odd[k].astype(BF)], axis=1)
        ref[idx, 1 : CB + 1, :, k * LANES : (k + 1) * LANES] = both.reshape(CB, SUB, LANES)
    seal(ref, idx, CB)


def pack_forms(forms):
    f = [x.reshape(CB // 2, 2, SUB, LANES) for x in forms]
    lo = low_half((CB // 2, SUB, LANES))
    return (f[0][:, 0], jnp.where(lo, f[1][:, 0], f[2][:, 1]), f[3][:, 1])


def coarse_patches(ref, idx):
    def tile(dr, dj, k):
        return ref[idx + dr, dj : dj + CB, :, k * LANES : (k + 1) * LANES].reshape(CB * SUB, LANES)

    lo = low_half((CB * SUB, LANES))

    def aligned(dr):
        return [
            tile(dr, 0, 0),
            jnp.where(lo, tile(dr, 0, 1), tile(dr, 1, 2)),
            tile(dr, 1, 3),
            tile(dr, 2, 0),
        ]

    parts = aligned(-1)
    parts.append(jnp.where(lo, tile(-1, 2, 1), tile(0, 0, 2)))
    parts += [tile(0, 0, 3), tile(0, 1, 0), jnp.where(lo, tile(0, 1, 1), tile(0, 2, 2)), tile(0, 2, 3)]
    parts += aligned(1)
    parts.append(tile(1, 2, 1))
    return jnp.concatenate(parts, axis=-1)[:, : 9 * C2]


def coarse_gru(x_ref, x_idx, h_ref, h_idx, w_x, w_h, acc_x, acc_h, valid):
    width = 3 * C2
    if w_h is not None:
        acc_h[:, :width] = jnp.dot(coarse_patches(h_ref, h_idx), w_h[...], preferred_element_type=F32)
    if x_ref is not None:
        acc_x[:, :width] = jnp.dot(coarse_patches(x_ref, x_idx), w_x[...], preferred_element_type=F32)

    def part(ref, k):
        return ref[:, k * LANES : (k + 1) * LANES]

    gates = []
    for k in range(3):
        mixed = part(acc_h, k)
        if x_ref is not None:
            mixed = part(acc_x, k) + mixed
        gates.append(sigmoid(mixed))
    lo = low_half(gates[0].shape)
    g1, g2 = swap_halves(gates[1]), swap_halves(gates[2])
    update = (jnp.where(lo, g1, g2), g2)
    out = []
    for k in range(2):
        cand = gates[k] * part(acc_h, 3 + k)
        if x_ref is not None:
            cand = part(acc_x, 3 + k) + cand
        cand = jnp.tanh(cand)
        old = h_ref[h_idx, 1 : CB + 1, :, k * LANES : (k + 1) * LANES].reshape(CB * SUB, LANES).astype(F32)
        new = (1.0 - update[k]) * cand + update[k] * old
        out.append(jnp.where(valid, new, 0.0).astype(BF).astype(F32))
    return coarse_forms(out[0], out[1])


def place(per_device):
    upper = lax.axis_index("section") == 0
    line = lax.axis_index("tile") * lax.axis_size("section") + lax.axis_index("section")
    return upper, line * per_device, lax.axis_size(LINE) * per_device


def in_grid(row, rows):
    return jnp.logical_and(row >= 0, row < rows)


def pack_body(fine, first, second, own, to_outer, to_inner):
    upper, _, _ = place(4)
    for r in range(4):
        own[r, :, : FB * C1] = fine[r]
        own[r, :, FB * C1 : FB * (C1 + PATCH)] = first[r]
        own[r, :, FB * (C1 + PATCH) :] = second[r]
    for r in range(3):
        to_outer[r] = jnp.where(upper, own[r], own[r + 1])
        to_inner[r] = jnp.where(upper, own[r + 1], own[r])


def fill_fine(get, count, w_stem, p1, stem2):
    lo = low_half((SUB, LANES))
    for frame in range(FRAMES):
        for t in range(4):
            at = FB * C1 + frame * FB * PATCH + t * LANES
            patches = jnp.concatenate([get(r, slice(at, at + LANES)) for r in range(count)], axis=0)
            for half in range(2):
                acc = jnp.dot(patches, w_stem[:, half * 512 : half * 512 + 512], preferred_element_type=F32)
                acc = leaky(acc).astype(BF)
                for k in range(4):
                    block = acc[:, k * LANES : (k + 1) * LANES].reshape(count, SUB, LANES)
                    at_block = 8 * t + 4 * half + k
                    if frame == 0:
                        p1[:, 1 + at_block] = block
                    else:
                        stem2[:, at_block] = block
    for r in range(count):
        for k in range(FB // 2):
            pair = get(r, slice(k * LANES, (k + 1) * LANES))
            p1[r, 1 + 2 * k] = jnp.where(lo, p1[r, 1 + 2 * k], swap_bf(pair))
            p1[r, 2 + 2 * k] = jnp.where(lo, p1[r, 2 + 2 * k], pair)
        seal(p1, r, FB)


def first_fine(src, idx, w_gru, valid, stems, dst, at):
    lo = low_half((1, SUB, LANES))

    def emit(lo_block, count, new):
        dst[at, pl.ds(1 + lo_block, count)] = jnp.where(lo, stems[pl.ds(lo_block, count)], new)

    fine_gru(src, idx, w_gru, valid, emit)
    seal(dst, at, FB)


def fine_own_body(own, w_stem, w_gru, p1, stem2, inside):
    fill_fine(lambda r, lanes: own[r, :, lanes], 4, w_stem, p1, stem2)
    for r in range(2):
        first_fine(p1, 1 + r, w_gru, True, stem2.at[1 + r], inside, r)


def fine_encoder_body(
    p1_own, stem2_own, inside, outer, inner, w_stem, w_gru, w_down,
    state_out, low_own, to_outer, to_inner, second_outer, second_inner, state_outer, state_inner,
    p1_halo, stem2_halo, p2_rest, p3,
):
    upper, first, rows = place(4)
    lo = low_half((1, SUB, LANES))

    def get(r, lanes):
        above = r < 3
        at = r if above else r - 3
        a, b = outer[at, :, lanes], inner[at, :, lanes]
        return jnp.where(upper, a, b) if above else jnp.where(upper, b, a)

    fill_fine(get, 5, w_stem, p1_halo, stem2_halo)
    p1 = [(p1_halo, r) for r in range(3)] + [(p1_own, r) for r in range(4)] + [(p1_halo, r) for r in (3, 4)]
    stem2 = [(stem2_halo, r) for r in range(3)] + [(stem2_own, r) for r in range(4)] + [(stem2_halo, 3)]
    p2 = [None] + [(p2_rest, r) for r in range(3)] + [(inside, 0), (inside, 1), (p2_rest, 3), (p2_rest, 4)]
    for idx in (1, 2, 3, 6, 7):
        dst, at = p2[idx]
        first_fine(p1, idx, w_gru, in_grid(first + idx - 3, rows), row_of(stem2, idx), dst, at)

    for idx in range(2, 7):
        def emit(lo_block, count, new):
            p3[idx, pl.ds(1 + lo_block, count)] = jnp.where(lo, jnp.zeros_like(new), new)

        fine_gru(p2, idx, w_gru, in_grid(first + idx - 3, rows), emit)
        seal(p3, idx, FB)

    def lowered(src, p):
        acc = leaky(down_row(src, 3 + 2 * p, w_down)).astype(BF).astype(F32)
        return pack_forms(coarse_forms(acc[:, :LANES], acc[:, LANES:]))

    def put(ref, at, tiles):
        for k, tile in enumerate(tiles):
            base = at * ROW_TILES + k * PAIRS
            ref[base : base + PAIRS] = tile

    for p in range(2):
        tiles = lowered(p2, p)
        put(low_own, p, tiles)
        put(to_outer, p, tiles)
        put(to_inner, p, tiles)
    for p in range(2):
        tiles = lowered(p3, p)
        put(low_own, 2 + p, tiles)
        outward = upper if p == 0 else jnp.logical_not(upper)

        @pl.when(outward)
        def _():
            put(second_outer, 0, tiles)

        @pl.when(jnp.logical_not(outward))
        def _():
            put(second_inner, 0, tiles)

    for r in range(4):
        for k in range(FB // 2):
            state_out[r, k] = jnp.where(lo[0], swap_bf(p3[3 + r, 1 + 2 * k]), p3[3 + r, 2 + 2 * k])
    for top, ref in ((upper, state_outer), (jnp.logical_not(upper), state_inner)):
        start = jnp.where(top, 0, 2)
        for r in range(2):
            ref[r] = state_out[start + r]


def zero_tail(acc):
    acc[:, 4 * LANES :] = jnp.zeros((CB * SUB, LANES), F32)


def packed_tiles(ref, at):
    return lambda i: ref[at * ROW_TILES + i * PAIRS : at * ROW_TILES + (i + 1) * PAIRS]


def raw_tiles(get):
    def tiles(i):
        return jnp.stack([get(slice((3 * k + i) * LANES, (3 * k + i + 1) * LANES)) for k in range(PAIRS)])

    return tiles


def coarse_state_body(own, outer, inner, w_h, acc_out, h_out, h0):
    upper, _, _ = place(2)
    for idx in range(6):
        if 2 <= idx < 4:
            put_packed(h0, idx, raw_tiles(lambda lanes: own[idx - 2, :, lanes]))
            continue
        r = idx if idx < 2 else idx - 4
        a, b = (outer, inner) if idx < 2 else (inner, outer)
        put_packed(h0, idx, raw_tiles(lambda lanes: jnp.where(upper, a[r, :, lanes], b[r, :, lanes])))

    for idx in range(0, 4):
        acc_out[idx, :, : 3 * C2] = jnp.dot(coarse_patches(h0, idx + 1), w_h[...], preferred_element_type=F32)
        acc_out[idx, :, 4 * LANES + C1 :] = jnp.zeros((CB * SUB, C1), F32)
        h_out[idx] = h0[idx + 1]


def put_row(ref, slot, forms):
    for k, tile in enumerate(pack_forms(forms)):
        base = slot * ROW_TILES + k * PAIRS
        ref[base : base + PAIRS] = tile


def coarse_encoder_body(low_own, low_outer, low_inner, acc_first, h_first, w_x, h1, x1, acc_x):
    upper, first, rows = place(2)
    zero_tail(acc_x)
    for idx in range(6):
        if 2 <= idx < 4:
            put_packed(x1, idx, packed_tiles(low_own, idx - 2))
            continue
        r = idx if idx < 2 else idx - 4
        a, b = (low_outer, low_inner) if idx < 2 else (low_inner, low_outer)
        put_packed(x1, idx, either(upper, a, r, b, r))
    for idx in range(4):
        forms = coarse_gru(
            x1, idx + 1, h_first, idx, w_x, None, acc_x, acc_first.at[idx], in_grid(first + idx - 1, rows)
        )
        put_forms(h1, idx, forms)


def coarse_second_body(low_own, second_outer, second_inner, h1, w_x, w_h, state, x2, acc_x, acc_h):
    upper, _, _ = place(2)
    zero_tail(acc_x)
    zero_tail(acc_h)
    put_packed(x2, 0, either(upper, second_outer, 0, second_inner, 0))
    put_packed(x2, 1, packed_tiles(low_own, 2))
    put_packed(x2, 2, packed_tiles(low_own, 3))
    put_packed(x2, 3, either(upper, second_inner, 0, second_outer, 0))
    for slot in range(2):
        idx = jnp.where(upper, slot, 1 - slot)
        put_row(state, slot, coarse_gru(x2, idx + 1, h1, idx + 1, w_x, w_h, acc_x, acc_h, True))


def raise_pair(src, idx, weight):
    def tile(dr, dj, k):
        return src[idx + dr, 1 + dj : 1 + dj + CB, :, k * LANES : (k + 1) * LANES].reshape(CB * SUB, LANES)

    lo = low_half((CB * SUB, LANES))
    parts = []
    for dr in (0, 1):
        parts += [tile(dr, 0, 0), jnp.where(lo, tile(dr, 0, 1), tile(dr, 1, 2)), tile(dr, 1, 3)]
    return jnp.dot(jnp.concatenate(parts, axis=-1), weight[...], preferred_element_type=F32)


def either(upper, a, i, b, j):
    return lambda t: jnp.where(upper, packed_tiles(a, i)(t), packed_tiles(b, j)(t))


def forecast_row(rows_of, w_h, h2, acc_h, dst, at, first, rows):
    for k, tiles in enumerate(rows_of):
        put_packed(h2, k, tiles)
    forms = coarse_gru(None, 0, h2, 1, None, w_h, None, acc_h, in_grid(first + at, rows))
    put_forms(dst, at, forms)
    return forms


def forecast_inner_body(own, in_near, w_h, s1, sent, h2, acc_h):
    upper, first, rows = place(2)
    zero_tail(acc_h)
    given = (either(upper, own, 0, in_near, 0), packed_tiles(own, 1), either(upper, in_near, 0, own, 0))
    at = jnp.where(upper, 3, 2)
    put_row(sent, 0, forecast_row(given, w_h, h2, acc_h, s1, at, first - 2, rows))


def forecast_outer_body(s1_given, own, outer, w_h, s1, sent, h2, acc_h):
    upper, first, rows = place(2)
    zero_tail(acc_h)
    given = (either(upper, outer, 0, own, 1), packed_tiles(own, 0), either(upper, own, 1, outer, 0))
    at = jnp.where(upper, 2, 3)
    put_row(sent, 0, forecast_row(given, w_h, h2, acc_h, s1, at, first - 2, rows))


def forecast_halo_body(s1_given, own, outer, w_h, s1, h2, acc_h):
    upper, first, rows = place(2)
    zero_tail(acc_h)
    given = (either(upper, outer, 1, own, 0), packed_tiles(outer, 0), either(upper, own, 0, outer, 1))
    forecast_row(given, w_h, h2, acc_h, s1, jnp.where(upper, 1, 4), first - 2, rows)


def forecast_second_body(s1_given, in_near, in_far, w_h, s1, s2, acc_h):
    upper, first, rows = place(2)
    zero_tail(acc_h)
    put_packed(s1, jnp.where(upper, 4, 1), packed_tiles(in_near, 0))
    put_packed(s1, jnp.where(upper, 5, 0), packed_tiles(in_far, 0))
    base = jnp.where(upper, 1, 0)
    for k in range(3):
        at = base + k
        forms = coarse_gru(None, 0, s1, at + 1, None, w_h, None, acc_h, in_grid(first + at - 1, rows))
        put_forms(s2, at, forms)
    s2[4] = jnp.zeros(s2.shape[1:], BF)


def forecaster_body(
    s1_given, s2_given, outer, rest, f_own, f_inner, w_h, w_up, w_gru, w_head,
    out, s1, s2, h2, pf1, pf2, states, acc_h,
):
    upper, first_c, rows_c = place(2)
    _, first_f, rows_f = place(4)
    lo = low_half((1, SUB, LANES))
    zero_tail(acc_h)

    given = (either(upper, rest, 0, outer, 0), packed_tiles(outer, 1), either(upper, outer, 0, rest, 0))
    forecast_row(given, w_h, h2, acc_h, s1, jnp.where(upper, 0, 5), first_c - 2, rows_c)
    at = jnp.where(upper, 0, 3)
    put_forms(
        s2, at, coarse_gru(None, 0, s1, at + 1, None, w_h, None, acc_h, in_grid(first_c + at - 1, rows_c))
    )

    for idx in range(8):
        for k in range(FB // 2):
            if 2 <= idx < 6:
                pair = f_own[idx - 2, k]
            elif idx < 2:
                pair = jnp.where(upper, rest[ROW_TILES + idx * FB // 2 + k], f_inner[idx, k])
            else:
                pair = jnp.where(upper, f_inner[idx - 6, k], rest[ROW_TILES + (idx - 6) * FB // 2 + k])
            pf1[idx, 1 + 2 * k] = swap_bf(pair)
            pf1[idx, 2 + 2 * k] = pair

    def raise_rows(src, idx, fine, at, coarse_row):
        acc = raise_pair(src, idx, w_up)
        acc = jnp.where(in_grid(coarse_row, rows_c), leaky(acc), 0.0)
        for half, row in enumerate(at):
            if row is None:
                continue
            tile = acc[:, half * LANES : (half + 1) * LANES]
            even = tile.astype(BF).reshape(CB, SUB, LANES)
            odd = swap_halves(tile).astype(BF).reshape(CB, SUB, LANES)
            both = jnp.stack([even, odd], axis=1).reshape(FB, SUB, LANES)
            fine[row, 1 : FB + 1] = jnp.where(lo, both, fine[row, 1 : FB + 1])

    for k in range(0, 4):
        raise_rows(s1, k + 1, pf1, (2 * k, 2 * k + 1), first_c + k - 1)
        seal(pf1, 2 * k, FB)
        seal(pf1, 2 * k + 1, FB)

    for idx in range(0, 6):
        def emit(lo_block, count, new):
            pf2[idx, pl.ds(1 + lo_block, count)] = new

        fine_gru(pf1, idx + 1, w_gru, in_grid(first_f + idx - 1, rows_f), emit)

    def head(step, ref, base):
        for t in range(4):
            lhs = jnp.concatenate(
                [ref[base : base + 4, 1 + 8 * t + k].reshape(4 * SUB, LANES) for k in range(8)], axis=-1
            )
            acc = jnp.dot(lhs, w_head[...], preferred_element_type=F32).astype(BF)
            out[step, :, :, t * LANES : (t + 1) * LANES] = acc.reshape(4, SUB, LANES)

    head(0, pf2, 1)

    raise_rows(s2, 0, pf2, (None, 0), first_c - 1)
    raise_rows(s2, 1, pf2, (1, 2), first_c)
    raise_rows(s2, 2, pf2, (3, 4), first_c + 1)
    raise_rows(s2, 3, pf2, (5, None), first_c + 2)
    for idx in range(6):
        seal(pf2, idx, FB)

    for idx in range(0, 4):
        def emit(lo_block, count, new):
            states[idx, pl.ds(1 + lo_block, count)] = new

        fine_gru(pf2, idx + 1, w_gru, True, emit)

    head(1, states, 0)


def to_upper(x):
    return jnp.concatenate([jnp.zeros(x.shape, F32), x.astype(F32)], axis=-1).astype(BF)


def to_lower(x):
    return jnp.concatenate([x.astype(F32), jnp.zeros(x.shape, F32)], axis=-1).astype(BF)


def fetch_all(given, copies, sems):
    fetches = [pltpu.make_async_copy(src, dst, sems.at[i]) for i, (src, dst) in enumerate(zip(given, copies))]
    for fetch in fetches:
        fetch.start()
    for fetch in fetches:
        fetch.wait()


def arrange_gru(kx, kh, w):
    for k in range(9):
        at = k * LANES
        w[at : at + C1, :LANES] = kx[k, :, :LANES]
        w[at : at + C1, LANES:] = to_upper(kx[k, :, LANES:])
        w[at + C1 : at + LANES, :LANES] = kh[k, :, :LANES]
        w[at + C1 : at + LANES, LANES:] = to_lower(kh[k, :, LANES:])


def prepare_encoder_body(*refs):
    given, (w_stem, w_enc, w_down), copies, sems = refs[:4], refs[4:7], refs[7:11], refs[11]
    fetch_all(given, copies, sems)
    stem, enc_x, enc_h, down = copies
    arrange_gru(enc_x, enc_h, w_enc)
    for k in range(9):
        at = k * LANES
        w_down[at : at + C1] = jnp.zeros((C1, 2 * LANES), BF)
        w_down[at + C1 : at + LANES, :LANES] = down[k, :, :LANES]
        w_down[at + C1 : at + LANES, LANES:] = to_lower(down[k, :, LANES:])
    w_stem[...] = jnp.zeros(w_stem.shape, BF)
    wide = to_lower(stem[...])
    for k in range(8):
        w_stem[k * PATCH : (k + 1) * PATCH, k * LANES : (k + 1) * LANES] = wide


def prepare_forecaster_body(*refs):
    given, (w_up, w_fc, w_head), copies, sems = refs[:4], refs[4:7], refs[7:11], refs[11]
    fetch_all(given, copies, sems)
    up, fc_x, fc_h, head = copies
    arrange_gru(fc_x, fc_h, w_fc)

    def tap(a, b):
        return jnp.zeros((C2, C1), F32) if a is None else up[3 * a + b].astype(F32).T

    none = (None, None)
    for g, taps in enumerate((
        ((1, 1), (1, 0), (0, 1), (0, 0)),
        (none, (1, 2), none, (0, 2)),
        (none, none, (2, 1), (2, 0)),
        (none, none, none, (2, 2)),
    )):
        for n in range(2):
            pair = jnp.concatenate([tap(*taps[2 * n]), tap(*taps[2 * n + 1])], axis=-1)
            w_up[g * C2 : (g + 1) * C2, n * LANES : (n + 1) * LANES] = pair.astype(BF)

    w_head[...] = jnp.zeros(w_head.shape, BF)
    tall = head[...].astype(F32).T.astype(BF)
    for k in range(8):
        w_head[k * LANES + C1 : (k + 1) * LANES, k * PATCH : (k + 1) * PATCH] = tall


def call(body, args, outs, scratch, aliases={}):
    return pl.pallas_call(
        body,
        out_shape=[s if isinstance(s, jax.ShapeDtypeStruct) else jax.ShapeDtypeStruct(s, BF) for s in outs],
        in_specs=[pl.BlockSpec(memory_space=space) for _, space in args],
        out_specs=[pl.BlockSpec(memory_space=pltpu.VMEM)] * len(outs),
        scratch_shapes=scratch,
        input_output_aliases=aliases,
        compiler_params=pltpu.CompilerParams(vmem_limit_bytes=24 * 1024 * 1024),
    )(*[arg for arg, _ in args])


def on_device(
    frames,
    start_fine,
    start_coarse,
    enc_stem,
    enc_fine_x,
    enc_fine_h,
    enc_down,
    enc_coarse_x,
    enc_coarse_h,
    fc_coarse_h,
    fc_up,
    fc_fine_x,
    fc_fine_h,
    fc_head,
):
    count = lax.axis_size(LINE)
    across = [(i, i + 1) for i in range(1, count - 1, 2)]
    across = across + [(b, a) for a, b in across]

    def outer_swap(x):
        return lax.ppermute(x, LINE, across)

    def inner_swap(x):
        return lax.ppermute(x, "section", [(0, 1), (1, 0)])

    fine = start_fine.reshape(4, SUB, FB * C1)
    patches = frames.reshape(FRAMES, 4, SUB, FB * PATCH)
    coarse = start_coarse.reshape(2, SUB, CB * C2)

    def on_chip(*values):
        return [(value, pltpu.VMEM) for value in values]

    def fine_buf(rows):
        return pltpu.VMEM((rows, FB + 2, SUB, LANES), BF)

    def coarse_buf(rows):
        return pltpu.VMEM((rows, CB + 2, SUB, 4 * LANES), BF)

    rows = (3, SUB, FB * (C1 + FRAMES * PATCH))
    own, to_outer, to_inner = call(pack_body, on_chip(fine, patches[0], patches[1]), [(4,) + rows[1:], rows, rows], [])
    outer, inner = outer_swap(to_outer), inner_swap(to_inner)

    acc_buf = pltpu.VMEM((CB * SUB, 5 * LANES), F32)
    flat = (9 * C2, 3 * C2)

    def prepare(body, values, outs):
        scratch = [pltpu.VMEM(value.shape, BF) for value in values]
        return call(
            body, [(value, pl.ANY) for value in values], outs, scratch + [pltpu.SemaphoreType.DMA((len(values),))]
        )

    kernel = (9, C1, 3 * C1)
    wide = (9 * LANES, 2 * LANES)
    w_stem, w_enc, w_down = prepare(
        prepare_encoder_body,
        [enc_stem, enc_fine_x.reshape(kernel), enc_fine_h.reshape(kernel), enc_down.reshape(kernel)],
        [(8 * PATCH, 8 * LANES), wide, wide],
    )
    w_up, w_fc, w_head = prepare(
        prepare_forecaster_body,
        [jnp.swapaxes(fc_up.reshape(9, C2, C1), 1, 2), fc_fine_x.reshape(kernel), fc_fine_h.reshape(kernel), fc_head.T],
        [(4 * C2, 2 * LANES), wide, (8 * LANES, 8 * PATCH)],
    )
    coarse_o, coarse_i = outer_swap(coarse), inner_swap(coarse)

    halo = (2 * ROW_TILES, SUB, LANES)
    row = (ROW_TILES, SUB, LANES)
    edge = (2, FB // 2, SUB, LANES)

    def fine_shape(count, blocks=FB + 2):
        return (count, blocks, SUB, LANES)

    p1_own, stem2_own, inside = call(
        fine_own_body, on_chip(own, w_stem, w_enc), [fine_shape(4), fine_shape(4, FB), fine_shape(2)], []
    )
    state_f, low_own, to_outer, to_inner, second_o, second_i, state_fo, state_fi = call(
        fine_encoder_body,
        on_chip(p1_own, stem2_own, inside, outer, inner, w_stem, w_enc, w_down),
        [(4, FB // 2, SUB, LANES), (4 * ROW_TILES, SUB, LANES), halo, halo, row, row, edge, edge],
        [fine_buf(5), pltpu.VMEM(fine_shape(5, FB), BF), fine_buf(5), fine_buf(9)],
    )
    got_o, got_i = outer_swap(to_outer), inner_swap(to_inner)
    second_o, second_i = outer_swap(second_o), inner_swap(second_i)

    acc_first, h_first = call(
        coarse_state_body,
        on_chip(coarse, coarse_o, coarse_i, enc_coarse_h.reshape(flat)),
        [jax.ShapeDtypeStruct((4, CB * SUB, 5 * LANES), F32), (4, CB + 2, SUB, 4 * LANES)],
        [coarse_buf(6)],
    )
    state_fi = inner_swap(state_fi)

    w_x, w_h = enc_coarse_x.reshape(flat), enc_coarse_h.reshape(flat)
    four = (4, CB + 2, SUB, 4 * LANES)
    (h1,) = call(
        coarse_encoder_body, on_chip(low_own, got_o, got_i, acc_first, h_first, w_x), [four], [coarse_buf(6), acc_buf]
    )
    (state_c,) = call(
        coarse_second_body,
        on_chip(low_own, second_o, second_i, h1, w_x, w_h),
        [(2 * ROW_TILES, SUB, LANES)],
        [coarse_buf(4), acc_buf, acc_buf],
    )
    in_near = inner_swap(state_c[ROW_TILES:])
    state_o = outer_swap(state_c)
    rest = outer_swap(jnp.concatenate([in_near, state_fo.reshape(FB, SUB, LANES)], axis=0))

    w_f = fc_coarse_h.reshape(flat)
    six, five = (6,) + four[1:], (5,) + four[1:]
    small = [coarse_buf(3), acc_buf]
    s1, sent = call(forecast_inner_body, on_chip(state_c, in_near, w_f), [six, row], small)
    in_near = inner_swap(sent)
    s1, sent = call(forecast_outer_body, on_chip(s1, state_c, state_o, w_f), [six, row], small, {0: 0})
    in_far = inner_swap(sent)
    (s1,) = call(forecast_halo_body, on_chip(s1, state_c, state_o, w_f), [six], small, {0: 0})
    s1, s2 = call(forecast_second_body, on_chip(s1, in_near, in_far, w_f), [six, five], [acc_buf], {0: 0})
    out, _, _ = call(
        forecaster_body,
        on_chip(s1, s2, state_o, rest, state_f, state_fi, w_f, w_up, w_fc, w_head),
        [(HORIZON, 4, SUB, FB * PATCH), six, five],
        [coarse_buf(3), fine_buf(8), fine_buf(6), fine_buf(4), acc_buf],
        {0: 1, 1: 2},
    )
    return out.reshape(HORIZON, 4, COLS * PATCH)


def solution(mesh):
    line = ("groups", "tile", "section")
    return jax.shard_map(
        on_device,
        mesh=mesh,
        in_specs=(P(None, line, None), P(line, None), P(line, None)) + (P(),) * 11,
        out_specs=P(None, line, None),
        check_vma=False,
    )
```

```python
import jax
import jax.numpy as jnp
from jax import lax
from jax.experimental import pallas as pl
from jax.experimental.pallas import tpu as pltpu
from jax.sharding import PartitionSpec as P


C1 = 64
C2 = 192
PATCH = 16
FRAMES = 2
HORIZON = 2
COLS = 512
SUB = 16
FB = COLS // SUB
CB = COLS // 2 // SUB
LANES = 128
BF = jnp.bfloat16
F32 = jnp.float32
LINE = ("tile", "section")
PAIRS = CB // 2
ROW_TILES = 3 * PAIRS


def leaky(values):
    return jnp.where(values > 0, values, 0.2 * values)


def low_half(shape):
    return lax.broadcasted_iota(jnp.int32, shape, len(shape) - 1) < 64


def swap_halves(x):
    flat = x.reshape(-1, LANES)
    return pltpu.roll(flat, 64, 1).reshape(x.shape)


def swap_bf(x):
    return swap_halves(x.astype(F32)).astype(BF)


def sigmoid(x):
    return 0.5 * jnp.tanh(0.5 * x) + 0.5


def shift_sub(x, by):
    wide = x.astype(F32)
    row = lax.broadcasted_iota(jnp.int32, wide.shape, 0)
    if by > 0:
        moved = jnp.where(row == 0, 0.0, pltpu.roll(wide, 1, 0))
    else:
        moved = jnp.where(row == SUB - 1, 0.0, pltpu.roll(wide, SUB - 1, 0))
    return moved.astype(BF)


def seal(ref, idx, blocks):
    ref[idx, 0] = shift_sub(ref[idx, blocks], 1)
    ref[idx, blocks + 1] = shift_sub(ref[idx, 1], -1)


def row_of(src, idx):
    if isinstance(src, list):
        ref, at = src[idx]
        return ref.at[at]
    return src.at[idx]


def fine_patches(src, idx, lo, count):
    parts = [
        row_of(src, idx + dr)[pl.ds(lo + dj, count)].reshape(count * SUB, LANES)
        for dr in (-1, 0, 1)
        for dj in (0, 1, 2)
    ]
    return jnp.concatenate(parts, axis=-1)


def fine_gru(src, idx, weight, valid, emit):
    count = 16
    for lo in range(0, FB, count):
        acc = jnp.dot(fine_patches(src, idx, lo, count), weight[...], preferred_element_type=F32)
        gates = sigmoid(acc[:, :LANES])
        cand = acc[:, LANES:]
        cand = jnp.tanh(cand + swap_halves(gates * cand))
        old = row_of(src, idx)[pl.ds(1 + lo, count)].reshape(count * SUB, LANES).astype(F32)
        new = (1.0 - gates) * cand + gates * old
        new = jnp.where(valid, new, 0.0).astype(BF)
        emit(lo, count, new.reshape(count, SUB, LANES))


def down_row(src, idx, weight):
    parts = []
    for dr in (-1, 0, 1):
        row = row_of(src, idx + dr)[...].reshape(FB // 2 + 1, 2, SUB, LANES)
        for tap in (row[:CB, 0], row[:CB, 1], row[1:, 0]):
            parts.append(tap.reshape(CB * SUB, LANES))
    lhs = jnp.concatenate(parts, axis=-1)
    return jnp.dot(lhs, weight[...], preferred_element_type=F32)


def coarse_forms(t0, t1):
    lo = low_half(t0.shape)
    r0, r1 = swap_halves(t0), swap_halves(t1)
    return (
        t0.astype(BF),
        jnp.where(lo, t1, 0.0).astype(BF),
        jnp.where(lo, 0.0, r0).astype(BF),
        jnp.where(lo, r0, r1).astype(BF),
    )


def put_forms(ref, idx, forms):
    for k, tile in enumerate(forms):
        ref[idx, 1 : CB + 1, :, k * LANES : (k + 1) * LANES] = tile.reshape(CB, SUB, LANES)
    seal(ref, idx, CB)


def put_packed(ref, idx, tiles):
    t = [tiles(i).astype(F32) for i in range(3)]
    r = [swap_halves(x) for x in t]
    lo = low_half(t[0].shape)
    even = (t[0], jnp.where(lo, t[1], 0.0), jnp.where(lo, 0.0, r[0]), jnp.where(lo, r[0], r[1]))
    odd = (
        jnp.where(lo, r[1], r[2]),
        jnp.where(lo, r[2], 0.0),
        jnp.where(lo, 0.0, t[1]),
        t[2],
    )
    for k in range(4):
        both = jnp.stack([even[k].astype(BF), odd[k].astype(BF)], axis=1)
        ref[idx, 1 : CB + 1, :, k * LANES : (k + 1) * LANES] = both.reshape(CB, SUB, LANES)
    seal(ref, idx, CB)


def pack_forms(forms):
    f = [x.reshape(CB // 2, 2, SUB, LANES) for x in forms]
    lo = low_half((CB // 2, SUB, LANES))
    return (f[0][:, 0], jnp.where(lo, f[1][:, 0], f[2][:, 1]), f[3][:, 1])


def coarse_patches(ref, idx):
    def tile(dr, dj, k):
        return ref[idx + dr, dj : dj + CB, :, k * LANES : (k + 1) * LANES].reshape(CB * SUB, LANES)

    lo = low_half((CB * SUB, LANES))

    def aligned(dr):
        return [
            tile(dr, 0, 0),
            jnp.where(lo, tile(dr, 0, 1), tile(dr, 1, 2)),
            tile(dr, 1, 3),
            tile(dr, 2, 0),
        ]

    parts = aligned(-1)
    parts.append(jnp.where(lo, tile(-1, 2, 1), tile(0, 0, 2)))
    parts += [tile(0, 0, 3), tile(0, 1, 0), jnp.where(lo, tile(0, 1, 1), tile(0, 2, 2)), tile(0, 2, 3)]
    parts += aligned(1)
    parts.append(tile(1, 2, 1))
    return jnp.concatenate(parts, axis=-1)[:, : 9 * C2]


def coarse_gru(x_ref, x_idx, h_ref, h_idx, w_x, w_h, acc_x, acc_h, valid):
    width = 3 * C2
    if w_h is not None:
        acc_h[:, :width] = jnp.dot(coarse_patches(h_ref, h_idx), w_h[...], preferred_element_type=F32)
    if x_ref is not None:
        acc_x[:, :width] = jnp.dot(coarse_patches(x_ref, x_idx), w_x[...], preferred_element_type=F32)

    def part(ref, k):
        return ref[:, k * LANES : (k + 1) * LANES]

    gates = []
    for k in range(3):
        mixed = part(acc_h, k)
        if x_ref is not None:
            mixed = part(acc_x, k) + mixed
        gates.append(sigmoid(mixed))
    lo = low_half(gates[0].shape)
    g1, g2 = swap_halves(gates[1]), swap_halves(gates[2])
    update = (jnp.where(lo, g1, g2), g2)
    out = []
    for k in range(2):
        cand = gates[k] * part(acc_h, 3 + k)
        if x_ref is not None:
            cand = part(acc_x, 3 + k) + cand
        cand = jnp.tanh(cand)
        old = h_ref[h_idx, 1 : CB + 1, :, k * LANES : (k + 1) * LANES].reshape(CB * SUB, LANES).astype(F32)
        new = (1.0 - update[k]) * cand + update[k] * old
        out.append(jnp.where(valid, new, 0.0).astype(BF).astype(F32))
    return coarse_forms(out[0], out[1])


def place(per_device):
    upper = lax.axis_index("section") == 0
    line = lax.axis_index("tile") * lax.axis_size("section") + lax.axis_index("section")
    return upper, line * per_device, lax.axis_size(LINE) * per_device


def in_grid(row, rows):
    return jnp.logical_and(row >= 0, row < rows)


def pack_body(fine, first, second, own, to_outer, to_inner):
    upper, _, _ = place(4)
    for r in range(4):
        own[r, :, : FB * C1] = fine[r]
        own[r, :, FB * C1 : FB * (C1 + PATCH)] = first[r]
        own[r, :, FB * (C1 + PATCH) :] = second[r]
    for r in range(3):
        to_outer[r] = jnp.where(upper, own[r], own[r + 1])
        to_inner[r] = jnp.where(upper, own[r + 1], own[r])


def fill_fine(get, count, w_stem, p1, stem2):
    lo = low_half((SUB, LANES))
    for frame in range(FRAMES):
        for t in range(4):
            at = FB * C1 + frame * FB * PATCH + t * LANES
            patches = jnp.concatenate([get(r, slice(at, at + LANES)) for r in range(count)], axis=0)
            for half in range(2):
                acc = jnp.dot(patches, w_stem[:, half * 512 : half * 512 + 512], preferred_element_type=F32)
                acc = leaky(acc).astype(BF)
                for k in range(4):
                    block = acc[:, k * LANES : (k + 1) * LANES].reshape(count, SUB, LANES)
                    at_block = 8 * t + 4 * half + k
                    if frame == 0:
                        p1[:, 1 + at_block] = block
                    else:
                        stem2[:, at_block] = block
    for r in range(count):
        for k in range(FB // 2):
            pair = get(r, slice(k * LANES, (k + 1) * LANES))
            p1[r, 1 + 2 * k] = jnp.where(lo, p1[r, 1 + 2 * k], swap_bf(pair))
            p1[r, 2 + 2 * k] = jnp.where(lo, p1[r, 2 + 2 * k], pair)
        seal(p1, r, FB)


def first_fine(src, idx, w_gru, valid, stems, dst, at):
    lo = low_half((1, SUB, LANES))

    def emit(lo_block, count, new):
        dst[at, pl.ds(1 + lo_block, count)] = jnp.where(lo, stems[pl.ds(lo_block, count)], new)

    fine_gru(src, idx, w_gru, valid, emit)
    seal(dst, at, FB)


def fine_own_body(own, w_stem, w_gru, p1, stem2, inside):
    fill_fine(lambda r, lanes: own[r, :, lanes], 4, w_stem, p1, stem2)
    for r in range(2):
        first_fine(p1, 1 + r, w_gru, True, stem2.at[1 + r], inside, r)


def fine_encoder_body(
    p1_own, stem2_own, inside, outer, inner, w_stem, w_gru, w_down,
    state_out, low_own, to_outer, to_inner, second_outer, second_inner, state_outer, state_inner,
    p1_halo, stem2_halo, p2_rest, p3,
):
    upper, first, rows = place(4)
    lo = low_half((1, SUB, LANES))

    def get(r, lanes):
        above = r < 3
        at = r if above else r - 3
        a, b = outer[at, :, lanes], inner[at, :, lanes]
        return jnp.where(upper, a, b) if above else jnp.where(upper, b, a)

    fill_fine(get, 5, w_stem, p1_halo, stem2_halo)
    p1 = [(p1_halo, r) for r in range(3)] + [(p1_own, r) for r in range(4)] + [(p1_halo, r) for r in (3, 4)]
    stem2 = [(stem2_halo, r) for r in range(3)] + [(stem2_own, r) for r in range(4)] + [(stem2_halo, 3)]
    p2 = [None] + [(p2_rest, r) for r in range(3)] + [(inside, 0), (inside, 1), (p2_rest, 3), (p2_rest, 4)]
    for idx in (1, 2, 3, 6, 7):
        dst, at = p2[idx]
        first_fine(p1, idx, w_gru, in_grid(first + idx - 3, rows), row_of(stem2, idx), dst, at)

    for idx in range(2, 7):
        def emit(lo_block, count, new):
            p3[idx, pl.ds(1 + lo_block, count)] = jnp.where(lo, jnp.zeros_like(new), new)

        fine_gru(p2, idx, w_gru, in_grid(first + idx - 3, rows), emit)
        seal(p3, idx, FB)

    def lowered(src, p):
        acc = leaky(down_row(src, 3 + 2 * p, w_down)).astype(BF).astype(F32)
        return pack_forms(coarse_forms(acc[:, :LANES], acc[:, LANES:]))

    def put(ref, at, tiles):
        for k, tile in enumerate(tiles):
            base = at * ROW_TILES + k * PAIRS
            ref[base : base + PAIRS] = tile

    for p in range(2):
        tiles = lowered(p2, p)
        put(low_own, p, tiles)
        put(to_outer, p, tiles)
        put(to_inner, p, tiles)
    for p in range(2):
        tiles = lowered(p3, p)
        put(low_own, 2 + p, tiles)
        outward = upper if p == 0 else jnp.logical_not(upper)

        @pl.when(outward)
        def _():
            put(second_outer, 0, tiles)

        @pl.when(jnp.logical_not(outward))
        def _():
            put(second_inner, 0, tiles)

    for r in range(4):
        for k in range(FB // 2):
            state_out[r, k] = jnp.where(lo[0], swap_bf(p3[3 + r, 1 + 2 * k]), p3[3 + r, 2 + 2 * k])
    for top, ref in ((upper, state_outer), (jnp.logical_not(upper), state_inner)):
        start = jnp.where(top, 0, 2)
        for r in range(2):
            ref[r] = state_out[start + r]


def zero_tail(acc):
    acc[:, 4 * LANES :] = jnp.zeros((CB * SUB, LANES), F32)


def packed_tiles(ref, at):
    return lambda i: ref[at * ROW_TILES + i * PAIRS : at * ROW_TILES + (i + 1) * PAIRS]


def raw_tiles(get):
    def tiles(i):
        return jnp.stack([get(slice((3 * k + i) * LANES, (3 * k + i + 1) * LANES)) for k in range(PAIRS)])

    return tiles


def coarse_state_body(own, outer, inner, w_h, acc_out, h_out, h0):
    upper, _, _ = place(2)
    for idx in range(6):
        if 2 <= idx < 4:
            put_packed(h0, idx, raw_tiles(lambda lanes: own[idx - 2, :, lanes]))
            continue
        r = idx if idx < 2 else idx - 4
        a, b = (outer, inner) if idx < 2 else (inner, outer)
        put_packed(h0, idx, raw_tiles(lambda lanes: jnp.where(upper, a[r, :, lanes], b[r, :, lanes])))

    base = jnp.where(upper, 1, 2)
    for k in range(3):
        acc_out[k, :, : 3 * C2] = jnp.dot(coarse_patches(h0, base + k), w_h[...], preferred_element_type=F32)
        acc_out[k, :, 4 * LANES + C1 :] = jnp.zeros((CB * SUB, C1), F32)
        h_out[k] = h0[base + k]


def put_row(ref, slot, forms):
    for k, tile in enumerate(pack_forms(forms)):
        base = slot * ROW_TILES + k * PAIRS
        ref[base : base + PAIRS] = tile


def first_inner_body(low_own, low_inner, acc_first, h_first, w_x, h1, sent, x1, acc_x):
    upper, _, _ = place(2)
    zero_tail(acc_x)
    put_packed(x1, 0, either(upper, low_own, 0, low_inner, 1))
    put_packed(x1, 1, either(upper, low_own, 1, low_own, 0))
    put_packed(x1, 2, either(upper, low_inner, 0, low_own, 1))
    k = jnp.where(upper, 2, 0)
    forms = coarse_gru(x1, 1, h_first, k, w_x, None, acc_x, acc_first.at[k], True)
    put_forms(h1, jnp.where(upper, 2, 1), forms)
    put_row(sent, 0, forms)


def first_outer_body(h1_given, low_own, low_outer, acc_first, h_first, w_x, h1, x1, acc_x):
    upper, first, rows = place(2)
    zero_tail(acc_x)
    put_packed(x1, 0, either(upper, low_outer, 0, low_own, 0))
    put_packed(x1, 1, either(upper, low_outer, 1, low_own, 1))
    put_packed(x1, 2, either(upper, low_own, 0, low_outer, 0))
    put_packed(x1, 3, either(upper, low_own, 1, low_outer, 1))
    for c in (1, 2):
        k = jnp.where(upper, c - 1, c)
        row = jnp.where(upper, c - 2, c)
        forms = coarse_gru(
            x1, c, h_first, k, w_x, None, acc_x, acc_first.at[k], in_grid(first + row, rows)
        )
        put_forms(h1, row + 1, forms)


def coarse_second_body(
    low_own, second_outer, second_inner, h1_given, h1_inner, w_x, w_h, state, h1, x2, acc_x, acc_h
):
    upper, _, _ = place(2)
    zero_tail(acc_x)
    zero_tail(acc_h)
    put_packed(x2, 0, either(upper, second_outer, 0, second_inner, 0))
    put_packed(x2, 1, packed_tiles(low_own, 2))
    put_packed(x2, 2, packed_tiles(low_own, 3))
    put_packed(x2, 3, either(upper, second_inner, 0, second_outer, 0))
    put_packed(h1, jnp.where(upper, 3, 0), packed_tiles(h1_inner, 0))
    for slot in range(2):
        idx = jnp.where(upper, slot, 1 - slot)
        put_row(state, slot, coarse_gru(x2, idx + 1, h1, idx + 1, w_x, w_h, acc_x, acc_h, True))


def raise_pair(src, idx, weight):
    def tile(dr, dj, k):
        return src[idx + dr, 1 + dj : 1 + dj + CB, :, k * LANES : (k + 1) * LANES].reshape(CB * SUB, LANES)

    lo = low_half((CB * SUB, LANES))
    parts = []
    for dr in (0, 1):
        parts += [tile(dr, 0, 0), jnp.where(lo, tile(dr, 0, 1), tile(dr, 1, 2)), tile(dr, 1, 3)]
    return jnp.dot(jnp.concatenate(parts, axis=-1), weight[...], preferred_element_type=F32)


def either(upper, a, i, b, j):
    return lambda t: jnp.where(upper, packed_tiles(a, i)(t), packed_tiles(b, j)(t))


def forecast_row(rows_of, w_h, h2, acc_h, dst, at, first, rows):
    for k, tiles in enumerate(rows_of):
        put_packed(h2, k, tiles)
    forms = coarse_gru(None, 0, h2, 1, None, w_h, None, acc_h, in_grid(first + at, rows))
    put_forms(dst, at, forms)
    return forms


def forecast_inner_body(own, in_near, w_h, s1, sent, h2, acc_h):
    upper, first, rows = place(2)
    zero_tail(acc_h)
    given = (either(upper, own, 0, in_near, 0), packed_tiles(own, 1), either(upper, in_near, 0, own, 0))
    at = jnp.where(upper, 3, 2)
    put_row(sent, 0, forecast_row(given, w_h, h2, acc_h, s1, at, first - 2, rows))


def forecast_outer_body(s1_given, own, outer, w_h, s1, sent, h2, acc_h):
    upper, first, rows = place(2)
    zero_tail(acc_h)
    given = (either(upper, outer, 0, own, 1), packed_tiles(own, 0), either(upper, own, 1, outer, 0))
    at = jnp.where(upper, 2, 3)
    put_row(sent, 0, forecast_row(given, w_h, h2, acc_h, s1, at, first - 2, rows))


def forecast_halo_body(s1_given, own, outer, w_h, s1, h2, acc_h):
    upper, first, rows = place(2)
    zero_tail(acc_h)
    given = (either(upper, outer, 1, own, 0), packed_tiles(outer, 0), either(upper, own, 0, outer, 1))
    forecast_row(given, w_h, h2, acc_h, s1, jnp.where(upper, 1, 4), first - 2, rows)


def forecast_second_body(s1_given, in_near, in_far, w_h, s1, s2, acc_h):
    upper, first, rows = place(2)
    zero_tail(acc_h)
    put_packed(s1, jnp.where(upper, 4, 1), packed_tiles(in_near, 0))
    put_packed(s1, jnp.where(upper, 5, 0), packed_tiles(in_far, 0))
    base = jnp.where(upper, 1, 0)
    for k in range(3):
        at = base + k
        forms = coarse_gru(None, 0, s1, at + 1, None, w_h, None, acc_h, in_grid(first + at - 1, rows))
        put_forms(s2, at, forms)
    s2[4] = jnp.zeros(s2.shape[1:], BF)


def forecaster_body(
    s1_given, s2_given, outer, rest, f_own, f_inner, w_h, w_up, w_gru, w_head,
    out, s1, s2, h2, pf1, pf2, states, acc_h,
):
    upper, first_c, rows_c = place(2)
    _, first_f, rows_f = place(4)
    lo = low_half((1, SUB, LANES))
    zero_tail(acc_h)

    given = (either(upper, rest, 0, outer, 0), packed_tiles(outer, 1), either(upper, outer, 0, rest, 0))
    forecast_row(given, w_h, h2, acc_h, s1, jnp.where(upper, 0, 5), first_c - 2, rows_c)
    at = jnp.where(upper, 0, 3)
    put_forms(
        s2, at, coarse_gru(None, 0, s1, at + 1, None, w_h, None, acc_h, in_grid(first_c + at - 1, rows_c))
    )

    for idx in range(8):
        for k in range(FB // 2):
            if 2 <= idx < 6:
                pair = f_own[idx - 2, k]
            elif idx < 2:
                pair = jnp.where(upper, rest[ROW_TILES + idx * FB // 2 + k], f_inner[idx, k])
            else:
                pair = jnp.where(upper, f_inner[idx - 6, k], rest[ROW_TILES + (idx - 6) * FB // 2 + k])
            pf1[idx, 1 + 2 * k] = swap_bf(pair)
            pf1[idx, 2 + 2 * k] = pair

    def raise_rows(src, idx, fine, at, coarse_row):
        acc = raise_pair(src, idx, w_up)
        acc = jnp.where(in_grid(coarse_row, rows_c), leaky(acc), 0.0)
        for half, row in enumerate(at):
            if row is None:
                continue
            tile = acc[:, half * LANES : (half + 1) * LANES]
            even = tile.astype(BF).reshape(CB, SUB, LANES)
            odd = swap_halves(tile).astype(BF).reshape(CB, SUB, LANES)
            both = jnp.stack([even, odd], axis=1).reshape(FB, SUB, LANES)
            fine[row, 1 : FB + 1] = jnp.where(lo, both, fine[row, 1 : FB + 1])

    for k in range(0, 4):
        raise_rows(s1, k + 1, pf1, (2 * k, 2 * k + 1), first_c + k - 1)
        seal(pf1, 2 * k, FB)
        seal(pf1, 2 * k + 1, FB)

    for idx in range(0, 6):
        def emit(lo_block, count, new):
            pf2[idx, pl.ds(1 + lo_block, count)] = new

        fine_gru(pf1, idx + 1, w_gru, in_grid(first_f + idx - 1, rows_f), emit)

    def head(step, ref, base):
        for t in range(4):
            lhs = jnp.concatenate(
                [ref[base : base + 4, 1 + 8 * t + k].reshape(4 * SUB, LANES) for k in range(8)], axis=-1
            )
            acc = jnp.dot(lhs, w_head[...], preferred_element_type=F32).astype(BF)
            out[step, :, :, t * LANES : (t + 1) * LANES] = acc.reshape(4, SUB, LANES)

    head(0, pf2, 1)

    raise_rows(s2, 0, pf2, (None, 0), first_c - 1)
    raise_rows(s2, 1, pf2, (1, 2), first_c)
    raise_rows(s2, 2, pf2, (3, 4), first_c + 1)
    raise_rows(s2, 3, pf2, (5, None), first_c + 2)
    for idx in range(6):
        seal(pf2, idx, FB)

    for idx in range(0, 4):
        def emit(lo_block, count, new):
            states[idx, pl.ds(1 + lo_block, count)] = new

        fine_gru(pf2, idx + 1, w_gru, True, emit)

    head(1, states, 0)


def to_upper(x):
    return jnp.concatenate([jnp.zeros(x.shape, F32), x.astype(F32)], axis=-1).astype(BF)


def to_lower(x):
    return jnp.concatenate([x.astype(F32), jnp.zeros(x.shape, F32)], axis=-1).astype(BF)


def fetch_all(given, copies, sems):
    fetches = [pltpu.make_async_copy(src, dst, sems.at[i]) for i, (src, dst) in enumerate(zip(given, copies))]
    for fetch in fetches:
        fetch.start()
    for fetch in fetches:
        fetch.wait()


def arrange_gru(kx, kh, w):
    for k in range(9):
        at = k * LANES
        w[at : at + C1, :LANES] = kx[k, :, :LANES]
        w[at : at + C1, LANES:] = to_upper(kx[k, :, LANES:])
        w[at + C1 : at + LANES, :LANES] = kh[k, :, :LANES]
        w[at + C1 : at + LANES, LANES:] = to_lower(kh[k, :, LANES:])


def prepare_encoder_body(*refs):
    given, (w_stem, w_enc, w_down), copies, sems = refs[:4], refs[4:7], refs[7:11], refs[11]
    fetch_all(given, copies, sems)
    stem, enc_x, enc_h, down = copies
    arrange_gru(enc_x, enc_h, w_enc)
    for k in range(9):
        at = k * LANES
        w_down[at : at + C1] = jnp.zeros((C1, 2 * LANES), BF)
        w_down[at + C1 : at + LANES, :LANES] = down[k, :, :LANES]
        w_down[at + C1 : at + LANES, LANES:] = to_lower(down[k, :, LANES:])
    w_stem[...] = jnp.zeros(w_stem.shape, BF)
    wide = to_lower(stem[...])
    for k in range(8):
        w_stem[k * PATCH : (k + 1) * PATCH, k * LANES : (k + 1) * LANES] = wide


def prepare_forecaster_body(*refs):
    given, (w_up, w_fc, w_head), copies, sems = refs[:4], refs[4:7], refs[7:11], refs[11]
    fetch_all(given, copies, sems)
    up, fc_x, fc_h, head = copies
    arrange_gru(fc_x, fc_h, w_fc)

    def tap(a, b):
        return jnp.zeros((C2, C1), F32) if a is None else up[3 * a + b].astype(F32).T

    none = (None, None)
    for g, taps in enumerate((
        ((1, 1), (1, 0), (0, 1), (0, 0)),
        (none, (1, 2), none, (0, 2)),
        (none, none, (2, 1), (2, 0)),
        (none, none, none, (2, 2)),
    )):
        for n in range(2):
            pair = jnp.concatenate([tap(*taps[2 * n]), tap(*taps[2 * n + 1])], axis=-1)
            w_up[g * C2 : (g + 1) * C2, n * LANES : (n + 1) * LANES] = pair.astype(BF)

    w_head[...] = jnp.zeros(w_head.shape, BF)
    tall = head[...].astype(F32).T.astype(BF)
    for k in range(8):
        w_head[k * LANES + C1 : (k + 1) * LANES, k * PATCH : (k + 1) * PATCH] = tall


def call(body, args, outs, scratch, aliases={}):
    return pl.pallas_call(
        body,
        out_shape=[s if isinstance(s, jax.ShapeDtypeStruct) else jax.ShapeDtypeStruct(s, BF) for s in outs],
        in_specs=[pl.BlockSpec(memory_space=space) for _, space in args],
        out_specs=[pl.BlockSpec(memory_space=pltpu.VMEM)] * len(outs),
        scratch_shapes=scratch,
        input_output_aliases=aliases,
        compiler_params=pltpu.CompilerParams(vmem_limit_bytes=24 * 1024 * 1024),
    )(*[arg for arg, _ in args])


def on_device(
    frames,
    start_fine,
    start_coarse,
    enc_stem,
    enc_fine_x,
    enc_fine_h,
    enc_down,
    enc_coarse_x,
    enc_coarse_h,
    fc_coarse_h,
    fc_up,
    fc_fine_x,
    fc_fine_h,
    fc_head,
):
    count = lax.axis_size(LINE)
    across = [(i, i + 1) for i in range(1, count - 1, 2)]
    across = across + [(b, a) for a, b in across]

    def outer_swap(x):
        return lax.ppermute(x, LINE, across)

    def inner_swap(x):
        return lax.ppermute(x, "section", [(0, 1), (1, 0)])

    coarse = start_coarse.reshape(2, SUB, CB * C2)

    def on_chip(*values):
        return [(value, pltpu.VMEM) for value in values]

    def fine_buf(rows):
        return pltpu.VMEM((rows, FB + 2, SUB, LANES), BF)

    def coarse_buf(rows):
        return pltpu.VMEM((rows, CB + 2, SUB, 4 * LANES), BF)

    fine = start_fine.reshape(4, SUB, FB * C1)
    patches = frames.reshape(FRAMES, 4, SUB, FB * PATCH)
    rows = (3, SUB, FB * (C1 + FRAMES * PATCH))
    own, to_outer, to_inner = call(pack_body, on_chip(fine, patches[0], patches[1]), [(4,) + rows[1:], rows, rows], [])
    outer, inner = outer_swap(to_outer), inner_swap(to_inner)

    acc_buf = pltpu.VMEM((CB * SUB, 5 * LANES), F32)
    flat = (9 * C2, 3 * C2)

    def prepare(body, values, outs):
        scratch = [pltpu.VMEM(value.shape, BF) for value in values]
        return call(
            body, [(value, pl.ANY) for value in values], outs, scratch + [pltpu.SemaphoreType.DMA((len(values),))]
        )

    kernel = (9, C1, 3 * C1)
    wide = (9 * LANES, 2 * LANES)
    w_stem, w_enc, w_down = prepare(
        prepare_encoder_body,
        [enc_stem, enc_fine_x.reshape(kernel), enc_fine_h.reshape(kernel), enc_down.reshape(kernel)],
        [(8 * PATCH, 8 * LANES), wide, wide],
    )
    w_up, w_fc, w_head = prepare(
        prepare_forecaster_body,
        [jnp.swapaxes(fc_up.reshape(9, C2, C1), 1, 2), fc_fine_x.reshape(kernel), fc_fine_h.reshape(kernel), fc_head.T],
        [(4 * C2, 2 * LANES), wide, (8 * LANES, 8 * PATCH)],
    )
    coarse_o, coarse_i = outer_swap(coarse), inner_swap(coarse)

    halo = (2 * ROW_TILES, SUB, LANES)
    row = (ROW_TILES, SUB, LANES)
    edge = (2, FB // 2, SUB, LANES)

    def fine_shape(count, blocks=FB + 2):
        return (count, blocks, SUB, LANES)

    p1_own, stem2_own, inside = call(
        fine_own_body, on_chip(own, w_stem, w_enc), [fine_shape(4), fine_shape(4, FB), fine_shape(2)], []
    )
    state_f, low_own, to_outer, to_inner, second_o, second_i, state_fo, state_fi = call(
        fine_encoder_body,
        on_chip(p1_own, stem2_own, inside, outer, inner, w_stem, w_enc, w_down),
        [(4, FB // 2, SUB, LANES), (4 * ROW_TILES, SUB, LANES), halo, halo, row, row, edge, edge],
        [fine_buf(5), pltpu.VMEM(fine_shape(5, FB), BF), fine_buf(5), fine_buf(9)],
    )
    got_o, got_i = outer_swap(to_outer), inner_swap(to_inner)
    second_o, second_i = outer_swap(second_o), inner_swap(second_i)

    acc_first, h_first = call(
        coarse_state_body,
        on_chip(coarse, coarse_o, coarse_i, enc_coarse_h.reshape(flat)),
        [jax.ShapeDtypeStruct((3, CB * SUB, 5 * LANES), F32), (3, CB + 2, SUB, 4 * LANES)],
        [coarse_buf(6)],
    )
    state_fi = inner_swap(state_fi)

    w_x, w_h = enc_coarse_x.reshape(flat), enc_coarse_h.reshape(flat)
    four = (4, CB + 2, SUB, 4 * LANES)
    h1, sent = call(
        first_inner_body, on_chip(low_own, got_i, acc_first, h_first, w_x), [four, row], [coarse_buf(3), acc_buf]
    )
    h1_inner = inner_swap(sent)
    (h1,) = call(
        first_outer_body, on_chip(h1, low_own, got_o, acc_first, h_first, w_x), [four], [coarse_buf(4), acc_buf], {0: 0}
    )
    state_c, _ = call(
        coarse_second_body,
        on_chip(low_own, second_o, second_i, h1, h1_inner, w_x, w_h),
        [(2 * ROW_TILES, SUB, LANES), four],
        [coarse_buf(4), acc_buf, acc_buf],
        {3: 1},
    )
    in_near = inner_swap(state_c[ROW_TILES:])
    state_o = outer_swap(state_c)
    rest = outer_swap(jnp.concatenate([in_near, state_fo.reshape(FB, SUB, LANES)], axis=0))

    w_f = fc_coarse_h.reshape(flat)
    six, five = (6,) + four[1:], (5,) + four[1:]
    small = [coarse_buf(3), acc_buf]
    s1, sent = call(forecast_inner_body, on_chip(state_c, in_near, w_f), [six, row], small)
    in_near = inner_swap(sent)
    s1, sent = call(forecast_outer_body, on_chip(s1, state_c, state_o, w_f), [six, row], small, {0: 0})
    in_far = inner_swap(sent)
    (s1,) = call(forecast_halo_body, on_chip(s1, state_c, state_o, w_f), [six], small, {0: 0})
    s1, s2 = call(forecast_second_body, on_chip(s1, in_near, in_far, w_f), [six, five], [acc_buf], {0: 0})
    out, _, _ = call(
        forecaster_body,
        on_chip(s1, s2, state_o, rest, state_f, state_fi, w_f, w_up, w_fc, w_head),
        [(HORIZON, 4, SUB, FB * PATCH), six, five],
        [coarse_buf(3), fine_buf(8), fine_buf(6), fine_buf(4), acc_buf],
        {0: 1, 1: 2},
    )
    return out.reshape(HORIZON, 4, COLS * PATCH)


def solution(mesh):
    line = ("groups", "tile", "section")
    return jax.shard_map(
        on_device,
        mesh=mesh,
        in_specs=(P(None, line, None), P(line, None), P(line, None)) + (P(),) * 11,
        out_specs=P(None, line, None),
        check_vma=False,
    )
```

```python
import jax
import jax.numpy as jnp
from jax import lax
from jax.experimental import pallas as pl
from jax.experimental.pallas import tpu as pltpu
from jax.sharding import PartitionSpec as P


C1 = 64
C2 = 192
PATCH = 16
FRAMES = 2
HORIZON = 2
COLS = 512
SUB = 16
FB = COLS // SUB
CB = COLS // 2 // SUB
LANES = 128
BF = jnp.bfloat16
F32 = jnp.float32
LINE = ("tile", "section")
PAIRS = CB // 2
ROW_TILES = 3 * PAIRS


def leaky(values):
    return jnp.where(values > 0, values, 0.2 * values)


def low_half(shape):
    return lax.broadcasted_iota(jnp.int32, shape, len(shape) - 1) < 64


def swap_halves(x):
    flat = x.reshape(-1, LANES)
    return pltpu.roll(flat, 64, 1).reshape(x.shape)


def swap_bf(x):
    return swap_halves(x.astype(F32)).astype(BF)


def sigmoid(x):
    return 0.5 * jnp.tanh(0.5 * x) + 0.5


def shift_sub(x, by):
    wide = x.astype(F32)
    row = lax.broadcasted_iota(jnp.int32, wide.shape, 0)
    if by > 0:
        moved = jnp.where(row == 0, 0.0, pltpu.roll(wide, 1, 0))
    else:
        moved = jnp.where(row == SUB - 1, 0.0, pltpu.roll(wide, SUB - 1, 0))
    return moved.astype(BF)


def seal(ref, idx, blocks):
    ref[idx, 0] = shift_sub(ref[idx, blocks], 1)
    ref[idx, blocks + 1] = shift_sub(ref[idx, 1], -1)


def row_of(src, idx):
    if isinstance(src, list):
        ref, at = src[idx]
        return ref.at[at]
    return src.at[idx]


def fine_patches(src, idx, lo, count):
    parts = [
        row_of(src, idx + dr)[pl.ds(lo + dj, count)].reshape(count * SUB, LANES)
        for dr in (-1, 0, 1)
        for dj in (0, 1, 2)
    ]
    return jnp.concatenate(parts, axis=-1)


def fine_gru(src, idx, weight, valid, emit):
    count = 16
    for lo in range(0, FB, count):
        acc = jnp.dot(fine_patches(src, idx, lo, count), weight[...], preferred_element_type=F32)
        gates = sigmoid(acc[:, :LANES])
        cand = acc[:, LANES:]
        cand = jnp.tanh(cand + swap_halves(gates * cand))
        old = row_of(src, idx)[pl.ds(1 + lo, count)].reshape(count * SUB, LANES).astype(F32)
        new = (1.0 - gates) * cand + gates * old
        new = jnp.where(valid, new, 0.0).astype(BF)
        emit(lo, count, new.reshape(count, SUB, LANES))


def down_row(src, idx, weight):
    parts = []
    for dr in (-1, 0, 1):
        row = row_of(src, idx + dr)[...].reshape(FB // 2 + 1, 2, SUB, LANES)
        for tap in (row[:CB, 0], row[:CB, 1], row[1:, 0]):
            parts.append(tap.reshape(CB * SUB, LANES))
    lhs = jnp.concatenate(parts, axis=-1)
    return jnp.dot(lhs, weight[...], preferred_element_type=F32)


def coarse_forms(t0, t1):
    lo = low_half(t0.shape)
    r0, r1 = swap_halves(t0), swap_halves(t1)
    return (
        t0.astype(BF),
        jnp.where(lo, t1, 0.0).astype(BF),
        jnp.where(lo, 0.0, r0).astype(BF),
        jnp.where(lo, r0, r1).astype(BF),
    )


def put_forms(ref, idx, forms):
    for k, tile in enumerate(forms):
        ref[idx, 1 : CB + 1, :, k * LANES : (k + 1) * LANES] = tile.reshape(CB, SUB, LANES)
    seal(ref, idx, CB)


def put_packed(ref, idx, tiles):
    t = [tiles(i).astype(F32) for i in range(3)]
    r = [swap_halves(x) for x in t]
    lo = low_half(t[0].shape)
    even = (t[0], jnp.where(lo, t[1], 0.0), jnp.where(lo, 0.0, r[0]), jnp.where(lo, r[0], r[1]))
    odd = (
        jnp.where(lo, r[1], r[2]),
        jnp.where(lo, r[2], 0.0),
        jnp.where(lo, 0.0, t[1]),
        t[2],
    )
    for k in range(4):
        both = jnp.stack([even[k].astype(BF), odd[k].astype(BF)], axis=1)
        ref[idx, 1 : CB + 1, :, k * LANES : (k + 1) * LANES] = both.reshape(CB, SUB, LANES)
    seal(ref, idx, CB)


def pack_forms(forms):
    f = [x.reshape(CB // 2, 2, SUB, LANES) for x in forms]
    lo = low_half((CB // 2, SUB, LANES))
    return (f[0][:, 0], jnp.where(lo, f[1][:, 0], f[2][:, 1]), f[3][:, 1])


def coarse_patches(ref, idx):
    def tile(dr, dj, k):
        return ref[idx + dr, dj : dj + CB, :, k * LANES : (k + 1) * LANES].reshape(CB * SUB, LANES)

    lo = low_half((CB * SUB, LANES))

    def aligned(dr):
        return [
            tile(dr, 0, 0),
            jnp.where(lo, tile(dr, 0, 1), tile(dr, 1, 2)),
            tile(dr, 1, 3),
            tile(dr, 2, 0),
        ]

    parts = aligned(-1)
    parts.append(jnp.where(lo, tile(-1, 2, 1), tile(0, 0, 2)))
    parts += [tile(0, 0, 3), tile(0, 1, 0), jnp.where(lo, tile(0, 1, 1), tile(0, 2, 2)), tile(0, 2, 3)]
    parts += aligned(1)
    parts.append(tile(1, 2, 1))
    return jnp.concatenate(parts, axis=-1)[:, : 9 * C2]


def coarse_gru(x_ref, x_idx, h_ref, h_idx, w_x, w_h, acc_x, acc_h, valid):
    width = 3 * C2
    if w_h is not None:
        acc_h[:, :width] = jnp.dot(coarse_patches(h_ref, h_idx), w_h[...], preferred_element_type=F32)
    if x_ref is not None:
        acc_x[:, :width] = jnp.dot(coarse_patches(x_ref, x_idx), w_x[...], preferred_element_type=F32)

    def part(ref, k):
        return ref[:, k * LANES : (k + 1) * LANES]

    gates = []
    for k in range(3):
        mixed = part(acc_h, k)
        if x_ref is not None:
            mixed = part(acc_x, k) + mixed
        gates.append(sigmoid(mixed))
    lo = low_half(gates[0].shape)
    g1, g2 = swap_halves(gates[1]), swap_halves(gates[2])
    update = (jnp.where(lo, g1, g2), g2)
    out = []
    for k in range(2):
        cand = gates[k] * part(acc_h, 3 + k)
        if x_ref is not None:
            cand = part(acc_x, 3 + k) + cand
        cand = jnp.tanh(cand)
        old = h_ref[h_idx, 1 : CB + 1, :, k * LANES : (k + 1) * LANES].reshape(CB * SUB, LANES).astype(F32)
        new = (1.0 - update[k]) * cand + update[k] * old
        out.append(jnp.where(valid, new, 0.0).astype(BF).astype(F32))
    return coarse_forms(out[0], out[1])


def place(per_device):
    upper = lax.axis_index("section") == 0
    line = lax.axis_index("tile") * lax.axis_size("section") + lax.axis_index("section")
    return upper, line * per_device, lax.axis_size(LINE) * per_device


def in_grid(row, rows):
    return jnp.logical_and(row >= 0, row < rows)


def pack_body(fine, first, second, own, to_outer, to_inner):
    upper, _, _ = place(4)
    for r in range(4):
        own[r, :, : FB * C1] = fine[r]
        own[r, :, FB * C1 : FB * (C1 + PATCH)] = first[r]
        own[r, :, FB * (C1 + PATCH) :] = second[r]
    for r in range(3):
        to_outer[r] = jnp.where(upper, own[r], own[r + 1])
        to_inner[r] = jnp.where(upper, own[r + 1], own[r])


def fill_fine(get, count, w_stem, p1, stem2):
    lo = low_half((SUB, LANES))
    for frame in range(FRAMES):
        for t in range(4):
            at = FB * C1 + frame * FB * PATCH + t * LANES
            patches = jnp.concatenate([get(r, slice(at, at + LANES)) for r in range(count)], axis=0)
            for half in range(2):
                acc = jnp.dot(patches, w_stem[:, half * 512 : half * 512 + 512], preferred_element_type=F32)
                acc = leaky(acc).astype(BF)
                for k in range(4):
                    block = acc[:, k * LANES : (k + 1) * LANES].reshape(count, SUB, LANES)
                    at_block = 8 * t + 4 * half + k
                    if frame == 0:
                        p1[:, 1 + at_block] = block
                    else:
                        stem2[:, at_block] = block
    for r in range(count):
        for k in range(FB // 2):
            pair = get(r, slice(k * LANES, (k + 1) * LANES))
            p1[r, 1 + 2 * k] = jnp.where(lo, p1[r, 1 + 2 * k], swap_bf(pair))
            p1[r, 2 + 2 * k] = jnp.where(lo, p1[r, 2 + 2 * k], pair)
        seal(p1, r, FB)


def first_fine(src, idx, w_gru, valid, stems, dst, at):
    lo = low_half((1, SUB, LANES))

    def emit(lo_block, count, new):
        dst[at, pl.ds(1 + lo_block, count)] = jnp.where(lo, stems[pl.ds(lo_block, count)], new)

    fine_gru(src, idx, w_gru, valid, emit)
    seal(dst, at, FB)


def fine_own_body(own, w_stem, w_gru, p1, stem2, inside):
    fill_fine(lambda r, lanes: own[r, :, lanes], 4, w_stem, p1, stem2)
    for r in range(2):
        first_fine(p1, 1 + r, w_gru, True, stem2.at[1 + r], inside, r)


def fine_encoder_body(
    p1_own, stem2_own, inside, outer, inner, w_stem, w_gru, w_down,
    state_out, low_own, to_outer, to_inner, second_outer, second_inner, state_outer, state_inner,
    p1_halo, stem2_halo, p2_rest, p3,
):
    upper, first, rows = place(4)
    lo = low_half((1, SUB, LANES))

    def get(r, lanes):
        above = r < 3
        at = r if above else r - 3
        a, b = outer[at, :, lanes], inner[at, :, lanes]
        return jnp.where(upper, a, b) if above else jnp.where(upper, b, a)

    fill_fine(get, 5, w_stem, p1_halo, stem2_halo)
    p1 = [(p1_halo, r) for r in range(3)] + [(p1_own, r) for r in range(4)] + [(p1_halo, r) for r in (3, 4)]
    stem2 = [(stem2_halo, r) for r in range(3)] + [(stem2_own, r) for r in range(4)] + [(stem2_halo, 3)]
    p2 = [None] + [(p2_rest, r) for r in range(3)] + [(inside, 0), (inside, 1), (p2_rest, 3), (p2_rest, 4)]
    for idx in (1, 2, 3, 6, 7):
        dst, at = p2[idx]
        first_fine(p1, idx, w_gru, in_grid(first + idx - 3, rows), row_of(stem2, idx), dst, at)

    for idx in range(2, 7):
        def emit(lo_block, count, new):
            p3[idx, pl.ds(1 + lo_block, count)] = jnp.where(lo, jnp.zeros_like(new), new)

        fine_gru(p2, idx, w_gru, in_grid(first + idx - 3, rows), emit)
        seal(p3, idx, FB)

    def lowered(src, p):
        acc = leaky(down_row(src, 3 + 2 * p, w_down)).astype(BF).astype(F32)
        return pack_forms(coarse_forms(acc[:, :LANES], acc[:, LANES:]))

    def put(ref, at, tiles):
        for k, tile in enumerate(tiles):
            base = at * ROW_TILES + k * PAIRS
            ref[base : base + PAIRS] = tile

    for p in range(2):
        tiles = lowered(p2, p)
        put(low_own, p, tiles)
        put(to_outer, p, tiles)
        put(to_inner, p, tiles)
    for p in range(2):
        tiles = lowered(p3, p)
        put(low_own, 2 + p, tiles)
        outward = upper if p == 0 else jnp.logical_not(upper)

        @pl.when(outward)
        def _():
            put(second_outer, 0, tiles)

        @pl.when(jnp.logical_not(outward))
        def _():
            put(second_inner, 0, tiles)

    for r in range(4):
        for k in range(FB // 2):
            state_out[r, k] = jnp.where(lo[0], swap_bf(p3[3 + r, 1 + 2 * k]), p3[3 + r, 2 + 2 * k])
    for top, ref in ((upper, state_outer), (jnp.logical_not(upper), state_inner)):
        start = jnp.where(top, 0, 2)
        for r in range(2):
            ref[r] = state_out[start + r]


def zero_tail(acc):
    acc[:, 4 * LANES :] = jnp.zeros((CB * SUB, LANES), F32)


def packed_tiles(ref, at):
    return lambda i: ref[at * ROW_TILES + i * PAIRS : at * ROW_TILES + (i + 1) * PAIRS]


def raw_tiles(get):
    def tiles(i):
        return jnp.stack([get(slice((3 * k + i) * LANES, (3 * k + i + 1) * LANES)) for k in range(PAIRS)])

    return tiles


def coarse_state_body(own, outer, inner, w_h, acc_out, h_out, h0):
    upper, _, _ = place(2)
    for idx in range(6):
        if 2 <= idx < 4:
            put_packed(h0, idx, raw_tiles(lambda lanes: own[idx - 2, :, lanes]))
            continue
        r = idx if idx < 2 else idx - 4
        a, b = (outer, inner) if idx < 2 else (inner, outer)
        put_packed(h0, idx, raw_tiles(lambda lanes: jnp.where(upper, a[r, :, lanes], b[r, :, lanes])))

    base = jnp.where(upper, 1, 2)
    for k in range(3):
        acc_out[k, :, : 3 * C2] = jnp.dot(coarse_patches(h0, base + k), w_h[...], preferred_element_type=F32)
        acc_out[k, :, 4 * LANES + C1 :] = jnp.zeros((CB * SUB, C1), F32)
        h_out[k] = h0[base + k]


def put_row(ref, slot, forms):
    for k, tile in enumerate(pack_forms(forms)):
        base = slot * ROW_TILES + k * PAIRS
        ref[base : base + PAIRS] = tile


def first_inner_body(low_own, low_inner, acc_first, h_first, w_x, h1, sent, x1, acc_x):
    upper, _, _ = place(2)
    zero_tail(acc_x)
    put_packed(x1, 0, either(upper, low_own, 0, low_inner, 1))
    put_packed(x1, 1, either(upper, low_own, 1, low_own, 0))
    put_packed(x1, 2, either(upper, low_inner, 0, low_own, 1))
    k = jnp.where(upper, 2, 0)
    forms = coarse_gru(x1, 1, h_first, k, w_x, None, acc_x, acc_first.at[k], True)
    put_forms(h1, jnp.where(upper, 2, 1), forms)
    put_row(sent, 0, forms)


def first_outer_body(h1_given, low_own, low_outer, acc_first, h_first, w_x, h1, x1, acc_x):
    upper, first, rows = place(2)
    zero_tail(acc_x)
    put_packed(x1, 0, either(upper, low_outer, 0, low_own, 0))
    put_packed(x1, 1, either(upper, low_outer, 1, low_own, 1))
    put_packed(x1, 2, either(upper, low_own, 0, low_outer, 0))
    put_packed(x1, 3, either(upper, low_own, 1, low_outer, 1))
    for c in (1, 2):
        k = jnp.where(upper, c - 1, c)
        row = jnp.where(upper, c - 2, c)
        forms = coarse_gru(
            x1, c, h_first, k, w_x, None, acc_x, acc_first.at[k], in_grid(first + row, rows)
        )
        put_forms(h1, row + 1, forms)


def coarse_second_body(
    low_own, second_outer, second_inner, h1_given, h1_inner, w_x, w_h, state, h1, x2, acc_x, acc_h
):
    upper, _, _ = place(2)
    zero_tail(acc_x)
    zero_tail(acc_h)
    put_packed(x2, 0, either(upper, second_outer, 0, second_inner, 0))
    put_packed(x2, 1, packed_tiles(low_own, 2))
    put_packed(x2, 2, packed_tiles(low_own, 3))
    put_packed(x2, 3, either(upper, second_inner, 0, second_outer, 0))
    put_packed(h1, jnp.where(upper, 3, 0), packed_tiles(h1_inner, 0))
    for slot in range(2):
        idx = jnp.where(upper, slot, 1 - slot)
        put_row(state, slot, coarse_gru(x2, idx + 1, h1, idx + 1, w_x, w_h, acc_x, acc_h, True))


def raise_pair(src, idx, weight):
    def tile(dr, dj, k):
        return src[idx + dr, 1 + dj : 1 + dj + CB, :, k * LANES : (k + 1) * LANES].reshape(CB * SUB, LANES)

    lo = low_half((CB * SUB, LANES))
    parts = []
    for dr in (0, 1):
        parts += [tile(dr, 0, 0), jnp.where(lo, tile(dr, 0, 1), tile(dr, 1, 2)), tile(dr, 1, 3)]
    return jnp.dot(jnp.concatenate(parts, axis=-1), weight[...], preferred_element_type=F32)


def either(upper, a, i, b, j):
    return lambda t: jnp.where(upper, packed_tiles(a, i)(t), packed_tiles(b, j)(t))


def forecast_row(rows_of, w_h, h2, acc_h, dst, at, first, rows):
    for k, tiles in enumerate(rows_of):
        put_packed(h2, k, tiles)
    forms = coarse_gru(None, 0, h2, 1, None, w_h, None, acc_h, in_grid(first + at, rows))
    put_forms(dst, at, forms)
    return forms


def forecast_inner_body(own, in_near, w_h, s1, sent, h2, acc_h):
    upper, first, rows = place(2)
    zero_tail(acc_h)
    given = (either(upper, own, 0, in_near, 0), packed_tiles(own, 1), either(upper, in_near, 0, own, 0))
    at = jnp.where(upper, 3, 2)
    put_row(sent, 0, forecast_row(given, w_h, h2, acc_h, s1, at, first - 2, rows))


def forecast_outer_body(s1_given, own, outer, w_h, s1, sent, h2, acc_h):
    upper, first, rows = place(2)
    zero_tail(acc_h)
    given = (either(upper, outer, 0, own, 1), packed_tiles(own, 0), either(upper, own, 1, outer, 0))
    at = jnp.where(upper, 2, 3)
    put_row(sent, 0, forecast_row(given, w_h, h2, acc_h, s1, at, first - 2, rows))


def forecast_halo_body(s1_given, own, outer, w_h, s1, h2, acc_h):
    upper, first, rows = place(2)
    zero_tail(acc_h)
    given = (either(upper, outer, 1, own, 0), packed_tiles(outer, 0), either(upper, own, 0, outer, 1))
    forecast_row(given, w_h, h2, acc_h, s1, jnp.where(upper, 1, 4), first - 2, rows)


def forecast_second_body(s1_given, in_near, in_far, w_h, s1, s2, acc_h):
    upper, first, rows = place(2)
    zero_tail(acc_h)
    put_packed(s1, jnp.where(upper, 4, 1), packed_tiles(in_near, 0))
    put_packed(s1, jnp.where(upper, 5, 0), packed_tiles(in_far, 0))
    base = jnp.where(upper, 1, 0)
    for k in range(3):
        at = base + k
        forms = coarse_gru(None, 0, s1, at + 1, None, w_h, None, acc_h, in_grid(first + at - 1, rows))
        put_forms(s2, at, forms)
    s2[4] = jnp.zeros(s2.shape[1:], BF)


def forecaster_body(
    s1_given, s2_given, outer, rest, f_own, f_inner, w_h, w_up, w_gru, w_head,
    out, s1, s2, h2, pf1, pf2, states, acc_h,
):
    upper, first_c, rows_c = place(2)
    _, first_f, rows_f = place(4)
    lo = low_half((1, SUB, LANES))
    zero_tail(acc_h)

    given = (either(upper, rest, 0, outer, 0), packed_tiles(outer, 1), either(upper, outer, 0, rest, 0))
    forecast_row(given, w_h, h2, acc_h, s1, jnp.where(upper, 0, 5), first_c - 2, rows_c)
    at = jnp.where(upper, 0, 3)
    put_forms(
        s2, at, coarse_gru(None, 0, s1, at + 1, None, w_h, None, acc_h, in_grid(first_c + at - 1, rows_c))
    )

    for idx in range(8):
        for k in range(FB // 2):
            if 2 <= idx < 6:
                pair = f_own[idx - 2, k]
            elif idx < 2:
                at = ROW_TILES + idx * FB // 2 + k
                pair = jnp.where(upper, rest[at], f_inner[at])
            else:
                at = ROW_TILES + (idx - 6) * FB // 2 + k
                pair = jnp.where(upper, f_inner[at], rest[at])
            pf1[idx, 1 + 2 * k] = swap_bf(pair)
            pf1[idx, 2 + 2 * k] = pair

    def raise_rows(src, idx, fine, at, coarse_row):
        acc = raise_pair(src, idx, w_up)
        acc = jnp.where(in_grid(coarse_row, rows_c), leaky(acc), 0.0)
        for half, row in enumerate(at):
            if row is None:
                continue
            tile = acc[:, half * LANES : (half + 1) * LANES]
            even = tile.astype(BF).reshape(CB, SUB, LANES)
            odd = swap_halves(tile).astype(BF).reshape(CB, SUB, LANES)
            both = jnp.stack([even, odd], axis=1).reshape(FB, SUB, LANES)
            fine[row, 1 : FB + 1] = jnp.where(lo, both, fine[row, 1 : FB + 1])

    for k in range(0, 4):
        raise_rows(s1, k + 1, pf1, (2 * k, 2 * k + 1), first_c + k - 1)
        seal(pf1, 2 * k, FB)
        seal(pf1, 2 * k + 1, FB)

    for idx in range(0, 6):
        def emit(lo_block, count, new):
            pf2[idx, pl.ds(1 + lo_block, count)] = new

        fine_gru(pf1, idx + 1, w_gru, in_grid(first_f + idx - 1, rows_f), emit)

    def head(step, ref, base):
        for t in range(4):
            lhs = jnp.concatenate(
                [ref[base : base + 4, 1 + 8 * t + k].reshape(4 * SUB, LANES) for k in range(8)], axis=-1
            )
            acc = jnp.dot(lhs, w_head[...], preferred_element_type=F32).astype(BF)
            out[step, :, :, t * LANES : (t + 1) * LANES] = acc.reshape(4, SUB, LANES)

    head(0, pf2, 1)

    raise_rows(s2, 0, pf2, (None, 0), first_c - 1)
    raise_rows(s2, 1, pf2, (1, 2), first_c)
    raise_rows(s2, 2, pf2, (3, 4), first_c + 1)
    raise_rows(s2, 3, pf2, (5, None), first_c + 2)
    for idx in range(6):
        seal(pf2, idx, FB)

    for idx in range(0, 4):
        def emit(lo_block, count, new):
            states[idx, pl.ds(1 + lo_block, count)] = new

        fine_gru(pf2, idx + 1, w_gru, True, emit)

    head(1, states, 0)


def to_upper(x):
    return jnp.concatenate([jnp.zeros(x.shape, F32), x.astype(F32)], axis=-1).astype(BF)


def to_lower(x):
    return jnp.concatenate([x.astype(F32), jnp.zeros(x.shape, F32)], axis=-1).astype(BF)


def fetch_all(given, copies, sems):
    fetches = [pltpu.make_async_copy(src, dst, sems.at[i]) for i, (src, dst) in enumerate(zip(given, copies))]
    for fetch in fetches:
        fetch.start()
    for fetch in fetches:
        fetch.wait()


def arrange_gru(kx, kh, w):
    for k in range(9):
        at = k * LANES
        w[at : at + C1, :LANES] = kx[k, :, :LANES]
        w[at : at + C1, LANES:] = to_upper(kx[k, :, LANES:])
        w[at + C1 : at + LANES, :LANES] = kh[k, :, :LANES]
        w[at + C1 : at + LANES, LANES:] = to_lower(kh[k, :, LANES:])


def prepare_encoder_body(*refs):
    given, (w_stem, w_enc, w_down), copies, sems = refs[:4], refs[4:7], refs[7:11], refs[11]
    fetch_all(given, copies, sems)
    stem, enc_x, enc_h, down = copies
    arrange_gru(enc_x, enc_h, w_enc)
    for k in range(9):
        at = k * LANES
        w_down[at : at + C1] = jnp.zeros((C1, 2 * LANES), BF)
        w_down[at + C1 : at + LANES, :LANES] = down[k, :, :LANES]
        w_down[at + C1 : at + LANES, LANES:] = to_lower(down[k, :, LANES:])
    w_stem[...] = jnp.zeros(w_stem.shape, BF)
    wide = to_lower(stem[...])
    for k in range(8):
        w_stem[k * PATCH : (k + 1) * PATCH, k * LANES : (k + 1) * LANES] = wide


def prepare_forecaster_body(*refs):
    given, (w_up, w_fc, w_head), copies, sems = refs[:4], refs[4:7], refs[7:11], refs[11]
    fetch_all(given, copies, sems)
    up, fc_x, fc_h, head = copies
    arrange_gru(fc_x, fc_h, w_fc)

    def tap(a, b):
        return jnp.zeros((C2, C1), F32) if a is None else up[3 * a + b].astype(F32).T

    none = (None, None)
    for g, taps in enumerate((
        ((1, 1), (1, 0), (0, 1), (0, 0)),
        (none, (1, 2), none, (0, 2)),
        (none, none, (2, 1), (2, 0)),
        (none, none, none, (2, 2)),
    )):
        for n in range(2):
            pair = jnp.concatenate([tap(*taps[2 * n]), tap(*taps[2 * n + 1])], axis=-1)
            w_up[g * C2 : (g + 1) * C2, n * LANES : (n + 1) * LANES] = pair.astype(BF)

    w_head[...] = jnp.zeros(w_head.shape, BF)
    tall = head[...].astype(F32).T.astype(BF)
    for k in range(8):
        w_head[k * LANES + C1 : (k + 1) * LANES, k * PATCH : (k + 1) * PATCH] = tall


def call(body, args, outs, scratch, aliases={}):
    return pl.pallas_call(
        body,
        out_shape=[s if isinstance(s, jax.ShapeDtypeStruct) else jax.ShapeDtypeStruct(s, BF) for s in outs],
        in_specs=[pl.BlockSpec(memory_space=space) for _, space in args],
        out_specs=[pl.BlockSpec(memory_space=pltpu.VMEM)] * len(outs),
        scratch_shapes=scratch,
        input_output_aliases=aliases,
        compiler_params=pltpu.CompilerParams(vmem_limit_bytes=24 * 1024 * 1024),
    )(*[arg for arg, _ in args])


def on_device(
    frames,
    start_fine,
    start_coarse,
    enc_stem,
    enc_fine_x,
    enc_fine_h,
    enc_down,
    enc_coarse_x,
    enc_coarse_h,
    fc_coarse_h,
    fc_up,
    fc_fine_x,
    fc_fine_h,
    fc_head,
):
    count = lax.axis_size(LINE)
    across = [(i, i + 1) for i in range(1, count - 1, 2)]
    across = across + [(b, a) for a, b in across]

    def outer_swap(x):
        return lax.ppermute(x, LINE, across)

    def inner_swap(x):
        return lax.ppermute(x, "section", [(0, 1), (1, 0)])

    coarse = start_coarse.reshape(2, SUB, CB * C2)

    def on_chip(*values):
        return [(value, pltpu.VMEM) for value in values]

    def fine_buf(rows):
        return pltpu.VMEM((rows, FB + 2, SUB, LANES), BF)

    def coarse_buf(rows):
        return pltpu.VMEM((rows, CB + 2, SUB, 4 * LANES), BF)

    fine = start_fine.reshape(4, SUB, FB * C1)
    patches = frames.reshape(FRAMES, 4, SUB, FB * PATCH)
    rows = (3, SUB, FB * (C1 + FRAMES * PATCH))
    own, to_outer, to_inner = call(pack_body, on_chip(fine, patches[0], patches[1]), [(4,) + rows[1:], rows, rows], [])
    outer, inner = outer_swap(to_outer), inner_swap(to_inner)

    acc_buf = pltpu.VMEM((CB * SUB, 5 * LANES), F32)
    flat = (9 * C2, 3 * C2)

    def prepare(body, values, outs):
        scratch = [pltpu.VMEM(value.shape, BF) for value in values]
        return call(
            body, [(value, pl.ANY) for value in values], outs, scratch + [pltpu.SemaphoreType.DMA((len(values),))]
        )

    kernel = (9, C1, 3 * C1)
    wide = (9 * LANES, 2 * LANES)
    w_stem, w_enc, w_down = prepare(
        prepare_encoder_body,
        [enc_stem, enc_fine_x.reshape(kernel), enc_fine_h.reshape(kernel), enc_down.reshape(kernel)],
        [(8 * PATCH, 8 * LANES), wide, wide],
    )
    w_up, w_fc, w_head = prepare(
        prepare_forecaster_body,
        [jnp.swapaxes(fc_up.reshape(9, C2, C1), 1, 2), fc_fine_x.reshape(kernel), fc_fine_h.reshape(kernel), fc_head.T],
        [(4 * C2, 2 * LANES), wide, (8 * LANES, 8 * PATCH)],
    )
    coarse_o, coarse_i = outer_swap(coarse), inner_swap(coarse)

    halo = (2 * ROW_TILES, SUB, LANES)
    row = (ROW_TILES, SUB, LANES)
    edge = (2, FB // 2, SUB, LANES)

    def fine_shape(count, blocks=FB + 2):
        return (count, blocks, SUB, LANES)

    p1_own, stem2_own, inside = call(
        fine_own_body, on_chip(own, w_stem, w_enc), [fine_shape(4), fine_shape(4, FB), fine_shape(2)], []
    )
    state_f, low_own, to_outer, to_inner, second_o, second_i, state_fo, state_fi = call(
        fine_encoder_body,
        on_chip(p1_own, stem2_own, inside, outer, inner, w_stem, w_enc, w_down),
        [(4, FB // 2, SUB, LANES), (4 * ROW_TILES, SUB, LANES), halo, halo, row, row, edge, edge],
        [fine_buf(5), pltpu.VMEM(fine_shape(5, FB), BF), fine_buf(5), fine_buf(9)],
    )
    got_o, got_i = outer_swap(to_outer), inner_swap(to_inner)
    second_o, second_i = outer_swap(second_o), inner_swap(second_i)

    acc_first, h_first = call(
        coarse_state_body,
        on_chip(coarse, coarse_o, coarse_i, enc_coarse_h.reshape(flat)),
        [jax.ShapeDtypeStruct((3, CB * SUB, 5 * LANES), F32), (3, CB + 2, SUB, 4 * LANES)],
        [coarse_buf(6)],
    )

    w_x, w_h = enc_coarse_x.reshape(flat), enc_coarse_h.reshape(flat)
    four = (4, CB + 2, SUB, 4 * LANES)
    h1, sent = call(
        first_inner_body, on_chip(low_own, got_i, acc_first, h_first, w_x), [four, row], [coarse_buf(3), acc_buf]
    )
    h1_inner = inner_swap(sent)
    (h1,) = call(
        first_outer_body, on_chip(h1, low_own, got_o, acc_first, h_first, w_x), [four], [coarse_buf(4), acc_buf], {0: 0}
    )
    state_c, _ = call(
        coarse_second_body,
        on_chip(low_own, second_o, second_i, h1, h1_inner, w_x, w_h),
        [(2 * ROW_TILES, SUB, LANES), four],
        [coarse_buf(4), acc_buf, acc_buf],
        {3: 1},
    )
    edge_i = jnp.concatenate([state_c[ROW_TILES:], state_fi.reshape(FB, SUB, LANES)], axis=0)
    edge_i = inner_swap(edge_i)
    in_near = edge_i[:ROW_TILES]
    state_o = outer_swap(state_c)
    rest = outer_swap(jnp.concatenate([in_near, state_fo.reshape(FB, SUB, LANES)], axis=0))

    w_f = fc_coarse_h.reshape(flat)
    six, five = (6,) + four[1:], (5,) + four[1:]
    small = [coarse_buf(3), acc_buf]
    s1, sent = call(forecast_inner_body, on_chip(state_c, edge_i, w_f), [six, row], small)
    in_near = inner_swap(sent)
    s1, sent = call(forecast_outer_body, on_chip(s1, state_c, state_o, w_f), [six, row], small, {0: 0})
    in_far = inner_swap(sent)
    (s1,) = call(forecast_halo_body, on_chip(s1, state_c, state_o, w_f), [six], small, {0: 0})
    s1, s2 = call(forecast_second_body, on_chip(s1, in_near, in_far, w_f), [six, five], [acc_buf], {0: 0})
    out, _, _ = call(
        forecaster_body,
        on_chip(s1, s2, state_o, rest, state_f, edge_i, w_f, w_up, w_fc, w_head),
        [(HORIZON, 4, SUB, FB * PATCH), six, five],
        [coarse_buf(3), fine_buf(8), fine_buf(6), fine_buf(4), acc_buf],
        {0: 1, 1: 2},
    )
    return out.reshape(HORIZON, 4, COLS * PATCH)


def solution(mesh):
    line = ("groups", "tile", "section")
    return jax.shard_map(
        on_device,
        mesh=mesh,
        in_specs=(P(None, line, None), P(line, None), P(line, None)) + (P(),) * 11,
        out_specs=P(None, line, None),
        check_vma=False,
    )
```

```python
import jax
import jax.numpy as jnp
from jax import lax
from jax.experimental import pallas as pl
from jax.experimental.pallas import tpu as pltpu
from jax.sharding import PartitionSpec as P


C1 = 64
C2 = 192
PATCH = 16
FRAMES = 2
HORIZON = 2
COLS = 512
SUB = 16
FB = COLS // SUB
CB = COLS // 2 // SUB
LANES = 128
BF = jnp.bfloat16
F32 = jnp.float32
LINE = ("tile", "section")
PAIRS = CB // 2
ROW_TILES = 3 * PAIRS


def leaky(values):
    return jnp.where(values > 0, values, 0.2 * values)


def low_half(shape):
    return lax.broadcasted_iota(jnp.int32, shape, len(shape) - 1) < 64


def swap_halves(x):
    flat = x.reshape(-1, LANES)
    return pltpu.roll(flat, 64, 1).reshape(x.shape)


def swap_bf(x):
    return swap_halves(x.astype(F32)).astype(BF)


def sigmoid(x):
    return 0.5 * jnp.tanh(0.5 * x) + 0.5


def shift_sub(x, by):
    wide = x.astype(F32)
    row = lax.broadcasted_iota(jnp.int32, wide.shape, 0)
    if by > 0:
        moved = jnp.where(row == 0, 0.0, pltpu.roll(wide, 1, 0))
    else:
        moved = jnp.where(row == SUB - 1, 0.0, pltpu.roll(wide, SUB - 1, 0))
    return moved.astype(BF)


def seal(ref, idx, blocks):
    ref[idx, 0] = shift_sub(ref[idx, blocks], 1)
    ref[idx, blocks + 1] = shift_sub(ref[idx, 1], -1)


def row_of(src, idx):
    if isinstance(src, list):
        ref, at = src[idx]
        return ref.at[at]
    return src.at[idx]


def fine_patches(src, idx, lo, count):
    parts = [
        row_of(src, idx + dr)[pl.ds(lo + dj, count)].reshape(count * SUB, LANES)
        for dr in (-1, 0, 1)
        for dj in (0, 1, 2)
    ]
    return jnp.concatenate(parts, axis=-1)


def fine_gru(src, idx, weight, valid, emit):
    count = 16
    for lo in range(0, FB, count):
        acc = jnp.dot(fine_patches(src, idx, lo, count), weight[...], preferred_element_type=F32)
        gates = sigmoid(acc[:, :LANES])
        cand = acc[:, LANES:]
        cand = jnp.tanh(cand + swap_halves(gates * cand))
        old = row_of(src, idx)[pl.ds(1 + lo, count)].reshape(count * SUB, LANES).astype(F32)
        new = (1.0 - gates) * cand + gates * old
        new = jnp.where(valid, new, 0.0).astype(BF)
        emit(lo, count, new.reshape(count, SUB, LANES))


def down_row(src, idx, weight):
    parts = []
    for dr in (-1, 0, 1):
        row = row_of(src, idx + dr)[...].reshape(FB // 2 + 1, 2, SUB, LANES)
        for tap in (row[:CB, 0], row[:CB, 1], row[1:, 0]):
            parts.append(tap.reshape(CB * SUB, LANES))
    lhs = jnp.concatenate(parts, axis=-1)
    return jnp.dot(lhs, weight[...], preferred_element_type=F32)


def coarse_forms(t0, t1):
    lo = low_half(t0.shape)
    r0, r1 = swap_halves(t0), swap_halves(t1)
    return (
        t0.astype(BF),
        jnp.where(lo, t1, 0.0).astype(BF),
        jnp.where(lo, 0.0, r0).astype(BF),
        jnp.where(lo, r0, r1).astype(BF),
    )


def put_forms(ref, idx, forms):
    for k, tile in enumerate(forms):
        ref[idx, 1 : CB + 1, :, k * LANES : (k + 1) * LANES] = tile.reshape(CB, SUB, LANES)
    seal(ref, idx, CB)


def put_packed(ref, idx, tiles):
    t = [tiles(i).astype(F32) for i in range(3)]
    r = [swap_halves(x) for x in t]
    lo = low_half(t[0].shape)
    even = (t[0], jnp.where(lo, t[1], 0.0), jnp.where(lo, 0.0, r[0]), jnp.where(lo, r[0], r[1]))
    odd = (
        jnp.where(lo, r[1], r[2]),
        jnp.where(lo, r[2], 0.0),
        jnp.where(lo, 0.0, t[1]),
        t[2],
    )
    for k in range(4):
        both = jnp.stack([even[k].astype(BF), odd[k].astype(BF)], axis=1)
        ref[idx, 1 : CB + 1, :, k * LANES : (k + 1) * LANES] = both.reshape(CB, SUB, LANES)
    seal(ref, idx, CB)


def pack_forms(forms):
    f = [x.reshape(CB // 2, 2, SUB, LANES) for x in forms]
    lo = low_half((CB // 2, SUB, LANES))
    return (f[0][:, 0], jnp.where(lo, f[1][:, 0], f[2][:, 1]), f[3][:, 1])


def coarse_patches(ref, idx):
    def tile(dr, dj, k):
        return ref[idx + dr, dj : dj + CB, :, k * LANES : (k + 1) * LANES].reshape(CB * SUB, LANES)

    lo = low_half((CB * SUB, LANES))

    def aligned(dr):
        return [
            tile(dr, 0, 0),
            jnp.where(lo, tile(dr, 0, 1), tile(dr, 1, 2)),
            tile(dr, 1, 3),
            tile(dr, 2, 0),
        ]

    parts = aligned(-1)
    parts.append(jnp.where(lo, tile(-1, 2, 1), tile(0, 0, 2)))
    parts += [tile(0, 0, 3), tile(0, 1, 0), jnp.where(lo, tile(0, 1, 1), tile(0, 2, 2)), tile(0, 2, 3)]
    parts += aligned(1)
    parts.append(tile(1, 2, 1))
    return jnp.concatenate(parts, axis=-1)[:, : 9 * C2]


def coarse_gru(x_ref, x_idx, h_ref, h_idx, w_x, w_h, acc_x, acc_h, valid):
    width = 3 * C2
    if w_h is not None:
        acc_h[:, :width] = jnp.dot(coarse_patches(h_ref, h_idx), w_h[...], preferred_element_type=F32)
    if x_ref is not None:
        acc_x[:, :width] = jnp.dot(coarse_patches(x_ref, x_idx), w_x[...], preferred_element_type=F32)

    def part(ref, k):
        return ref[:, k * LANES : (k + 1) * LANES]

    gates = []
    for k in range(3):
        mixed = part(acc_h, k)
        if x_ref is not None:
            mixed = part(acc_x, k) + mixed
        gates.append(sigmoid(mixed))
    lo = low_half(gates[0].shape)
    g1, g2 = swap_halves(gates[1]), swap_halves(gates[2])
    update = (jnp.where(lo, g1, g2), g2)
    out = []
    for k in range(2):
        cand = gates[k] * part(acc_h, 3 + k)
        if x_ref is not None:
            cand = part(acc_x, 3 + k) + cand
        cand = jnp.tanh(cand)
        old = h_ref[h_idx, 1 : CB + 1, :, k * LANES : (k + 1) * LANES].reshape(CB * SUB, LANES).astype(F32)
        new = (1.0 - update[k]) * cand + update[k] * old
        out.append(jnp.where(valid, new, 0.0).astype(BF).astype(F32))
    return coarse_forms(out[0], out[1])


def place(per_device):
    upper = lax.axis_index("section") == 0
    line = lax.axis_index("tile") * lax.axis_size("section") + lax.axis_index("section")
    return upper, line * per_device, lax.axis_size(LINE) * per_device


def in_grid(row, rows):
    return jnp.logical_and(row >= 0, row < rows)


def pack_body(fine, first, second, own, to_outer, to_inner):
    upper, _, _ = place(4)
    for r in range(4):
        own[r, :, : FB * C1] = fine[r]
        own[r, :, FB * C1 : FB * (C1 + PATCH)] = first[r]
        own[r, :, FB * (C1 + PATCH) :] = second[r]
    for r in range(3):
        to_outer[r] = jnp.where(upper, own[r], own[r + 1])
        to_inner[r] = jnp.where(upper, own[r + 1], own[r])


def fill_fine(get, count, w_stem, p1, stem2):
    lo = low_half((SUB, LANES))
    for frame in range(FRAMES):
        for t in range(4):
            at = FB * C1 + frame * FB * PATCH + t * LANES
            patches = jnp.concatenate([get(r, slice(at, at + LANES)) for r in range(count)], axis=0)
            acc = leaky(jnp.dot(patches, w_stem[...], preferred_element_type=F32))
            for k in range(8):
                tile = acc[:, k // 2 * LANES : (k // 2 + 1) * LANES]
                tile = swap_halves(tile) if k % 2 else tile
                block = tile.astype(BF).reshape(count, SUB, LANES)
                if frame == 0:
                    p1[:, 1 + 8 * t + k] = block
                else:
                    stem2[:, 8 * t + k] = block
    for r in range(count):
        for k in range(FB // 2):
            pair = get(r, slice(k * LANES, (k + 1) * LANES))
            p1[r, 1 + 2 * k] = jnp.where(lo, p1[r, 1 + 2 * k], swap_bf(pair))
            p1[r, 2 + 2 * k] = jnp.where(lo, p1[r, 2 + 2 * k], pair)
        seal(p1, r, FB)


def first_fine(src, idx, w_gru, valid, stems, dst, at):
    lo = low_half((1, SUB, LANES))

    def emit(lo_block, count, new):
        dst[at, pl.ds(1 + lo_block, count)] = jnp.where(lo, stems[pl.ds(lo_block, count)], new)

    fine_gru(src, idx, w_gru, valid, emit)
    seal(dst, at, FB)


def fine_own_body(own, w_stem, w_gru, p1, stem2, inside):
    fill_fine(lambda r, lanes: own[r, :, lanes], 4, w_stem, p1, stem2)
    for r in range(2):
        first_fine(p1, 1 + r, w_gru, True, stem2.at[1 + r], inside, r)


def fine_encoder_body(
    p1_own, stem2_own, inside, outer, inner, w_stem, w_gru, w_down,
    state_out, low_own, to_outer, to_inner, state_outer, state_inner,
    p1_halo, stem2_halo, p2_rest, p3,
):
    upper, first, rows = place(4)
    lo = low_half((1, SUB, LANES))

    def get(r, lanes):
        above = r < 3
        at = r if above else r - 3
        a, b = outer[at, :, lanes], inner[at, :, lanes]
        return jnp.where(upper, a, b) if above else jnp.where(upper, b, a)

    fill_fine(get, 5, w_stem, p1_halo, stem2_halo)
    p1 = [(p1_halo, r) for r in range(3)] + [(p1_own, r) for r in range(4)] + [(p1_halo, r) for r in (3, 4)]
    stem2 = [(stem2_halo, r) for r in range(3)] + [(stem2_own, r) for r in range(4)] + [(stem2_halo, 3)]
    p2 = [None] + [(p2_rest, r) for r in range(3)] + [(inside, 0), (inside, 1), (p2_rest, 3), (p2_rest, 4)]
    for idx in (1, 2, 3, 6, 7):
        dst, at = p2[idx]
        first_fine(p1, idx, w_gru, in_grid(first + idx - 3, rows), row_of(stem2, idx), dst, at)

    for idx in range(2, 7):
        def emit(lo_block, count, new):
            p3[idx, pl.ds(1 + lo_block, count)] = jnp.where(lo, jnp.zeros_like(new), new)

        fine_gru(p2, idx, w_gru, in_grid(first + idx - 3, rows), emit)
        seal(p3, idx, FB)

    def lowered(src, p):
        acc = leaky(down_row(src, 3 + 2 * p, w_down)).astype(BF).astype(F32)
        return pack_forms(coarse_forms(acc[:, :LANES], acc[:, LANES:]))

    def put(ref, at, tiles):
        for k, tile in enumerate(tiles):
            base = at * ROW_TILES + k * PAIRS
            ref[base : base + PAIRS] = tile

    for p in range(2):
        tiles = lowered(p2, p)
        put(low_own, p, tiles)
        put(to_outer, p, tiles)
        put(to_inner, p, tiles)
    for p in range(2):
        tiles = lowered(p3, p)
        put(low_own, 2 + p, tiles)
        outward = upper if p == 0 else jnp.logical_not(upper)

        @pl.when(outward)
        def _():
            put(to_outer, 2, tiles)

        @pl.when(jnp.logical_not(outward))
        def _():
            put(to_inner, 2, tiles)

    for r in range(4):
        for k in range(FB // 2):
            state_out[r, k] = jnp.where(lo[0], swap_bf(p3[3 + r, 1 + 2 * k]), p3[3 + r, 2 + 2 * k])
    for top, ref in ((upper, state_outer), (jnp.logical_not(upper), state_inner)):
        start = jnp.where(top, 0, 2)
        for r in range(2):
            ref[r] = state_out[start + r]


def zero_tail(acc):
    acc[:, 4 * LANES :] = jnp.zeros((CB * SUB, LANES), F32)


def packed_tiles(ref, at):
    return lambda i: ref[at * ROW_TILES + i * PAIRS : at * ROW_TILES + (i + 1) * PAIRS]


def raw_tiles(get):
    def tiles(i):
        return jnp.stack([get(slice((3 * k + i) * LANES, (3 * k + i + 1) * LANES)) for k in range(PAIRS)])

    return tiles


def coarse_state_body(own, outer, inner, w_h, acc_out, h_out, h0):
    upper, _, _ = place(2)
    for idx in range(6):
        if 2 <= idx < 4:
            put_packed(h0, idx, raw_tiles(lambda lanes: own[idx - 2, :, lanes]))
            continue
        r = idx if idx < 2 else idx - 4
        a, b = (outer, inner) if idx < 2 else (inner, outer)
        put_packed(h0, idx, raw_tiles(lambda lanes: jnp.where(upper, a[r, :, lanes], b[r, :, lanes])))

    base = jnp.where(upper, 1, 2)
    for k in range(3):
        acc_out[k, :, : 3 * C2] = jnp.dot(coarse_patches(h0, base + k), w_h[...], preferred_element_type=F32)
        acc_out[k, :, 4 * LANES + C1 :] = jnp.zeros((CB * SUB, C1), F32)
        h_out[k] = h0[base + k]


def put_row(ref, slot, forms):
    for k, tile in enumerate(pack_forms(forms)):
        base = slot * ROW_TILES + k * PAIRS
        ref[base : base + PAIRS] = tile


def first_inner_body(low_own, low_inner, acc_first, h_first, w_x, h1, sent, x1, acc_x):
    upper, _, _ = place(2)
    zero_tail(acc_x)
    put_packed(x1, 0, either(upper, low_own, 0, low_inner, 1))
    put_packed(x1, 1, either(upper, low_own, 1, low_own, 0))
    put_packed(x1, 2, either(upper, low_inner, 0, low_own, 1))
    k = jnp.where(upper, 2, 0)
    forms = coarse_gru(x1, 1, h_first, k, w_x, None, acc_x, acc_first.at[k], True)
    put_forms(h1, jnp.where(upper, 2, 1), forms)
    put_row(sent, 0, forms)


def first_outer_body(h1_given, low_own, low_outer, acc_first, h_first, w_x, h1, x1, acc_x):
    upper, first, rows = place(2)
    zero_tail(acc_x)
    put_packed(x1, 0, either(upper, low_outer, 0, low_own, 0))
    put_packed(x1, 1, either(upper, low_outer, 1, low_own, 1))
    put_packed(x1, 2, either(upper, low_own, 0, low_outer, 0))
    put_packed(x1, 3, either(upper, low_own, 1, low_outer, 1))
    for c in (1, 2):
        k = jnp.where(upper, c - 1, c)
        row = jnp.where(upper, c - 2, c)
        forms = coarse_gru(
            x1, c, h_first, k, w_x, None, acc_x, acc_first.at[k], in_grid(first + row, rows)
        )
        put_forms(h1, row + 1, forms)


def coarse_second_body(
    low_own, low_outer, low_inner, h1_given, h1_inner, w_x, w_h, state, h1, x2, acc_x, acc_h
):
    upper, _, _ = place(2)
    zero_tail(acc_x)
    zero_tail(acc_h)
    put_packed(x2, 0, either(upper, low_outer, 2, low_inner, 2))
    put_packed(x2, 1, packed_tiles(low_own, 2))
    put_packed(x2, 2, packed_tiles(low_own, 3))
    put_packed(x2, 3, either(upper, low_inner, 2, low_outer, 2))
    put_packed(h1, jnp.where(upper, 3, 0), packed_tiles(h1_inner, 0))
    for slot in range(2):
        idx = jnp.where(upper, slot, 1 - slot)
        put_row(state, slot, coarse_gru(x2, idx + 1, h1, idx + 1, w_x, w_h, acc_x, acc_h, True))


def raise_pair(src, idx, weight):
    def tile(dr, dj, k):
        return src[idx + dr, 1 + dj : 1 + dj + CB, :, k * LANES : (k + 1) * LANES].reshape(CB * SUB, LANES)

    lo = low_half((CB * SUB, LANES))
    parts = []
    for dr in (0, 1):
        parts += [tile(dr, 0, 0), jnp.where(lo, tile(dr, 0, 1), tile(dr, 1, 2)), tile(dr, 1, 3)]
    return jnp.dot(jnp.concatenate(parts, axis=-1), weight[...], preferred_element_type=F32)


def either(upper, a, i, b, j):
    return lambda t: jnp.where(upper, packed_tiles(a, i)(t), packed_tiles(b, j)(t))


def forecast_row(rows_of, w_h, h2, acc_h, dst, at, first, rows):
    for k, tiles in enumerate(rows_of):
        put_packed(h2, k, tiles)
    forms = coarse_gru(None, 0, h2, 1, None, w_h, None, acc_h, in_grid(first + at, rows))
    put_forms(dst, at, forms)
    return forms


def forecast_inner_body(own, in_near, w_h, s1, sent, h2, acc_h):
    upper, first, rows = place(2)
    zero_tail(acc_h)
    given = (either(upper, own, 0, in_near, 0), packed_tiles(own, 1), either(upper, in_near, 0, own, 0))
    at = jnp.where(upper, 3, 2)
    put_row(sent, 0, forecast_row(given, w_h, h2, acc_h, s1, at, first - 2, rows))


def forecast_outer_body(s1_given, own, outer, w_h, s1, sent, h2, acc_h):
    upper, first, rows = place(2)
    zero_tail(acc_h)
    given = (either(upper, outer, 0, own, 1), packed_tiles(own, 0), either(upper, own, 1, outer, 0))
    at = jnp.where(upper, 2, 3)
    put_row(sent, 0, forecast_row(given, w_h, h2, acc_h, s1, at, first - 2, rows))


def forecast_halo_body(s1_given, own, outer, w_h, s1, h2, acc_h):
    upper, first, rows = place(2)
    zero_tail(acc_h)
    given = (either(upper, outer, 1, own, 0), packed_tiles(outer, 0), either(upper, own, 0, outer, 1))
    forecast_row(given, w_h, h2, acc_h, s1, jnp.where(upper, 1, 4), first - 2, rows)


def forecast_second_body(s1_given, in_near, in_far, w_h, s1, s2, acc_h):
    upper, first, rows = place(2)
    zero_tail(acc_h)
    put_packed(s1, jnp.where(upper, 4, 1), packed_tiles(in_near, 0))
    put_packed(s1, jnp.where(upper, 5, 0), packed_tiles(in_far, 0))
    base = jnp.where(upper, 1, 0)
    for k in range(3):
        at = base + k
        forms = coarse_gru(None, 0, s1, at + 1, None, w_h, None, acc_h, in_grid(first + at - 1, rows))
        put_forms(s2, at, forms)
    s2[4] = jnp.zeros(s2.shape[1:], BF)


def forecaster_body(
    s1_given, s2_given, outer, rest, f_own, f_inner, w_h, w_up, w_gru, w_head,
    out, s1, s2, h2, pf1, pf2, states, acc_h,
):
    upper, first_c, rows_c = place(2)
    _, first_f, rows_f = place(4)
    lo = low_half((1, SUB, LANES))
    zero_tail(acc_h)

    given = (either(upper, rest, 0, outer, 0), packed_tiles(outer, 1), either(upper, outer, 0, rest, 0))
    forecast_row(given, w_h, h2, acc_h, s1, jnp.where(upper, 0, 5), first_c - 2, rows_c)
    at = jnp.where(upper, 0, 3)
    put_forms(
        s2, at, coarse_gru(None, 0, s1, at + 1, None, w_h, None, acc_h, in_grid(first_c + at - 1, rows_c))
    )

    for idx in range(8):
        for k in range(FB // 2):
            if 2 <= idx < 6:
                pair = f_own[idx - 2, k]
            elif idx < 2:
                at = ROW_TILES + idx * FB // 2 + k
                pair = jnp.where(upper, rest[at], f_inner[at])
            else:
                at = ROW_TILES + (idx - 6) * FB // 2 + k
                pair = jnp.where(upper, f_inner[at], rest[at])
            pf1[idx, 1 + 2 * k] = swap_bf(pair)
            pf1[idx, 2 + 2 * k] = pair

    def raise_rows(src, idx, fine, at, coarse_row):
        acc = raise_pair(src, idx, w_up)
        acc = jnp.where(in_grid(coarse_row, rows_c), leaky(acc), 0.0)
        for half, row in enumerate(at):
            if row is None:
                continue
            tile = acc[:, half * LANES : (half + 1) * LANES]
            even = tile.astype(BF).reshape(CB, SUB, LANES)
            odd = swap_halves(tile).astype(BF).reshape(CB, SUB, LANES)
            both = jnp.stack([even, odd], axis=1).reshape(FB, SUB, LANES)
            fine[row, 1 : FB + 1] = jnp.where(lo, both, fine[row, 1 : FB + 1])

    for k in range(0, 4):
        raise_rows(s1, k + 1, pf1, (2 * k, 2 * k + 1), first_c + k - 1)
        seal(pf1, 2 * k, FB)
        seal(pf1, 2 * k + 1, FB)

    for idx in range(0, 6):
        def emit(lo_block, count, new):
            pf2[idx, pl.ds(1 + lo_block, count)] = new

        fine_gru(pf1, idx + 1, w_gru, in_grid(first_f + idx - 1, rows_f), emit)

    def head(step, ref, base):
        for t in range(4):
            lhs = jnp.concatenate(
                [ref[base : base + 4, 1 + 8 * t + k].reshape(4 * SUB, LANES) for k in range(8)], axis=-1
            )
            acc = jnp.dot(lhs, w_head[...], preferred_element_type=F32).astype(BF)
            out[step, :, :, t * LANES : (t + 1) * LANES] = acc.reshape(4, SUB, LANES)

    head(0, pf2, 1)

    raise_rows(s2, 0, pf2, (None, 0), first_c - 1)
    raise_rows(s2, 1, pf2, (1, 2), first_c)
    raise_rows(s2, 2, pf2, (3, 4), first_c + 1)
    raise_rows(s2, 3, pf2, (5, None), first_c + 2)
    for idx in range(6):
        seal(pf2, idx, FB)

    for idx in range(0, 4):
        def emit(lo_block, count, new):
            states[idx, pl.ds(1 + lo_block, count)] = new

        fine_gru(pf2, idx + 1, w_gru, True, emit)

    head(1, states, 0)


def to_upper(x):
    return jnp.concatenate([jnp.zeros(x.shape, F32), x.astype(F32)], axis=-1).astype(BF)


def to_lower(x):
    return jnp.concatenate([x.astype(F32), jnp.zeros(x.shape, F32)], axis=-1).astype(BF)


def fetch_all(given, copies, sems):
    fetches = [pltpu.make_async_copy(src, dst, sems.at[i]) for i, (src, dst) in enumerate(zip(given, copies))]
    for fetch in fetches:
        fetch.start()
    for fetch in fetches:
        fetch.wait()


def arrange_gru(kx, kh, w):
    for k in range(9):
        at = k * LANES
        w[at : at + C1, :LANES] = kx[k, :, :LANES]
        w[at : at + C1, LANES:] = to_upper(kx[k, :, LANES:])
        w[at + C1 : at + LANES, :LANES] = kh[k, :, :LANES]
        w[at + C1 : at + LANES, LANES:] = to_lower(kh[k, :, LANES:])


def prepare_encoder_body(*refs):
    given, (w_stem, w_enc, w_down), copies, sems = refs[:4], refs[4:7], refs[7:11], refs[11]
    fetch_all(given, copies, sems)
    stem, enc_x, enc_h, down = copies
    arrange_gru(enc_x, enc_h, w_enc)
    for k in range(9):
        at = k * LANES
        w_down[at : at + C1] = jnp.zeros((C1, 2 * LANES), BF)
        w_down[at + C1 : at + LANES, :LANES] = down[k, :, :LANES]
        w_down[at + C1 : at + LANES, LANES:] = to_lower(down[k, :, LANES:])
    w_stem[...] = jnp.zeros(w_stem.shape, BF)
    for k in range(8):
        wide = to_upper(stem[...]) if k % 2 else to_lower(stem[...])
        w_stem[k * PATCH : (k + 1) * PATCH, k // 2 * LANES : (k // 2 + 1) * LANES] = wide


def prepare_forecaster_body(*refs):
    given, (w_up, w_fc, w_head), copies, sems = refs[:4], refs[4:7], refs[7:11], refs[11]
    fetch_all(given, copies, sems)
    up, fc_x, fc_h, head = copies
    arrange_gru(fc_x, fc_h, w_fc)

    def tap(a, b):
        return jnp.zeros((C2, C1), F32) if a is None else up[3 * a + b].astype(F32).T

    none = (None, None)
    for g, taps in enumerate((
        ((1, 1), (1, 0), (0, 1), (0, 0)),
        (none, (1, 2), none, (0, 2)),
        (none, none, (2, 1), (2, 0)),
        (none, none, none, (2, 2)),
    )):
        for n in range(2):
            pair = jnp.concatenate([tap(*taps[2 * n]), tap(*taps[2 * n + 1])], axis=-1)
            w_up[g * C2 : (g + 1) * C2, n * LANES : (n + 1) * LANES] = pair.astype(BF)

    w_head[...] = jnp.zeros(w_head.shape, BF)
    tall = head[...].astype(F32).T.astype(BF)
    for k in range(8):
        w_head[k * LANES + C1 : (k + 1) * LANES, k * PATCH : (k + 1) * PATCH] = tall


def call(body, args, outs, scratch, aliases={}):
    return pl.pallas_call(
        body,
        out_shape=[s if isinstance(s, jax.ShapeDtypeStruct) else jax.ShapeDtypeStruct(s, BF) for s in outs],
        in_specs=[pl.BlockSpec(memory_space=space) for _, space in args],
        out_specs=[pl.BlockSpec(memory_space=pltpu.VMEM)] * len(outs),
        scratch_shapes=scratch,
        input_output_aliases=aliases,
        compiler_params=pltpu.CompilerParams(vmem_limit_bytes=24 * 1024 * 1024),
    )(*[arg for arg, _ in args])


def on_device(
    frames,
    start_fine,
    start_coarse,
    enc_stem,
    enc_fine_x,
    enc_fine_h,
    enc_down,
    enc_coarse_x,
    enc_coarse_h,
    fc_coarse_h,
    fc_up,
    fc_fine_x,
    fc_fine_h,
    fc_head,
):
    count = lax.axis_size(LINE)
    across = [(i, i + 1) for i in range(1, count - 1, 2)]
    across = across + [(b, a) for a, b in across]

    def outer_swap(x):
        return lax.ppermute(x, LINE, across)

    def inner_swap(x):
        return lax.ppermute(x, "section", [(0, 1), (1, 0)])

    coarse = start_coarse.reshape(2, SUB, CB * C2)

    def on_chip(*values):
        return [(value, pltpu.VMEM) for value in values]

    def fine_buf(rows):
        return pltpu.VMEM((rows, FB + 2, SUB, LANES), BF)

    def coarse_buf(rows):
        return pltpu.VMEM((rows, CB + 2, SUB, 4 * LANES), BF)

    fine = start_fine.reshape(4, SUB, FB * C1)
    patches = frames.reshape(FRAMES, 4, SUB, FB * PATCH)
    rows = (3, SUB, FB * (C1 + FRAMES * PATCH))
    own, to_outer, to_inner = call(pack_body, on_chip(fine, patches[0], patches[1]), [(4,) + rows[1:], rows, rows], [])
    outer, inner = outer_swap(to_outer), inner_swap(to_inner)

    acc_buf = pltpu.VMEM((CB * SUB, 5 * LANES), F32)
    flat = (9 * C2, 3 * C2)

    def prepare(body, values, outs):
        scratch = [pltpu.VMEM(value.shape, BF) for value in values]
        return call(
            body, [(value, pl.ANY) for value in values], outs, scratch + [pltpu.SemaphoreType.DMA((len(values),))]
        )

    kernel = (9, C1, 3 * C1)
    wide = (9 * LANES, 2 * LANES)
    w_stem, w_enc, w_down = prepare(
        prepare_encoder_body,
        [enc_stem, enc_fine_x.reshape(kernel), enc_fine_h.reshape(kernel), enc_down.reshape(kernel)],
        [(8 * PATCH, 4 * LANES), wide, wide],
    )
    w_up, w_fc, w_head = prepare(
        prepare_forecaster_body,
        [jnp.swapaxes(fc_up.reshape(9, C2, C1), 1, 2), fc_fine_x.reshape(kernel), fc_fine_h.reshape(kernel), fc_head.T],
        [(4 * C2, 2 * LANES), wide, (8 * LANES, 8 * PATCH)],
    )
    coarse_o, coarse_i = outer_swap(coarse), inner_swap(coarse)

    halo = (3 * ROW_TILES, SUB, LANES)
    row = (ROW_TILES, SUB, LANES)
    edge = (2, FB // 2, SUB, LANES)

    def fine_shape(count, blocks=FB + 2):
        return (count, blocks, SUB, LANES)

    p1_own, stem2_own, inside = call(
        fine_own_body, on_chip(own, w_stem, w_enc), [fine_shape(4), fine_shape(4, FB), fine_shape(2)], []
    )
    state_f, low_own, to_outer, to_inner, state_fo, state_fi = call(
        fine_encoder_body,
        on_chip(p1_own, stem2_own, inside, outer, inner, w_stem, w_enc, w_down),
        [(4, FB // 2, SUB, LANES), (4 * ROW_TILES, SUB, LANES), halo, halo, edge, edge],
        [fine_buf(5), pltpu.VMEM(fine_shape(5, FB), BF), fine_buf(5), fine_buf(9)],
    )
    got_o, got_i = outer_swap(to_outer), inner_swap(to_inner)

    acc_first, h_first = call(
        coarse_state_body,
        on_chip(coarse, coarse_o, coarse_i, enc_coarse_h.reshape(flat)),
        [jax.ShapeDtypeStruct((3, CB * SUB, 5 * LANES), F32), (3, CB + 2, SUB, 4 * LANES)],
        [coarse_buf(6)],
    )

    w_x, w_h = enc_coarse_x.reshape(flat), enc_coarse_h.reshape(flat)
    four = (4, CB + 2, SUB, 4 * LANES)
    h1, sent = call(
        first_inner_body, on_chip(low_own, got_i, acc_first, h_first, w_x), [four, row], [coarse_buf(3), acc_buf]
    )
    h1_inner = inner_swap(sent)
    (h1,) = call(
        first_outer_body, on_chip(h1, low_own, got_o, acc_first, h_first, w_x), [four], [coarse_buf(4), acc_buf], {0: 0}
    )
    state_c, _ = call(
        coarse_second_body,
        on_chip(low_own, got_o, got_i, h1, h1_inner, w_x, w_h),
        [(2 * ROW_TILES, SUB, LANES), four],
        [coarse_buf(4), acc_buf, acc_buf],
        {3: 1},
    )
    edge_i = jnp.concatenate([state_c[ROW_TILES:], state_fi.reshape(FB, SUB, LANES)], axis=0)
    edge_i = inner_swap(edge_i)
    in_near = edge_i[:ROW_TILES]
    state_o = outer_swap(state_c)
    rest = outer_swap(jnp.concatenate([in_near, state_fo.reshape(FB, SUB, LANES)], axis=0))

    w_f = fc_coarse_h.reshape(flat)
    six, five = (6,) + four[1:], (5,) + four[1:]
    small = [coarse_buf(3), acc_buf]
    s1, sent = call(forecast_inner_body, on_chip(state_c, edge_i, w_f), [six, row], small)
    in_near = inner_swap(sent)
    s1, sent = call(forecast_outer_body, on_chip(s1, state_c, state_o, w_f), [six, row], small, {0: 0})
    in_far = inner_swap(sent)
    (s1,) = call(forecast_halo_body, on_chip(s1, state_c, state_o, w_f), [six], small, {0: 0})
    s1, s2 = call(forecast_second_body, on_chip(s1, in_near, in_far, w_f), [six, five], [acc_buf], {0: 0})
    out, _, _ = call(
        forecaster_body,
        on_chip(s1, s2, state_o, rest, state_f, edge_i, w_f, w_up, w_fc, w_head),
        [(HORIZON, 4, SUB, FB * PATCH), six, five],
        [coarse_buf(3), fine_buf(8), fine_buf(6), fine_buf(4), acc_buf],
        {0: 1, 1: 2},
    )
    return out.reshape(HORIZON, 4, COLS * PATCH)


def solution(mesh):
    line = ("groups", "tile", "section")
    return jax.shard_map(
        on_device,
        mesh=mesh,
        in_specs=(P(None, line, None), P(line, None), P(line, None)) + (P(),) * 11,
        out_specs=P(None, line, None),
        check_vma=False,
    )
```

```python
import jax
import jax.numpy as jnp
from jax import lax
from jax.experimental import pallas as pl
from jax.experimental.pallas import tpu as pltpu
from jax.sharding import PartitionSpec as P


C1 = 64
C2 = 192
PATCH = 16
FRAMES = 2
HORIZON = 2
COLS = 512
SUB = 16
FB = COLS // SUB
CB = COLS // 2 // SUB
LANES = 128
BF = jnp.bfloat16
F32 = jnp.float32
LINE = ("tile", "section")
PAIRS = CB // 2
ROW_TILES = 3 * PAIRS


def leaky(values):
    return jnp.where(values > 0, values, 0.2 * values)


def low_half(shape):
    return lax.broadcasted_iota(jnp.int32, shape, len(shape) - 1) < 64


def swap_halves(x):
    flat = x.reshape(-1, LANES)
    return pltpu.roll(flat, 64, 1).reshape(x.shape)


def swap_bf(x):
    return swap_halves(x.astype(F32)).astype(BF)


def sigmoid(x):
    return 0.5 * jnp.tanh(0.5 * x) + 0.5


def shift_sub(x, by):
    wide = x.astype(F32)
    row = lax.broadcasted_iota(jnp.int32, wide.shape, 0)
    if by > 0:
        moved = jnp.where(row == 0, 0.0, pltpu.roll(wide, 1, 0))
    else:
        moved = jnp.where(row == SUB - 1, 0.0, pltpu.roll(wide, SUB - 1, 0))
    return moved.astype(BF)


def seal(ref, idx, blocks):
    ref[idx, 0] = shift_sub(ref[idx, blocks], 1)
    ref[idx, blocks + 1] = shift_sub(ref[idx, 1], -1)


def row_of(src, idx):
    if isinstance(src, list):
        ref, at = src[idx]
        return ref.at[at]
    return src.at[idx]


def fine_patches(src, idx, lo, count):
    parts = [
        row_of(src, idx + dr)[pl.ds(lo + dj, count)].reshape(count * SUB, LANES)
        for dr in (-1, 0, 1)
        for dj in (0, 1, 2)
    ]
    return jnp.concatenate(parts, axis=-1)


def fine_gru(src, idx, weight, valid, emit):
    count = 16
    for lo in range(0, FB, count):
        acc = jnp.dot(fine_patches(src, idx, lo, count), weight[...], preferred_element_type=F32)
        gates = sigmoid(acc[:, :LANES])
        cand = acc[:, LANES:]
        cand = jnp.tanh(cand + swap_halves(gates * cand))
        old = row_of(src, idx)[pl.ds(1 + lo, count)].reshape(count * SUB, LANES).astype(F32)
        new = (1.0 - gates) * cand + gates * old
        new = jnp.where(valid, new, 0.0).astype(BF)
        emit(lo, count, new.reshape(count, SUB, LANES))


def down_row(src, idx, weight):
    parts = []
    for dr in (-1, 0, 1):
        row = row_of(src, idx + dr)[...].reshape(FB // 2 + 1, 2, SUB, LANES)
        for tap in (row[:CB, 0], row[:CB, 1], row[1:, 0]):
            parts.append(tap.reshape(CB * SUB, LANES))
    lhs = jnp.concatenate(parts, axis=-1)
    return jnp.dot(lhs, weight[...], preferred_element_type=F32)


def coarse_forms(t0, t1):
    lo = low_half(t0.shape)
    r0, r1 = swap_halves(t0), swap_halves(t1)
    return (
        t0.astype(BF),
        jnp.where(lo, t1, 0.0).astype(BF),
        jnp.where(lo, 0.0, r0).astype(BF),
        jnp.where(lo, r0, r1).astype(BF),
    )


def put_forms(ref, idx, forms):
    for k, tile in enumerate(forms):
        ref[idx, 1 : CB + 1, :, k * LANES : (k + 1) * LANES] = tile.reshape(CB, SUB, LANES)
    seal(ref, idx, CB)


def put_packed(ref, idx, tiles):
    t = [tiles(i).astype(F32) for i in range(3)]
    r = [swap_halves(x) for x in t]
    lo = low_half(t[0].shape)
    even = (t[0], jnp.where(lo, t[1], 0.0), jnp.where(lo, 0.0, r[0]), jnp.where(lo, r[0], r[1]))
    odd = (
        jnp.where(lo, r[1], r[2]),
        jnp.where(lo, r[2], 0.0),
        jnp.where(lo, 0.0, t[1]),
        t[2],
    )
    for k in range(4):
        both = jnp.stack([even[k].astype(BF), odd[k].astype(BF)], axis=1)
        ref[idx, 1 : CB + 1, :, k * LANES : (k + 1) * LANES] = both.reshape(CB, SUB, LANES)
    seal(ref, idx, CB)


def pack_forms(forms):
    f = [x.reshape(CB // 2, 2, SUB, LANES) for x in forms]
    lo = low_half((CB // 2, SUB, LANES))
    return (f[0][:, 0], jnp.where(lo, f[1][:, 0], f[2][:, 1]), f[3][:, 1])


def coarse_patches(ref, idx):
    def tile(dr, dj, k):
        return ref[idx + dr, dj : dj + CB, :, k * LANES : (k + 1) * LANES].reshape(CB * SUB, LANES)

    lo = low_half((CB * SUB, LANES))

    def aligned(dr):
        return [
            tile(dr, 0, 0),
            jnp.where(lo, tile(dr, 0, 1), tile(dr, 1, 2)),
            tile(dr, 1, 3),
            tile(dr, 2, 0),
        ]

    parts = aligned(-1)
    parts.append(jnp.where(lo, tile(-1, 2, 1), tile(0, 0, 2)))
    parts += [tile(0, 0, 3), tile(0, 1, 0), jnp.where(lo, tile(0, 1, 1), tile(0, 2, 2)), tile(0, 2, 3)]
    parts += aligned(1)
    parts.append(tile(1, 2, 1))
    return jnp.concatenate(parts, axis=-1)[:, : 9 * C2]


def coarse_gru(x_ref, x_idx, h_ref, h_idx, w_x, w_h, acc_x, acc_h, valid):
    width = 3 * C2
    if w_h is not None:
        acc_h[:, :width] = jnp.dot(coarse_patches(h_ref, h_idx), w_h[...], preferred_element_type=F32)
    if x_ref is not None:
        acc_x[:, :width] = jnp.dot(coarse_patches(x_ref, x_idx), w_x[...], preferred_element_type=F32)

    def part(ref, k):
        return ref[:, k * LANES : (k + 1) * LANES]

    gates = []
    for k in range(3):
        mixed = part(acc_h, k)
        if x_ref is not None:
            mixed = part(acc_x, k) + mixed
        gates.append(sigmoid(mixed))
    lo = low_half(gates[0].shape)
    g1, g2 = swap_halves(gates[1]), swap_halves(gates[2])
    update = (jnp.where(lo, g1, g2), g2)
    out = []
    for k in range(2):
        cand = gates[k] * part(acc_h, 3 + k)
        if x_ref is not None:
            cand = part(acc_x, 3 + k) + cand
        cand = jnp.tanh(cand)
        old = h_ref[h_idx, 1 : CB + 1, :, k * LANES : (k + 1) * LANES].reshape(CB * SUB, LANES).astype(F32)
        new = (1.0 - update[k]) * cand + update[k] * old
        out.append(jnp.where(valid, new, 0.0).astype(BF).astype(F32))
    return coarse_forms(out[0], out[1])


def place(per_device):
    upper = lax.axis_index("section") == 0
    line = lax.axis_index("tile") * lax.axis_size("section") + lax.axis_index("section")
    return upper, line * per_device, lax.axis_size(LINE) * per_device


def in_grid(row, rows):
    return jnp.logical_and(row >= 0, row < rows)


def pack_body(fine, first, second, own, to_outer, to_inner):
    upper, _, _ = place(4)
    for r in range(4):
        own[r, :, : FB * C1] = fine[r]
        own[r, :, FB * C1 : FB * (C1 + PATCH)] = first[r]
        own[r, :, FB * (C1 + PATCH) :] = second[r]
    for r in range(3):
        to_outer[r] = jnp.where(upper, own[r], own[r + 1])
        to_inner[r] = jnp.where(upper, own[r + 1], own[r])


def fill_fine(get, count, w_stem, p1, stem2):
    lo = low_half((SUB, LANES))
    for frame in range(FRAMES):
        for t in range(4):
            at = FB * C1 + frame * FB * PATCH + t * LANES
            patches = jnp.concatenate([get(r, slice(at, at + LANES)) for r in range(count)], axis=0)
            acc = leaky(jnp.dot(patches, w_stem[...], preferred_element_type=F32))
            for k in range(8):
                tile = acc[:, k // 2 * LANES : (k // 2 + 1) * LANES]
                tile = swap_halves(tile) if k % 2 else tile
                block = tile.astype(BF).reshape(count, SUB, LANES)
                if frame == 0:
                    p1[:, 1 + 8 * t + k] = block
                else:
                    stem2[:, 8 * t + k] = block
    for r in range(count):
        for k in range(FB // 2):
            pair = get(r, slice(k * LANES, (k + 1) * LANES))
            p1[r, 1 + 2 * k] = jnp.where(lo, p1[r, 1 + 2 * k], swap_bf(pair))
            p1[r, 2 + 2 * k] = jnp.where(lo, p1[r, 2 + 2 * k], pair)
        seal(p1, r, FB)


def first_fine(src, idx, w_gru, valid, stems, dst, at):
    lo = low_half((1, SUB, LANES))

    def emit(lo_block, count, new):
        dst[at, pl.ds(1 + lo_block, count)] = jnp.where(lo, stems[pl.ds(lo_block, count)], new)

    fine_gru(src, idx, w_gru, valid, emit)
    seal(dst, at, FB)


def fine_own_body(own, w_stem, w_gru, p1, stem2, inside):
    fill_fine(lambda r, lanes: own[r, :, lanes], 4, w_stem, p1, stem2)
    for r in range(2):
        first_fine(p1, 1 + r, w_gru, True, stem2.at[1 + r], inside, r)


def fine_encoder_body(
    p1_own, stem2_own, inside, outer, inner, w_stem, w_gru, w_down,
    low_own, to_outer, to_inner, p3, p1_halo, stem2_halo, p2_rest,
):
    upper, first, rows = place(4)
    lo = low_half((1, SUB, LANES))

    def get(r, lanes):
        above = r < 3
        at = r if above else r - 3
        a, b = outer[at, :, lanes], inner[at, :, lanes]
        return jnp.where(upper, a, b) if above else jnp.where(upper, b, a)

    fill_fine(get, 5, w_stem, p1_halo, stem2_halo)
    p1 = [(p1_halo, r) for r in range(3)] + [(p1_own, r) for r in range(4)] + [(p1_halo, r) for r in (3, 4)]
    stem2 = [(stem2_halo, r) for r in range(3)] + [(stem2_own, r) for r in range(4)] + [(stem2_halo, 3)]
    p2 = [None] + [(p2_rest, r) for r in range(3)] + [(inside, 0), (inside, 1), (p2_rest, 3), (p2_rest, 4)]
    for idx in (1, 2, 3, 6, 7):
        dst, at = p2[idx]
        first_fine(p1, idx, w_gru, in_grid(first + idx - 3, rows), row_of(stem2, idx), dst, at)

    for idx in range(2, 7):
        def emit(lo_block, count, new):
            p3[idx, pl.ds(1 + lo_block, count)] = jnp.where(lo, jnp.zeros_like(new), new)

        fine_gru(p2, idx, w_gru, in_grid(first + idx - 3, rows), emit)
        seal(p3, idx, FB)

    def lowered(src, p):
        acc = leaky(down_row(src, 3 + 2 * p, w_down)).astype(BF).astype(F32)
        return pack_forms(coarse_forms(acc[:, :LANES], acc[:, LANES:]))

    def put(ref, at, tiles):
        for k, tile in enumerate(tiles):
            base = at * ROW_TILES + k * PAIRS
            ref[base : base + PAIRS] = tile

    for p in range(2):
        tiles = lowered(p2, p)
        put(low_own, p, tiles)
        put(to_outer, p, tiles)
        put(to_inner, p, tiles)
    for p in range(2):
        tiles = lowered(p3, p)
        put(low_own, 2 + p, tiles)
        outward = upper if p == 0 else jnp.logical_not(upper)

        @pl.when(outward)
        def _():
            put(to_outer, 2, tiles)

        @pl.when(jnp.logical_not(outward))
        def _():
            put(to_inner, 2, tiles)


def fine_state_body(p3, state_out, state_outer, state_inner):
    upper, _, _ = place(4)
    lo = low_half((1, SUB, LANES))
    for r in range(4):
        for k in range(FB // 2):
            state_out[r, k] = jnp.where(lo[0], swap_bf(p3[3 + r, 1 + 2 * k]), p3[3 + r, 2 + 2 * k])
    for top, ref in ((upper, state_outer), (jnp.logical_not(upper), state_inner)):
        start = jnp.where(top, 0, 2)
        for r in range(2):
            ref[r] = state_out[start + r]


def zero_tail(acc):
    acc[:, 4 * LANES :] = jnp.zeros((CB * SUB, LANES), F32)


def packed_tiles(ref, at):
    return lambda i: ref[at * ROW_TILES + i * PAIRS : at * ROW_TILES + (i + 1) * PAIRS]


def raw_tiles(get):
    def tiles(i):
        return jnp.stack([get(slice((3 * k + i) * LANES, (3 * k + i + 1) * LANES)) for k in range(PAIRS)])

    return tiles


def coarse_state_body(own, outer, inner, w_h, acc_out, h_out, h0):
    upper, _, _ = place(2)
    for idx in range(6):
        if 2 <= idx < 4:
            put_packed(h0, idx, raw_tiles(lambda lanes: own[idx - 2, :, lanes]))
            continue
        r = idx if idx < 2 else idx - 4
        a, b = (outer, inner) if idx < 2 else (inner, outer)
        put_packed(h0, idx, raw_tiles(lambda lanes: jnp.where(upper, a[r, :, lanes], b[r, :, lanes])))

    base = jnp.where(upper, 1, 2)
    for k in range(3):
        acc_out[k, :, : 3 * C2] = jnp.dot(coarse_patches(h0, base + k), w_h[...], preferred_element_type=F32)
        acc_out[k, :, 4 * LANES + C1 :] = jnp.zeros((CB * SUB, C1), F32)
        h_out[k] = h0[base + k]


def put_row(ref, slot, forms):
    for k, tile in enumerate(pack_forms(forms)):
        base = slot * ROW_TILES + k * PAIRS
        ref[base : base + PAIRS] = tile


def first_inner_body(low_own, low_inner, acc_first, h_first, w_x, h1, sent, x1, acc_x):
    upper, _, _ = place(2)
    zero_tail(acc_x)
    put_packed(x1, 0, either(upper, low_own, 0, low_inner, 1))
    put_packed(x1, 1, either(upper, low_own, 1, low_own, 0))
    put_packed(x1, 2, either(upper, low_inner, 0, low_own, 1))
    k = jnp.where(upper, 2, 0)
    forms = coarse_gru(x1, 1, h_first, k, w_x, None, acc_x, acc_first.at[k], True)
    put_forms(h1, jnp.where(upper, 2, 1), forms)
    put_row(sent, 0, forms)


def first_outer_body(h1_given, low_own, low_outer, acc_first, h_first, w_x, h1, x1, acc_x):
    upper, first, rows = place(2)
    zero_tail(acc_x)
    put_packed(x1, 0, either(upper, low_outer, 0, low_own, 0))
    put_packed(x1, 1, either(upper, low_outer, 1, low_own, 1))
    put_packed(x1, 2, either(upper, low_own, 0, low_outer, 0))
    put_packed(x1, 3, either(upper, low_own, 1, low_outer, 1))
    for c in (1, 2):
        k = jnp.where(upper, c - 1, c)
        row = jnp.where(upper, c - 2, c)
        forms = coarse_gru(
            x1, c, h_first, k, w_x, None, acc_x, acc_first.at[k], in_grid(first + row, rows)
        )
        put_forms(h1, row + 1, forms)


def coarse_second_body(
    low_own, low_outer, low_inner, h1_given, h1_inner, w_x, w_h, state, h1, x2, acc_x, acc_h
):
    upper, _, _ = place(2)
    zero_tail(acc_x)
    zero_tail(acc_h)
    put_packed(x2, 0, either(upper, low_outer, 2, low_inner, 2))
    put_packed(x2, 1, packed_tiles(low_own, 2))
    put_packed(x2, 2, packed_tiles(low_own, 3))
    put_packed(x2, 3, either(upper, low_inner, 2, low_outer, 2))
    put_packed(h1, jnp.where(upper, 3, 0), packed_tiles(h1_inner, 0))
    for slot in range(2):
        idx = jnp.where(upper, slot, 1 - slot)
        put_row(state, slot, coarse_gru(x2, idx + 1, h1, idx + 1, w_x, w_h, acc_x, acc_h, True))


def raise_pair(src, idx, weight):
    def tile(dr, dj, k):
        return src[idx + dr, 1 + dj : 1 + dj + CB, :, k * LANES : (k + 1) * LANES].reshape(CB * SUB, LANES)

    lo = low_half((CB * SUB, LANES))
    parts = []
    for dr in (0, 1):
        parts += [tile(dr, 0, 0), jnp.where(lo, tile(dr, 0, 1), tile(dr, 1, 2)), tile(dr, 1, 3)]
    return jnp.dot(jnp.concatenate(parts, axis=-1), weight[...], preferred_element_type=F32)


def either(upper, a, i, b, j):
    return lambda t: jnp.where(upper, packed_tiles(a, i)(t), packed_tiles(b, j)(t))


def forecast_row(rows_of, w_h, h2, acc_h, dst, at, first, rows):
    for k, tiles in enumerate(rows_of):
        put_packed(h2, k, tiles)
    forms = coarse_gru(None, 0, h2, 1, None, w_h, None, acc_h, in_grid(first + at, rows))
    put_forms(dst, at, forms)
    return forms


def forecast_inner_body(own, in_near, w_h, s1, sent, h2, acc_h):
    upper, first, rows = place(2)
    zero_tail(acc_h)
    given = (either(upper, own, 0, in_near, 0), packed_tiles(own, 1), either(upper, in_near, 0, own, 0))
    at = jnp.where(upper, 3, 2)
    put_row(sent, 0, forecast_row(given, w_h, h2, acc_h, s1, at, first - 2, rows))


def forecast_outer_body(s1_given, own, outer, w_h, s1, sent, h2, acc_h):
    upper, first, rows = place(2)
    zero_tail(acc_h)
    given = (either(upper, outer, 0, own, 1), packed_tiles(own, 0), either(upper, own, 1, outer, 0))
    at = jnp.where(upper, 2, 3)
    put_row(sent, 0, forecast_row(given, w_h, h2, acc_h, s1, at, first - 2, rows))


def forecast_halo_body(s1_given, own, outer, w_h, s1, h2, acc_h):
    upper, first, rows = place(2)
    zero_tail(acc_h)
    given = (either(upper, outer, 1, own, 0), packed_tiles(outer, 0), either(upper, own, 0, outer, 1))
    forecast_row(given, w_h, h2, acc_h, s1, jnp.where(upper, 1, 4), first - 2, rows)


def forecast_second_body(s1_given, in_near, in_far, w_h, s1, s2, acc_h):
    upper, first, rows = place(2)
    zero_tail(acc_h)
    put_packed(s1, jnp.where(upper, 4, 1), packed_tiles(in_near, 0))
    put_packed(s1, jnp.where(upper, 5, 0), packed_tiles(in_far, 0))
    base = jnp.where(upper, 1, 0)
    for k in range(3):
        at = base + k
        forms = coarse_gru(None, 0, s1, at + 1, None, w_h, None, acc_h, in_grid(first + at - 1, rows))
        put_forms(s2, at, forms)
    s2[4] = jnp.zeros(s2.shape[1:], BF)


def forecaster_body(
    s1_given, s2_given, outer, rest, f_own, f_inner, w_h, w_up, w_gru, w_head,
    out, s1, s2, h2, pf1, pf2, states, acc_h,
):
    upper, first_c, rows_c = place(2)
    _, first_f, rows_f = place(4)
    lo = low_half((1, SUB, LANES))
    zero_tail(acc_h)

    given = (either(upper, rest, 0, outer, 0), packed_tiles(outer, 1), either(upper, outer, 0, rest, 0))
    forecast_row(given, w_h, h2, acc_h, s1, jnp.where(upper, 0, 5), first_c - 2, rows_c)
    at = jnp.where(upper, 0, 3)
    put_forms(
        s2, at, coarse_gru(None, 0, s1, at + 1, None, w_h, None, acc_h, in_grid(first_c + at - 1, rows_c))
    )

    for idx in range(8):
        for k in range(FB // 2):
            if 2 <= idx < 6:
                pair = f_own[idx - 2, k]
            elif idx < 2:
                at = ROW_TILES + idx * FB // 2 + k
                pair = jnp.where(upper, rest[at], f_inner[at])
            else:
                at = ROW_TILES + (idx - 6) * FB // 2 + k
                pair = jnp.where(upper, f_inner[at], rest[at])
            pf1[idx, 1 + 2 * k] = swap_bf(pair)
            pf1[idx, 2 + 2 * k] = pair

    def raise_rows(src, idx, fine, at, coarse_row):
        acc = raise_pair(src, idx, w_up)
        acc = jnp.where(in_grid(coarse_row, rows_c), leaky(acc), 0.0)
        for half, row in enumerate(at):
            if row is None:
                continue
            tile = acc[:, half * LANES : (half + 1) * LANES]
            even = tile.astype(BF).reshape(CB, SUB, LANES)
            odd = swap_halves(tile).astype(BF).reshape(CB, SUB, LANES)
            both = jnp.stack([even, odd], axis=1).reshape(FB, SUB, LANES)
            fine[row, 1 : FB + 1] = jnp.where(lo, both, fine[row, 1 : FB + 1])

    for k in range(0, 4):
        raise_rows(s1, k + 1, pf1, (2 * k, 2 * k + 1), first_c + k - 1)
        seal(pf1, 2 * k, FB)
        seal(pf1, 2 * k + 1, FB)

    for idx in range(0, 6):
        def emit(lo_block, count, new):
            pf2[idx, pl.ds(1 + lo_block, count)] = new

        fine_gru(pf1, idx + 1, w_gru, in_grid(first_f + idx - 1, rows_f), emit)

    def head(step, ref, base):
        for t in range(4):
            lhs = jnp.concatenate(
                [ref[base : base + 4, 1 + 8 * t + k].reshape(4 * SUB, LANES) for k in range(8)], axis=-1
            )
            acc = jnp.dot(lhs, w_head[...], preferred_element_type=F32).astype(BF)
            out[step, :, :, t * LANES : (t + 1) * LANES] = acc.reshape(4, SUB, LANES)

    head(0, pf2, 1)

    raise_rows(s2, 0, pf2, (None, 0), first_c - 1)
    raise_rows(s2, 1, pf2, (1, 2), first_c)
    raise_rows(s2, 2, pf2, (3, 4), first_c + 1)
    raise_rows(s2, 3, pf2, (5, None), first_c + 2)
    for idx in range(6):
        seal(pf2, idx, FB)

    for idx in range(0, 4):
        def emit(lo_block, count, new):
            states[idx, pl.ds(1 + lo_block, count)] = new

        fine_gru(pf2, idx + 1, w_gru, True, emit)

    head(1, states, 0)


def to_upper(x):
    return jnp.concatenate([jnp.zeros(x.shape, F32), x.astype(F32)], axis=-1).astype(BF)


def to_lower(x):
    return jnp.concatenate([x.astype(F32), jnp.zeros(x.shape, F32)], axis=-1).astype(BF)


def fetch_all(given, copies, sems):
    fetches = [pltpu.make_async_copy(src, dst, sems.at[i]) for i, (src, dst) in enumerate(zip(given, copies))]
    for fetch in fetches:
        fetch.start()
    for fetch in fetches:
        fetch.wait()


def arrange_gru(kx, kh, w):
    for k in range(9):
        at = k * LANES
        w[at : at + C1, :LANES] = kx[k, :, :LANES]
        w[at : at + C1, LANES:] = to_upper(kx[k, :, LANES:])
        w[at + C1 : at + LANES, :LANES] = kh[k, :, :LANES]
        w[at + C1 : at + LANES, LANES:] = to_lower(kh[k, :, LANES:])


def prepare_encoder_body(*refs):
    given, (w_stem, w_enc, w_down), copies, sems = refs[:4], refs[4:7], refs[7:11], refs[11]
    fetch_all(given, copies, sems)
    stem, enc_x, enc_h, down = copies
    arrange_gru(enc_x, enc_h, w_enc)
    for k in range(9):
        at = k * LANES
        w_down[at : at + C1] = jnp.zeros((C1, 2 * LANES), BF)
        w_down[at + C1 : at + LANES, :LANES] = down[k, :, :LANES]
        w_down[at + C1 : at + LANES, LANES:] = to_lower(down[k, :, LANES:])
    w_stem[...] = jnp.zeros(w_stem.shape, BF)
    for k in range(8):
        wide = to_upper(stem[...]) if k % 2 else to_lower(stem[...])
        w_stem[k * PATCH : (k + 1) * PATCH, k // 2 * LANES : (k // 2 + 1) * LANES] = wide


def prepare_forecaster_body(*refs):
    given, (w_up, w_fc, w_head), copies, sems = refs[:4], refs[4:7], refs[7:11], refs[11]
    fetch_all(given, copies, sems)
    up, fc_x, fc_h, head = copies
    arrange_gru(fc_x, fc_h, w_fc)

    def tap(a, b):
        return jnp.zeros((C2, C1), F32) if a is None else up[3 * a + b].astype(F32).T

    none = (None, None)
    for g, taps in enumerate((
        ((1, 1), (1, 0), (0, 1), (0, 0)),
        (none, (1, 2), none, (0, 2)),
        (none, none, (2, 1), (2, 0)),
        (none, none, none, (2, 2)),
    )):
        for n in range(2):
            pair = jnp.concatenate([tap(*taps[2 * n]), tap(*taps[2 * n + 1])], axis=-1)
            w_up[g * C2 : (g + 1) * C2, n * LANES : (n + 1) * LANES] = pair.astype(BF)

    w_head[...] = jnp.zeros(w_head.shape, BF)
    tall = head[...].astype(F32).T.astype(BF)
    for k in range(8):
        w_head[k * LANES + C1 : (k + 1) * LANES, k * PATCH : (k + 1) * PATCH] = tall


def call(body, args, outs, scratch, aliases={}):
    return pl.pallas_call(
        body,
        out_shape=[s if isinstance(s, jax.ShapeDtypeStruct) else jax.ShapeDtypeStruct(s, BF) for s in outs],
        in_specs=[pl.BlockSpec(memory_space=space) for _, space in args],
        out_specs=[pl.BlockSpec(memory_space=pltpu.VMEM)] * len(outs),
        scratch_shapes=scratch,
        input_output_aliases=aliases,
        compiler_params=pltpu.CompilerParams(vmem_limit_bytes=24 * 1024 * 1024),
    )(*[arg for arg, _ in args])


def on_device(
    frames,
    start_fine,
    start_coarse,
    enc_stem,
    enc_fine_x,
    enc_fine_h,
    enc_down,
    enc_coarse_x,
    enc_coarse_h,
    fc_coarse_h,
    fc_up,
    fc_fine_x,
    fc_fine_h,
    fc_head,
):
    count = lax.axis_size(LINE)
    across = [(i, i + 1) for i in range(1, count - 1, 2)]
    across = across + [(b, a) for a, b in across]

    def outer_swap(x):
        return lax.ppermute(x, LINE, across)

    def inner_swap(x):
        return lax.ppermute(x, "section", [(0, 1), (1, 0)])

    coarse = start_coarse.reshape(2, SUB, CB * C2)

    def on_chip(*values):
        return [(value, pltpu.VMEM) for value in values]

    def fine_buf(rows):
        return pltpu.VMEM((rows, FB + 2, SUB, LANES), BF)

    def coarse_buf(rows):
        return pltpu.VMEM((rows, CB + 2, SUB, 4 * LANES), BF)

    fine = start_fine.reshape(4, SUB, FB * C1)
    patches = frames.reshape(FRAMES, 4, SUB, FB * PATCH)
    rows = (3, SUB, FB * (C1 + FRAMES * PATCH))
    own, to_outer, to_inner = call(pack_body, on_chip(fine, patches[0], patches[1]), [(4,) + rows[1:], rows, rows], [])
    outer, inner = outer_swap(to_outer), inner_swap(to_inner)

    acc_buf = pltpu.VMEM((CB * SUB, 5 * LANES), F32)
    flat = (9 * C2, 3 * C2)

    def prepare(body, values, outs):
        scratch = [pltpu.VMEM(value.shape, BF) for value in values]
        return call(
            body, [(value, pl.ANY) for value in values], outs, scratch + [pltpu.SemaphoreType.DMA((len(values),))]
        )

    kernel = (9, C1, 3 * C1)
    wide = (9 * LANES, 2 * LANES)
    w_stem, w_enc, w_down = prepare(
        prepare_encoder_body,
        [enc_stem, enc_fine_x.reshape(kernel), enc_fine_h.reshape(kernel), enc_down.reshape(kernel)],
        [(8 * PATCH, 4 * LANES), wide, wide],
    )
    w_up, w_fc, w_head = prepare(
        prepare_forecaster_body,
        [jnp.swapaxes(fc_up.reshape(9, C2, C1), 1, 2), fc_fine_x.reshape(kernel), fc_fine_h.reshape(kernel), fc_head.T],
        [(4 * C2, 2 * LANES), wide, (8 * LANES, 8 * PATCH)],
    )
    coarse_o, coarse_i = outer_swap(coarse), inner_swap(coarse)

    halo = (3 * ROW_TILES, SUB, LANES)
    row = (ROW_TILES, SUB, LANES)
    edge = (2, FB // 2, SUB, LANES)

    def fine_shape(count, blocks=FB + 2):
        return (count, blocks, SUB, LANES)

    p1_own, stem2_own, inside = call(
        fine_own_body, on_chip(own, w_stem, w_enc), [fine_shape(4), fine_shape(4, FB), fine_shape(2)], []
    )
    low_own, to_outer, to_inner, p3 = call(
        fine_encoder_body,
        on_chip(p1_own, stem2_own, inside, outer, inner, w_stem, w_enc, w_down),
        [(4 * ROW_TILES, SUB, LANES), halo, halo, fine_shape(9)],
        [fine_buf(5), pltpu.VMEM(fine_shape(5, FB), BF), fine_buf(5)],
    )
    state_f, state_fo, state_fi = call(fine_state_body, on_chip(p3), [(4, FB // 2, SUB, LANES), edge, edge], [])
    got_o, got_i = outer_swap(to_outer), inner_swap(to_inner)

    acc_first, h_first = call(
        coarse_state_body,
        on_chip(coarse, coarse_o, coarse_i, enc_coarse_h.reshape(flat)),
        [jax.ShapeDtypeStruct((3, CB * SUB, 5 * LANES), F32), (3, CB + 2, SUB, 4 * LANES)],
        [coarse_buf(6)],
    )

    w_x, w_h = enc_coarse_x.reshape(flat), enc_coarse_h.reshape(flat)
    four = (4, CB + 2, SUB, 4 * LANES)
    h1, sent = call(
        first_inner_body, on_chip(low_own, got_i, acc_first, h_first, w_x), [four, row], [coarse_buf(3), acc_buf]
    )
    h1_inner = inner_swap(sent)
    (h1,) = call(
        first_outer_body, on_chip(h1, low_own, got_o, acc_first, h_first, w_x), [four], [coarse_buf(4), acc_buf], {0: 0}
    )
    state_c, _ = call(
        coarse_second_body,
        on_chip(low_own, got_o, got_i, h1, h1_inner, w_x, w_h),
        [(2 * ROW_TILES, SUB, LANES), four],
        [coarse_buf(4), acc_buf, acc_buf],
        {3: 1},
    )
    edge_i = jnp.concatenate([state_c[ROW_TILES:], state_fi.reshape(FB, SUB, LANES)], axis=0)
    edge_i = inner_swap(edge_i)
    in_near = edge_i[:ROW_TILES]
    state_o = outer_swap(state_c)
    rest = outer_swap(jnp.concatenate([in_near, state_fo.reshape(FB, SUB, LANES)], axis=0))

    w_f = fc_coarse_h.reshape(flat)
    six, five = (6,) + four[1:], (5,) + four[1:]
    small = [coarse_buf(3), acc_buf]
    s1, sent = call(forecast_inner_body, on_chip(state_c, edge_i, w_f), [six, row], small)
    in_near = inner_swap(sent)
    s1, sent = call(forecast_outer_body, on_chip(s1, state_c, state_o, w_f), [six, row], small, {0: 0})
    in_far = inner_swap(sent)
    (s1,) = call(forecast_halo_body, on_chip(s1, state_c, state_o, w_f), [six], small, {0: 0})
    s1, s2 = call(forecast_second_body, on_chip(s1, in_near, in_far, w_f), [six, five], [acc_buf], {0: 0})
    out, _, _ = call(
        forecaster_body,
        on_chip(s1, s2, state_o, rest, state_f, edge_i, w_f, w_up, w_fc, w_head),
        [(HORIZON, 4, SUB, FB * PATCH), six, five],
        [coarse_buf(3), fine_buf(8), fine_buf(6), fine_buf(4), acc_buf],
        {0: 1, 1: 2},
    )
    return out.reshape(HORIZON, 4, COLS * PATCH)


def solution(mesh):
    line = ("groups", "tile", "section")
    return jax.shard_map(
        on_device,
        mesh=mesh,
        in_specs=(P(None, line, None), P(line, None), P(line, None)) + (P(),) * 11,
        out_specs=P(None, line, None),
        check_vma=False,
    )
```
